32 devices in a mesh: groups: 2 (over y), freq: 4 (over z), sub: 4 (over x, core).
Axes of the slice: x: 2, y: 2, z: 4, core: 2. Of those that a mesh axis runs over, the one named last changes fastest.
Arguments:
- wavenumbers: float32 [512, 300], replicated, may hold values from 1 to 20
- receiver_shapes: bfloat16 [512, 300], replicated, may hold values from -6 to 6
- source_shapes: bfloat16 [512, 4, 300], replicated, may hold values from -6 to 6
- mode_counts: int32 [512], replicated, may hold values from 64 to 300, as said below
- source_depths: int32 [32], P('groups'), parts along dimension 0, may hold values from 0 to 3
- source_ranges: float32 [32], P('groups'), parts along dimension 0, may hold values from 0 to 0.5
- sections: int32 [2048], P(('freq', 'sub')), may hold values from 0 to 511, as said below
- recorded: bfloat16 [2048, 4096], P(('freq', 'sub')), may hold values from -6 to 6
Outputs:
- scores: float32 [32, 512], P('groups', ('freq', 'sub')), parts along dimension 0
The draws below stay inside these ranges and needn't reach their ends.
There are 2 independent parts, one for each index of `groups`. The reference program is written for one: setup_inputs(seed, part) draws one part's arguments, and reference() takes and returns one part's arrays. A program takes and returns all parts, laid end to end along the dimension named above; an argument that names none is the same for every part. Nothing has to cross between parts.
Inputs may be any that keep to these rules, and one draw needn't show every extreme that they name: `mode_counts`: counts rise with the bin index: bin f holds within 16 of 64 + floor((236) f / 511) modes, clipped to the range; the first bin holds 64 and the last 300. `sections`: each section holds exactly 4 channels.
All inputs are finite; a program needn't handle non-finite values.
Results may differ from the reference program's by a relative error of at most 0.0068.
Values may be sent and summed in bfloat16 or wider, within the bound.
A program may use at most 64 MiB of HBM per device.

```python
import math
import jax
import jax.numpy as jnp
from jax import lax

F = 512
MMAX = 300
MMIN = 64
NT = 4096
R = 2048
SEC = 512
NZ = 4
S = 16
F0 = 256


def draw_mode_counts(key, part):
    bin_numbers = jnp.arange(F, dtype=jnp.int32)
    ramp = MMIN + (MMAX - MMIN) * bin_numbers // max(F - 1, 1)
    jitter = jax.random.randint(key, (F,), -16, 17, dtype=jnp.int32)
    counts = jnp.clip(ramp + jitter, MMIN, MMAX)
    return counts.at[0].set(MMIN).at[F - 1].set(MMAX).astype(jnp.int32)


def draw_source_depths(key, part):
    depths = jax.random.randint(jax.random.fold_in(key, 7), (S,), 0, NZ, dtype=jnp.int32)
    return depths.at[0].set(0).at[S - 1].set(NZ - 1).astype(jnp.int32)


def draw_sections(key, part):
    order = jax.random.permutation(jax.random.fold_in(key, 11), R)
    return (order % SEC).astype(jnp.int32)


def shard_levels(rng, shape, split, low, top_value):
    factor_of = 1.0
    for position, parts in split:
        steps = jax.random.uniform(jax.random.fold_in(jax.random.fold_in(rng, 6), position), (parts,), jnp.float32, low / len(split), top_value / len(split))
        factor_of = factor_of * jnp.repeat(jnp.exp(steps), shape[position] // parts).reshape((-1,) + (1,) * (len(shape) - 1 - position))
    return factor_of


def scatter_about(own_key, extent, deviation, reach, cuts=(), kind=jnp.bfloat16):
    values = deviation * jax.random.normal(own_key, extent, jnp.float32)
    if cuts:
        values = values * shard_levels(own_key, extent, cuts, -0.22, 0.18)
    return jnp.clip(values, -reach, reach).astype(kind)


def setup_inputs(seed: int = 0, part: int = 0) -> dict:
    key_list = jax.random.split(jax.random.key(seed), 9)
    part_keys = jax.random.split(jax.random.fold_in(key_list[8], part), 9)
    wavenumbers = jnp.clip(jax.random.uniform(key_list[0], (F, MMAX), jnp.float32, 1.0, 20.0), 1.0, 20.0)
    receiver_shapes = scatter_about(key_list[1], (F, MMAX), 1.0, 6.0)
    source_shapes = scatter_about(key_list[2], (F, NZ, MMAX), 1.0, 6.0)
    mode_counts = draw_mode_counts(jax.random.fold_in(key_list[8], 71), part)
    source_depths = draw_source_depths(jax.random.fold_in(jax.random.fold_in(key_list[8], part), 71), part)
    source_ranges = jnp.clip(jax.random.uniform(part_keys[5], (S,), jnp.float32, 0.0, 0.5), 0.0, 0.5)
    sections = draw_sections(jax.random.fold_in(key_list[8], 71), part)
    recorded = scatter_about(key_list[7], (R, NT), 1.0, 6.0, ((0, 16),))
    return dict(wavenumbers=wavenumbers, receiver_shapes=receiver_shapes, source_shapes=source_shapes, mode_counts=mode_counts, source_depths=source_depths, source_ranges=source_ranges, sections=sections, recorded=recorded)


def rounded(operand):
    return lax.optimization_barrier(operand.astype(jnp.bfloat16)).astype(jnp.float32)

def source_factor(wave_part, source_table, counts, depths, ranges):
    depth_grid = source_table.shape[1]
    mode_width = wave_part.shape[1]
    chooser = (depths[:, None] == jnp.arange(depth_grid, dtype=jnp.int32)[None, :]).astype(jnp.float32)
    at_source = jnp.einsum('sz,bzm->bsm', chooser, source_table.astype(jnp.float32), precision=lax.Precision.HIGHEST)
    mode_live = (jnp.arange(mode_width, dtype=jnp.int32)[None, :] < counts[:, None]).astype(jnp.float32)
    phases = wave_part[:, None, :] * ranges[None, :, None]
    weighted = at_source * mode_live[:, None, :]
    return jnp.concatenate([weighted * jnp.cos(phases), -weighted * jnp.sin(phases)], axis=2).astype(jnp.bfloat16)

def receiver_factor(wave_part, receiver_table, positions):
    mode_width = wave_part.shape[1]
    phases = wave_part[:, :, None] * positions[None, None, :]
    amplitude = receiver_table.astype(jnp.float32)[:, :, None] * 8.0 / jnp.sqrt(phases * mode_width)
    real_part = amplitude * jnp.cos(phases)
    imag_part = amplitude * jnp.sin(phases)
    upper_rows = jnp.concatenate([real_part, imag_part], axis=2)
    lower_rows = jnp.concatenate([-imag_part, real_part], axis=2)
    return jnp.concatenate([upper_rows, lower_rows], axis=1).astype(jnp.bfloat16)

def time_table(start_time, time_span):
    bin_numbers = F0 + jnp.arange(F, dtype=jnp.int32)
    sample_times = start_time + jnp.arange(time_span, dtype=jnp.int32)
    phase_turns = bin_numbers[:, None] * sample_times[None, :] % NT
    angles = phase_turns.astype(jnp.float32) * (2.0 * math.pi / NT)
    return jnp.stack([jnp.cos(angles), -jnp.sin(angles)], axis=1).astype(jnp.bfloat16)

def reference(wavenumbers, receiver_shapes, source_shapes, mode_counts, source_depths, source_ranges, sections, recorded):
    source_side = rounded(source_factor(wavenumbers, source_shapes, mode_counts, source_depths, source_ranges))
    dft_table = rounded(time_table(jnp.int32(0), NT))
    channel_block = R // 32

    def one_block(first_row):
        channel = first_row + jnp.arange(channel_block, dtype=jnp.int32)
        positions = 1.0 + 2.0 * channel.astype(jnp.float32) / R
        receiver_side = rounded(receiver_factor(wavenumbers, receiver_shapes, positions))
        spectra = rounded(jnp.einsum('fsk,fkn->fsn', source_side, receiver_side))
        spectra = spectra.reshape(F, S, 2, channel_block)
        series = jnp.einsum('fsqn,fqt->snt', spectra, dft_table) * (1.0 / math.sqrt(F))
        waveform = lax.dynamic_slice_in_dim(recorded, first_row, channel_block, 0).astype(jnp.float32)
        return lax.optimization_barrier(jnp.sum(jnp.tanh(series) * waveform[None, :, :], axis=2))
    first_rows = jnp.arange(32, dtype=jnp.int32) * channel_block
    correlation = lax.map(one_block, first_rows)
    correlation = jnp.transpose(correlation, (1, 0, 2)).reshape(S, R)
    member = (sections[:, None] == jnp.arange(SEC, dtype=jnp.int32)[None, :]).astype(jnp.float32)
    return jnp.dot(correlation, member, precision=lax.Precision.HIGHEST) * (1.0 / math.sqrt(NT * (R // SEC)))
```

```python
import functools
import math

import jax
import jax.numpy as jnp
import numpy as np
from jax import lax
from jax.experimental import pallas as pl
from jax.experimental.pallas import tpu as pltpu
from jax.sharding import PartitionSpec as P

MMIN = 64
F0 = 256
SPREAD = 16
K_LOW, K_TOP = 1.0, 20.0
R_TOP = 0.5
K_MID, K_HALF = 0.5 * (K_LOW + K_TOP), 0.5 * (K_TOP - K_LOW)
LANES = 128
TERMS = 16
TWO_PI = 2.0 * math.pi


def sincos_turns(turns):
    part = turns - jnp.floor(turns + 0.5)
    sq = part * part
    p2 = math.pi * math.pi
    s = jnp.full_like(part, -(p2**5) / math.factorial(11))
    for n in (9, 7, 5, 3, 1):
        s = s * sq + ((-1) ** ((n - 1) // 2)) * p2 ** ((n - 1) // 2) / math.factorial(n)
    s = s * (part * math.pi)
    c = jnp.full_like(part, p2**6 / math.factorial(12))
    for n in (10, 8, 6, 4, 2, 0):
        c = c * sq + ((-1) ** (n // 2)) * p2 ** (n // 2) / math.factorial(n)
    return 1.0 - 2.0 * s * s, 2.0 * s * c


def term_constants():
    nodes = np.cos(np.pi * (np.arange(TERMS) + 0.5) / TERMS)[: TERMS // 2]
    order = np.arange(TERMS)
    table = np.cos(order[:, None] * np.arccos(nodes)[None, :])
    table *= (np.where(order == 0, 1.0, 2.0) * 2.0 / TERMS)[:, None]
    half = TERMS // 2
    out = np.zeros((half, LANES), np.float32)
    out[:, 0] = K_HALF * nodes
    out[:, 1 : 1 + half] = table[0::2]
    out[:, 1 + half : 1 + 2 * half] = table[1::2]
    return out


def place_of(n):
    return n // 2 if n % 2 == 0 else TERMS // 2 + n // 2


def replica_kernel(
    shape,
    depths_ref,
    place_ref,
    ranges_ref,
    consts_ref,
    wave_ref,
    factor_ref,
    source_ref,
    recorded_ref,
    out_ref,
    sum_ref,
    weight_ref,
    term_ref,
    tab_ref,
    part_ref,
    psi_ref,
    coef_ref,
):
    bins, modes, depth_grid, sources, channels, samples, receivers = shape
    quarter = bins // 4
    span = samples // 4
    half = TERMS // 2
    first_x = place_ref[0]
    centre = place_ref[1]

    for first in range(0, bins, LANES):
        last = first + LANES - 1
        top = min(modes, MMIN + (modes - MMIN) * last // max(bins - 1, 1) + SPREAD)
        cols = slice(first, first + LANES)

        def modal(step, sums, cols=cols):
            start = pl.multiple_of(step * 8, 8)
            rows = pl.ds(start, 8)
            wave = wave_ref[rows, cols]
            cosine, sine = sincos_turns(wave * (centre * (1.0 / TWO_PI)))
            factor = factor_ref[rows, cols]
            weight_ref[0:8, :] = factor * cosine
            weight_ref[8:16, :] = factor * sine
            xi = (wave - K_MID) * (1.0 / K_HALF)
            before, now = jnp.ones_like(xi), xi
            for n in range(1, TERMS):
                term_ref[n * 8 : n * 8 + 8, :] = now
                before, now = now, 2.0 * xi * now - before
            sums = list(sums)
            for i in range(8):
                source = source_ref[jnp.minimum(start + i, modes - 1), :, cols].astype(jnp.float32)
                value = jnp.concatenate(
                    [source * weight_ref[i : i + 1, :], source * weight_ref[8 + i : 9 + i, :]], axis=0
                )
                sums[0] = sums[0] + value
                for n in range(1, TERMS):
                    sums[n] = sums[n] + value * term_ref[n * 8 + i : n * 8 + i + 1, :]
            return tuple(sums)

        zero = jnp.zeros((2 * depth_grid, LANES), jnp.float32)
        sums = lax.fori_loop(0, -(-top // 8), modal, (zero,) * TERMS)
        for n in range(TERMS):
            for z in range(depth_grid):
                for c in range(2):
                    at = z * 2 * TERMS + c * TERMS + place_of(n)
                    row = c * depth_grid + z
                    sum_ref[at : at + 1, cols] = sums[n][row : row + 1, :]

    def times_i(value):
        blocks = []
        for z in range(depth_grid):
            base = z * 2 * TERMS
            blocks.append(-value[base + TERMS : base + 2 * TERMS])
            blocks.append(value[base : base + TERMS])
        return jnp.concatenate(blocks, axis=0)

    moments = sum_ref[...]
    moments = jnp.concatenate([moments, -times_i(moments)], axis=0).astype(jnp.bfloat16)
    group = depth_grid * 2 * TERMS

    for r in range(4):
        row = lax.broadcasted_iota(jnp.int32, (quarter, LANES), 0)
        column = lax.broadcasted_iota(jnp.int32, (quarter, LANES), 1)
        number = F0 + 4 * row + r
        whole = (number * column) % samples
        cosine, sine = sincos_turns(whole.astype(jnp.float32) * (1.0 / samples))
        turn = (number * LANES) % samples
        step_c, step_s = sincos_turns(turn.astype(jnp.float32) * (1.0 / samples))
        for block in range(span // LANES):
            cols = slice(block * LANES, (block + 1) * LANES)
            tab_ref[:quarter, cols] = cosine.astype(jnp.bfloat16)
            tab_ref[quarter:, cols] = (-sine).astype(jnp.bfloat16)
            cosine, sine = cosine * step_c - sine * step_s, cosine * step_s + sine * step_c
        bin_row = lax.broadcasted_iota(jnp.int32, (bins, quarter), 0)
        bin_column = lax.broadcasted_iota(jnp.int32, (bins, quarter), 1)
        chosen = (bin_row == 4 * bin_column + r).astype(jnp.float32).astype(jnp.bfloat16)
        picked = jnp.dot(moments, chosen, preferred_element_type=jnp.float32)
        left = jnp.concatenate([picked[:group], picked[group:]], axis=1)
        part_ref[r] = jnp.dot(
            left.astype(jnp.bfloat16), tab_ref[...], preferred_element_type=jnp.float32
        )

    for block in range(span // LANES):
        cols = slice(block * LANES, (block + 1) * LANES)
        p0, p1, p2, p3 = (part_ref[r, :, cols] for r in range(4))
        even, odd = p0 + p2, p1 + p3
        gap, turned = p0 - p2, times_i(p1 - p3)
        for q, value in enumerate((even + odd, gap + turned, even - odd, gap - turned)):
            at = q * span + block * LANES
            psi_ref[:, at : at + LANES] = value.astype(jnp.bfloat16)

    channel = lax.broadcasted_iota(jnp.int32, (1, channels), 1).astype(jnp.float32)
    position = first_x + channel * (2.0 / receivers)
    spread = lax.rsqrt(position)
    nodes = consts_ref[:, 0:1]
    for s in range(sources):
        offset = position - (ranges_ref[s] + centre)
        cosine, sine = sincos_turns(nodes * offset * (1.0 / TWO_PI))
        even = jnp.zeros((half, channels), jnp.float32)
        odd = jnp.zeros((half, channels), jnp.float32)
        for j in range(half):
            even = even + consts_ref[:, 1 + j : 2 + j] * cosine[j : j + 1, :]
            odd = odd + consts_ref[:, 1 + half + j : 2 + half + j] * sine[j : j + 1, :]
        mid_c, mid_s = sincos_turns(offset * (K_MID / TWO_PI))
        mid_c, mid_s = mid_c * spread, mid_s * spread
        rows = jnp.concatenate([mid_c * even, -mid_s * odd, -mid_s * even, -mid_c * odd], axis=0)
        coef_ref[s] = rows.T.astype(jnp.bfloat16)

    chunk = 512

    def source(s, matched):
        z = depths_ref[s]
        terms = pl.ds(pl.multiple_of(z * (2 * TERMS), 2 * TERMS), 2 * TERMS)
        coef = coef_ref[s]
        total = jnp.zeros((channels, LANES), jnp.float32)
        for start in range(0, samples, chunk):
            series = jnp.dot(
                coef, psi_ref[terms, start : start + chunk], preferred_element_type=jnp.float32
            )
            product = jnp.tanh(series) * recorded_ref[:, start : start + chunk].astype(jnp.float32)
            for tile in range(chunk // LANES):
                total = total + product[:, tile * LANES : (tile + 1) * LANES]
        value = jnp.sum(total, axis=1, keepdims=True)
        lane = lax.broadcasted_iota(jnp.int32, (channels, LANES), 1)
        return jnp.where(lane % sources == s, value, matched)

    out_ref[...] = lax.fori_loop(
        0, sources, source, jnp.zeros((channels, LANES), jnp.float32)
    )


def exchange_kernel(sizes, block_ref, out_ref, held_ref, send_sem, recv_sem):
    freq_size, sub_size = sizes
    count = freq_size * sub_size
    me = lax.axis_index("freq") * sub_size + lax.axis_index("sub")
    barrier = pltpu.get_barrier_semaphore()

    def place(number):
        return {"freq": number // sub_size, "sub": number % sub_size}

    def greet(i, carry):
        pl.semaphore_signal(
            barrier,
            inc=1,
            device_id=place((me + i) % count),
            device_id_type=pl.DeviceIdType.MESH,
        )
        return carry

    lax.fori_loop(1, count, greet, 0)
    pl.semaphore_wait(barrier, count - 1)

    def copy_to(target, source):
        return pltpu.make_async_remote_copy(
            src_ref=block_ref.at[target],
            dst_ref=held_ref.at[source],
            send_sem=send_sem.at[target],
            recv_sem=recv_sem.at[source],
            device_id=place(target),
            device_id_type=pl.DeviceIdType.MESH,
        )

    def send(i, carry):
        copy_to((me + i) % count, me).start()
        return carry

    lax.fori_loop(1, count, send, 0)

    def receive(i, total):
        source = (me + count - i) % count
        copy_to(source, source).wait_recv()
        return total + held_ref[source]

    out_ref[...] = lax.fori_loop(1, count, receive, block_ref[me])

    def drain(i, carry):
        copy_to((me + i) % count, me).wait_send()
        return carry

    lax.fori_loop(1, count, drain, 0)

FAST_TERMS = 12
FAST_HALF = 8


def fast_constants():
    nodes = np.cos(np.pi * (np.arange(FAST_TERMS) + 0.5) / FAST_TERMS)[: FAST_TERMS // 2]
    order = np.arange(FAST_TERMS)
    table = np.cos(order[:, None] * np.arccos(nodes)[None, :])
    table *= (np.where(order == 0, 1.0, 2.0) * 2.0 / FAST_TERMS)[:, None]
    half = FAST_TERMS // 2
    out = np.zeros((FAST_HALF, LANES), np.float32)
    out[:half, 0] = K_HALF * nodes
    out[half, 0] = K_MID
    out[:half, 1 : 1 + half] = table[0::2]
    out[:half, 1 + half : 1 + 2 * half] = table[1::2]
    return out


def fast_place(n):
    return n // 2 if n % 2 == 0 else FAST_HALF + n // 2


def score_kernel(
    shape,
    depths_ref,
    ranges_ref,
    consts_ref,
    sections_ref,
    wave_ref,
    factor_ref,
    source_ref,
    recorded_ref,
    out_ref,
    sum_ref,
    weight_ref,
    term_ref,
    tab_ref,
    psi_ref,
    coef_ref,
    wave_t_ref,
    kept_ref,
    block_ref,
    held_ref,
    send_sem,
    recv_sem,
):
    bins, modes, depth_grid, sources, channels, samples, sizes = shape
    freq_size, sub_size = sizes
    count = freq_size * sub_size
    receivers = channels * count
    quarter = bins // 4
    span = samples // 4
    half = FAST_TERMS // 2
    group = depth_grid * 4 * FAST_HALF
    me = lax.axis_index("freq") * sub_size + lax.axis_index("sub")
    barrier = pltpu.get_barrier_semaphore()

    def place(number):
        return {"freq": number // sub_size, "sub": number % sub_size}

    def greet(i, carry):
        pl.semaphore_signal(
            barrier,
            inc=1,
            device_id=place((me + i) % count),
            device_id_type=pl.DeviceIdType.MESH,
        )
        return carry

    lax.fori_loop(1, count, greet, 0)

    reach = 2.0 * (channels - 1) / receivers
    first_x = 1.0 + (me * channels).astype(jnp.float32) * (2.0 / receivers)
    centre = first_x + 0.5 * (reach - R_TOP)

    for block in range(samples // LANES):
        rows = slice(block * LANES, (block + 1) * LANES)
        wave_t_ref[rows, :] = recorded_ref[:, rows].T

    lane = lax.broadcasted_iota(jnp.int32, (8, LANES), 1)
    row = lax.broadcasted_iota(jnp.int32, (8, LANES), 0)
    for r in range(4):
        number = F0 + 4 * lane + r
        whole = (number * row) % samples
        cosine, sine = sincos_turns(whole.astype(jnp.float32) * (1.0 / samples))
        turn = (number * 8) % samples
        step_c, step_s = sincos_turns(turn.astype(jnp.float32) * (1.0 / samples))
        for pair in range(span // 16):
            turned_c = cosine * step_c - sine * step_s
            turned_s = cosine * step_s + sine * step_c
            rows = slice(pair * 16, pair * 16 + 16)
            tab_ref[r, rows, :quarter] = jnp.concatenate([cosine, turned_c], axis=0).astype(jnp.bfloat16)
            tab_ref[r, rows, quarter:] = jnp.concatenate([sine, turned_s], axis=0).astype(jnp.bfloat16)
            cosine = turned_c * step_c - turned_s * step_s
            sine = turned_c * step_s + turned_s * step_c

    channel = lax.broadcasted_iota(jnp.int32, (1, channels), 1).astype(jnp.float32)
    position = first_x + channel * (2.0 / receivers)
    spread = lax.rsqrt(position)
    nodes = consts_ref[:, 0:1]
    for s in range(sources):
        offset = position - (ranges_ref[s] + centre)
        cosine, sine = sincos_turns(nodes * offset * (1.0 / TWO_PI))
        even = jnp.zeros((FAST_HALF, channels), jnp.float32)
        odd = jnp.zeros((FAST_HALF, channels), jnp.float32)
        for j in range(half):
            even = even + consts_ref[:, 1 + j : 2 + j] * cosine[j : j + 1, :]
            odd = odd + consts_ref[:, 1 + half + j : 2 + half + j] * sine[j : j + 1, :]
        mid_c, mid_s = cosine[half : half + 1, :] * spread, sine[half : half + 1, :] * spread
        parts = jnp.concatenate([mid_c * even, -mid_s * odd, -mid_s * even, -mid_c * odd], axis=0)
        for z in range(depth_grid):
            here = jnp.where(depths_ref[s] == z, 1.0, 0.0)
            rows = slice(z * 4 * FAST_HALF, (z + 1) * 4 * FAST_HALF)
            coef_ref[rows, s * channels : (s + 1) * channels] = (parts * here).astype(jnp.bfloat16)

    sum_ref[...] = jnp.zeros_like(sum_ref)
    for first in range(0, bins, LANES):
        last = first + LANES - 1
        top = min(modes, MMIN + (modes - MMIN) * last // max(bins - 1, 1) + SPREAD)
        cols = slice(first, first + LANES)

        def modal(step, sums, cols=cols):
            start = pl.multiple_of(step * 8, 8)
            rows = pl.ds(start, 8)
            wave = wave_ref[rows, cols]
            cosine, sine = sincos_turns(wave * (centre * (1.0 / TWO_PI)))
            factor = factor_ref[rows, cols]
            weight_ref[0:8, :] = factor * cosine
            weight_ref[8:16, :] = factor * sine
            xi = (wave - K_MID) * (1.0 / K_HALF)
            before, now = jnp.ones_like(xi), xi
            for n in range(1, FAST_TERMS):
                term_ref[n * 8 : n * 8 + 8, :] = now
                before, now = now, 2.0 * xi * now - before
            sums = list(sums)
            for i in range(8):
                source = source_ref[jnp.minimum(start + i, modes - 1), :, cols].astype(jnp.float32)
                value = jnp.concatenate(
                    [source * weight_ref[i : i + 1, :], source * weight_ref[8 + i : 9 + i, :]], axis=0
                )
                sums[0] = sums[0] + value
                for n in range(1, FAST_TERMS):
                    sums[n] = sums[n] + value * term_ref[n * 8 + i : n * 8 + i + 1, :]
            return tuple(sums)

        zero = jnp.zeros((2 * depth_grid, LANES), jnp.float32)
        sums = lax.fori_loop(0, -(-top // 8), modal, (zero,) * FAST_TERMS)
        for n in range(FAST_TERMS):
            for z in range(depth_grid):
                for c in range(2):
                    at = (z * 2 + c) * 2 * FAST_HALF + fast_place(n)
                    r = c * depth_grid + z
                    sum_ref[at : at + 1, cols] = sums[n][r : r + 1, :]

    moments = jnp.concatenate(
        [sum_ref[:, b * LANES : (b + 1) * LANES].T for b in range(bins // LANES)], axis=0
    ).astype(jnp.bfloat16)
    pick_row = lax.broadcasted_iota(jnp.int32, (quarter, bins), 0)
    pick_bin = lax.broadcasted_iota(jnp.int32, (quarter, bins), 1)
    swap_row = lax.broadcasted_iota(jnp.int32, (group, group), 0)
    swap_col = lax.broadcasted_iota(jnp.int32, (group, group), 1)
    width = 2 * FAST_HALF
    first_half = swap_col // width % 2 == 0
    swap = jnp.where(
        first_half & (swap_row == swap_col + width),
        -1.0,
        jnp.where((swap_col // width % 2 == 1) & (swap_row == swap_col - width), 1.0, 0.0),
    ).astype(jnp.bfloat16)
    weights = []
    for r in range(4):
        chosen = (pick_bin == 4 * pick_row + r).astype(jnp.float32).astype(jnp.bfloat16)
        plain = jnp.dot(chosen, moments, preferred_element_type=jnp.float32).astype(jnp.bfloat16)
        turned = jnp.dot(plain, swap, preferred_element_type=jnp.float32).astype(jnp.bfloat16)
        weight = jnp.concatenate([plain, turned], axis=0)
        if r % 2:
            weight = jnp.concatenate([weight, jnp.concatenate([turned, -plain], axis=0)], axis=1)
        weights.append(weight)
    piece = 128
    for start in range(0, span, piece):
        rows = slice(start, start + piece)
        p0, p1, p2, p3 = (
            jnp.dot(tab_ref[r, rows, :], weights[r], preferred_element_type=jnp.float32)
            for r in range(4)
        )
        odd, turned = p1[:, :group] + p3[:, :group], p1[:, group:] - p3[:, group:]
        even, gap = p0 + p2, p0 - p2
        for q, value in enumerate((even + odd, gap + turned, even - odd, gap - turned)):
            psi_ref[q * span + start : q * span + start + piece, :] = value.astype(jnp.bfloat16)

    width = 4 * channels
    section_row = sections_ref[...]
    lane_in_row = section_row % 8

    def quad(i, carry):
        cols = pl.ds(pl.multiple_of(i * width, width), width)
        series = jnp.dot(psi_ref[...], coef_ref[:, cols], preferred_element_type=jnp.float32)
        waveform = wave_t_ref[...].astype(jnp.float32)
        slot = lax.broadcasted_iota(jnp.int32, (8, channels), 0)
        for s in range(4):
            product = jnp.tanh(series[:, s * channels : (s + 1) * channels]) * waveform
            total = jnp.sum(product.reshape(samples // 8, 8, channels), axis=0)
            for shift in (4, 2, 1):
                total = total + pltpu.roll(total, shift, 0)
            rows = pl.ds(pl.multiple_of((sources - 1 - s - 4 * i) * 8, 8), 8)
            kept_ref[rows, :] = jnp.where(slot == lane_in_row, total, 0.0)
        return carry

    lax.fori_loop(0, sources // 4, quad, 0)

    own_rows = receivers // 4 // count // 8
    slots = lax.broadcasted_iota(jnp.int32, (count * 8, channels), 0)
    wanted = section_row // 8
    wanted = wanted // own_rows * 8 + wanted % own_rows
    member = (slots == wanted).astype(jnp.float32).astype(jnp.bfloat16)
    kept = kept_ref[...] * (1.0 / math.sqrt(samples * 4))
    high = kept.astype(jnp.bfloat16)
    low = (kept - high.astype(jnp.float32)).astype(jnp.bfloat16)
    across = (((1,), (1,)), ((), ()))
    blocks = lax.dot_general(
        jnp.concatenate([member, member], axis=1),
        jnp.concatenate([high, low], axis=1),
        across,
        preferred_element_type=jnp.float32,
    )
    block_ref[...] = blocks.reshape(count, 8, LANES)

    pl.semaphore_wait(barrier, count - 1)

    def copy_to(target, source):
        return pltpu.make_async_remote_copy(
            src_ref=block_ref.at[target],
            dst_ref=held_ref.at[source],
            send_sem=send_sem.at[target],
            recv_sem=recv_sem.at[source],
            device_id=place(target),
            device_id_type=pl.DeviceIdType.MESH,
        )

    def send(i, carry):
        copy_to((me + i) % count, me).start()
        return carry

    lax.fori_loop(1, count, send, 0)

    def receive(i, total):
        source = (me + count - i) % count
        copy_to(source, source).wait_recv()
        return total + held_ref[source]

    total = lax.fori_loop(1, count, receive, block_ref[me])

    halves = [jnp.zeros((8, LANES), jnp.float32)] * (sources // 8)
    for r in range(own_rows):
        spread_row = jnp.broadcast_to(total[r : r + 1, :], (8, LANES))
        moved = pltpu.roll(spread_row, 0, 1, stride=8, stride_axis=0)
        for h in range(sources // 8):
            placed = pltpu.roll(moved, (8 * r + 8 + 64 * h) % LANES, 1)
            halves[h] = jnp.where(lane // 8 == r, placed, halves[h])
    out_ref[...] = jnp.concatenate(halves, axis=0)[:, : own_rows * 8]

    def drain(i, carry):
        copy_to((me + i) % count, me).wait_send()
        return carry

    lax.fori_loop(1, count, drain, 0)


def fast_fits(mesh_sizes, wavenumbers, source_shapes, source_depths, recorded):
    count = mesh_sizes[0] * mesh_sizes[1]
    bins = wavenumbers.shape[0]
    channels, samples = recorded.shape
    own = channels // 4
    return (
        channels == LANES
        and source_depths.shape[0] * 8 == LANES
        and source_shapes.shape[1] * 4 * FAST_HALF == LANES
        and bins == 4 * LANES
        and samples % (4 * LANES) == 0
        and own % 8 == 0
        and own // 8 <= 8
        and count * 8 % LANES == 0
    )


def per_device(
    mesh_sizes,
    wavenumbers,
    receiver_shapes,
    source_shapes,
    mode_counts,
    source_depths,
    source_ranges,
    sections,
    recorded,
):
    args = (
        wavenumbers,
        receiver_shapes,
        source_shapes,
        mode_counts,
        source_depths,
        source_ranges,
        sections,
        recorded,
    )
    if not fast_fits(mesh_sizes, wavenumbers, source_shapes, source_depths, recorded):
        return per_device_general(mesh_sizes, *args)
    freq_size, sub_size = mesh_sizes
    count = freq_size * sub_size
    bins, modes = wavenumbers.shape
    depth_grid = source_shapes.shape[1]
    sources = source_depths.shape[0]
    channels, samples = recorded.shape
    receivers = channels * count
    reach = 2.0 * (channels - 1) / receivers
    top_phase = K_HALF * 0.5 * (reach + R_TOP)
    assert 2.0 * (0.5 * top_phase) ** FAST_TERMS / math.factorial(FAST_TERMS) < 1e-6

    extra = -modes % 8
    wave = wavenumbers.T
    live = jnp.arange(modes, dtype=jnp.int32)[:, None] < mode_counts[None, :]
    factor = receiver_shapes.T.astype(jnp.float32) * (8.0 / math.sqrt(bins))
    factor = jnp.where(live, factor / jnp.sqrt(wave * modes), 0.0)
    factor = jnp.pad(factor, ((0, extra), (0, 0)))
    wave = jnp.pad(wave, ((0, extra), (0, 0)), constant_values=K_MID)
    shape = (bins, modes, depth_grid, sources, channels, samples, mesh_sizes)
    group = depth_grid * 4 * FAST_HALF
    own = channels // 4
    return pl.pallas_call(
        functools.partial(score_kernel, shape),
        out_shape=jax.ShapeDtypeStruct((sources, own), jnp.float32),
        in_specs=[pl.BlockSpec(memory_space=pltpu.SMEM)] * 2
        + [pl.BlockSpec(memory_space=pltpu.VMEM)] * 6,
        out_specs=pl.BlockSpec(memory_space=pltpu.VMEM),
        scratch_shapes=[
            pltpu.VMEM((group, bins), jnp.float32),
            pltpu.VMEM((16, LANES), jnp.float32),
            pltpu.VMEM((FAST_TERMS * 8, LANES), jnp.float32),
            pltpu.VMEM((4, samples // 4, bins // 2), jnp.bfloat16),
            pltpu.VMEM((samples, group), jnp.bfloat16),
            pltpu.VMEM((group, sources * channels), jnp.bfloat16),
            pltpu.VMEM((samples, channels), jnp.bfloat16),
            pltpu.VMEM((sources * 8, channels), jnp.float32),
            pltpu.VMEM((count, 8, LANES), jnp.float32),
            pltpu.VMEM((count, 8, LANES), jnp.float32),
            pltpu.SemaphoreType.DMA((count,)),
            pltpu.SemaphoreType.DMA((count,)),
        ],
        compiler_params=pltpu.CompilerParams(
            vmem_limit_bytes=48 * 1024 * 1024, collective_id=1, has_side_effects=True
        ),
        name="score",
    )(
        source_depths,
        source_ranges,
        jnp.asarray(fast_constants()),
        sections.reshape(1, channels),
        wave,
        factor,
        source_shapes.transpose(2, 1, 0),
        recorded,
    )


def per_device_general(
    mesh_sizes,
    wavenumbers,
    receiver_shapes,
    source_shapes,
    mode_counts,
    source_depths,
    source_ranges,
    sections,
    recorded,
):
    freq_size, sub_size = mesh_sizes
    count = freq_size * sub_size
    me = lax.axis_index("freq") * sub_size + lax.axis_index("sub")
    bins, modes = wavenumbers.shape
    depth_grid = source_shapes.shape[1]
    sources = source_depths.shape[0]
    channels, samples = recorded.shape
    receivers = channels * count

    first_x = 1.0 + 2.0 * (me * channels).astype(jnp.float32) / receivers
    reach = 2.0 * (channels - 1) / receivers
    centre = first_x + 0.5 * (reach - R_TOP)
    top_phase = K_HALF * 0.5 * (reach + R_TOP)
    assert 2.0 * (0.5 * top_phase) ** TERMS / math.factorial(TERMS) < 1e-9
    assert depth_grid * 2 * TERMS <= LANES

    extra = -modes % 8
    wave = wavenumbers.T
    live = jnp.arange(modes, dtype=jnp.int32)[:, None] < mode_counts[None, :]
    factor = receiver_shapes.T.astype(jnp.float32) * (8.0 / math.sqrt(bins))
    factor = jnp.where(live, factor / jnp.sqrt(wave * modes), 0.0)
    factor = jnp.pad(factor, ((0, extra), (0, 0)))
    wave = jnp.pad(wave, ((0, extra), (0, 0)), constant_values=K_MID)
    shape = (bins, modes, depth_grid, sources, channels, samples, receivers)
    matched = pl.pallas_call(
        functools.partial(replica_kernel, shape),
        out_shape=jax.ShapeDtypeStruct((channels, LANES), jnp.float32),
        in_specs=[pl.BlockSpec(memory_space=pltpu.SMEM)] * 3
        + [pl.BlockSpec(memory_space=pltpu.VMEM)] * 5,
        out_specs=pl.BlockSpec(memory_space=pltpu.VMEM),
        scratch_shapes=[
            pltpu.VMEM((depth_grid * 2 * TERMS, bins), jnp.float32),
            pltpu.VMEM((16, LANES), jnp.float32),
            pltpu.VMEM((TERMS * 8, LANES), jnp.float32),
            pltpu.VMEM((bins // 2, samples // 4), jnp.bfloat16),
            pltpu.VMEM((4, depth_grid * 2 * TERMS, samples // 4), jnp.float32),
            pltpu.VMEM((depth_grid * 2 * TERMS, samples), jnp.bfloat16),
            pltpu.VMEM((sources, channels, 2 * TERMS), jnp.bfloat16),
        ],
        compiler_params=pltpu.CompilerParams(vmem_limit_bytes=48 * 1024 * 1024),
        name="replica",
    )(
        source_depths,
        jnp.stack([first_x, centre]),
        source_ranges,
        jnp.asarray(term_constants()),
        wave,
        factor,
        source_shapes.transpose(2, 1, 0),
        recorded,
    )

    section_count = receivers // 4
    own = section_count // count
    per_row = min(LANES // sources, own)
    own_rows = own // per_row
    assert LANES % sources == 0 and own % per_row == 0
    padded = -(-own_rows // 8) * 8
    slot = jnp.arange(count * padded, dtype=jnp.int32)
    wanted = jnp.where(
        slot % padded < own_rows, slot // padded * own_rows + slot % padded, -1
    )
    member = (wanted[:, None] == (sections // per_row)[None, :]).astype(jnp.float32)
    lane_part = jnp.arange(LANES, dtype=jnp.int32) // sources
    kept = jnp.where((sections % per_row)[:, None] == lane_part[None, :], matched, 0.0)
    blocks = jnp.dot(member, kept, precision=lax.Precision.HIGHEST) * (
        1.0 / math.sqrt(samples * (receivers // section_count))
    )
    blocks = blocks.reshape(count, padded, LANES)
    total = pl.pallas_call(
        functools.partial(exchange_kernel, (freq_size, sub_size)),
        out_shape=jax.ShapeDtypeStruct((padded, LANES), jnp.float32),
        in_specs=[pl.BlockSpec(memory_space=pltpu.VMEM)],
        out_specs=pl.BlockSpec(memory_space=pltpu.VMEM),
        scratch_shapes=[
            pltpu.VMEM((count, padded, LANES), jnp.float32),
            pltpu.SemaphoreType.DMA((count,)),
            pltpu.SemaphoreType.DMA((count,)),
        ],
        compiler_params=pltpu.CompilerParams(collective_id=0, has_side_effects=True),
        name="exchange",
    )(blocks)
    total = total[:own_rows, : per_row * sources].reshape(own_rows, per_row, sources)
    return total.transpose(2, 0, 1).reshape(sources, own)


def solution(mesh):
    sizes = (mesh.shape["freq"], mesh.shape["sub"])
    in_specs = (
        P(),
        P(),
        P(),
        P(),
        P("groups"),
        P("groups"),
        P(("freq", "sub")),
        P(("freq", "sub"), None),
    )
    out_specs = P("groups", ("freq", "sub"))
    return jax.shard_map(
        functools.partial(per_device, sizes),
        mesh=mesh,
        in_specs=in_specs,
        out_specs=out_specs,
        check_vma=False,
    )
```

```python
import functools
import math

import jax
import jax.numpy as jnp
import numpy as np
from jax import lax
from jax.experimental import pallas as pl
from jax.experimental.pallas import tpu as pltpu
from jax.sharding import PartitionSpec as P

MMIN = 64
F0 = 256
SPREAD = 16
K_LOW, K_TOP = 1.0, 20.0
R_TOP = 0.5
K_MID, K_HALF = 0.5 * (K_LOW + K_TOP), 0.5 * (K_TOP - K_LOW)
LANES = 128
TERMS = 16
TWO_PI = 2.0 * math.pi


def sincos_turns(turns):
    part = turns - jnp.floor(turns + 0.5)
    sq = part * part
    p2 = math.pi * math.pi
    s = jnp.full_like(part, -(p2**5) / math.factorial(11))
    for n in (9, 7, 5, 3, 1):
        s = s * sq + ((-1) ** ((n - 1) // 2)) * p2 ** ((n - 1) // 2) / math.factorial(n)
    s = s * (part * math.pi)
    c = jnp.full_like(part, p2**6 / math.factorial(12))
    for n in (10, 8, 6, 4, 2, 0):
        c = c * sq + ((-1) ** (n // 2)) * p2 ** (n // 2) / math.factorial(n)
    return 1.0 - 2.0 * s * s, 2.0 * s * c


def term_constants():
    nodes = np.cos(np.pi * (np.arange(TERMS) + 0.5) / TERMS)[: TERMS // 2]
    order = np.arange(TERMS)
    table = np.cos(order[:, None] * np.arccos(nodes)[None, :])
    table *= (np.where(order == 0, 1.0, 2.0) * 2.0 / TERMS)[:, None]
    half = TERMS // 2
    out = np.zeros((half, LANES), np.float32)
    out[:, 0] = K_HALF * nodes
    out[:, 1 : 1 + half] = table[0::2]
    out[:, 1 + half : 1 + 2 * half] = table[1::2]
    return out


def place_of(n):
    return n // 2 if n % 2 == 0 else TERMS // 2 + n // 2


def replica_kernel(
    shape,
    depths_ref,
    place_ref,
    ranges_ref,
    consts_ref,
    wave_ref,
    factor_ref,
    source_ref,
    recorded_ref,
    out_ref,
    sum_ref,
    weight_ref,
    term_ref,
    tab_ref,
    part_ref,
    psi_ref,
    coef_ref,
):
    bins, modes, depth_grid, sources, channels, samples, receivers = shape
    quarter = bins // 4
    span = samples // 4
    half = TERMS // 2
    first_x = place_ref[0]
    centre = place_ref[1]

    for first in range(0, bins, LANES):
        last = first + LANES - 1
        top = min(modes, MMIN + (modes - MMIN) * last // max(bins - 1, 1) + SPREAD)
        cols = slice(first, first + LANES)

        def modal(step, sums, cols=cols):
            start = pl.multiple_of(step * 8, 8)
            rows = pl.ds(start, 8)
            wave = wave_ref[rows, cols]
            cosine, sine = sincos_turns(wave * (centre * (1.0 / TWO_PI)))
            factor = factor_ref[rows, cols]
            weight_ref[0:8, :] = factor * cosine
            weight_ref[8:16, :] = factor * sine
            xi = (wave - K_MID) * (1.0 / K_HALF)
            before, now = jnp.ones_like(xi), xi
            for n in range(1, TERMS):
                term_ref[n * 8 : n * 8 + 8, :] = now
                before, now = now, 2.0 * xi * now - before
            sums = list(sums)
            for i in range(8):
                source = source_ref[jnp.minimum(start + i, modes - 1), :, cols].astype(jnp.float32)
                value = jnp.concatenate(
                    [source * weight_ref[i : i + 1, :], source * weight_ref[8 + i : 9 + i, :]], axis=0
                )
                sums[0] = sums[0] + value
                for n in range(1, TERMS):
                    sums[n] = sums[n] + value * term_ref[n * 8 + i : n * 8 + i + 1, :]
            return tuple(sums)

        zero = jnp.zeros((2 * depth_grid, LANES), jnp.float32)
        sums = lax.fori_loop(0, -(-top // 8), modal, (zero,) * TERMS)
        for n in range(TERMS):
            for z in range(depth_grid):
                for c in range(2):
                    at = z * 2 * TERMS + c * TERMS + place_of(n)
                    row = c * depth_grid + z
                    sum_ref[at : at + 1, cols] = sums[n][row : row + 1, :]

    def times_i(value):
        blocks = []
        for z in range(depth_grid):
            base = z * 2 * TERMS
            blocks.append(-value[base + TERMS : base + 2 * TERMS])
            blocks.append(value[base : base + TERMS])
        return jnp.concatenate(blocks, axis=0)

    moments = sum_ref[...]
    moments = jnp.concatenate([moments, -times_i(moments)], axis=0).astype(jnp.bfloat16)
    group = depth_grid * 2 * TERMS

    for r in range(4):
        row = lax.broadcasted_iota(jnp.int32, (quarter, LANES), 0)
        column = lax.broadcasted_iota(jnp.int32, (quarter, LANES), 1)
        number = F0 + 4 * row + r
        whole = (number * column) % samples
        cosine, sine = sincos_turns(whole.astype(jnp.float32) * (1.0 / samples))
        turn = (number * LANES) % samples
        step_c, step_s = sincos_turns(turn.astype(jnp.float32) * (1.0 / samples))
        for block in range(span // LANES):
            cols = slice(block * LANES, (block + 1) * LANES)
            tab_ref[:quarter, cols] = cosine.astype(jnp.bfloat16)
            tab_ref[quarter:, cols] = (-sine).astype(jnp.bfloat16)
            cosine, sine = cosine * step_c - sine * step_s, cosine * step_s + sine * step_c
        bin_row = lax.broadcasted_iota(jnp.int32, (bins, quarter), 0)
        bin_column = lax.broadcasted_iota(jnp.int32, (bins, quarter), 1)
        chosen = (bin_row == 4 * bin_column + r).astype(jnp.float32).astype(jnp.bfloat16)
        picked = jnp.dot(moments, chosen, preferred_element_type=jnp.float32)
        left = jnp.concatenate([picked[:group], picked[group:]], axis=1)
        part_ref[r] = jnp.dot(
            left.astype(jnp.bfloat16), tab_ref[...], preferred_element_type=jnp.float32
        )

    for block in range(span // LANES):
        cols = slice(block * LANES, (block + 1) * LANES)
        p0, p1, p2, p3 = (part_ref[r, :, cols] for r in range(4))
        even, odd = p0 + p2, p1 + p3
        gap, turned = p0 - p2, times_i(p1 - p3)
        for q, value in enumerate((even + odd, gap + turned, even - odd, gap - turned)):
            at = q * span + block * LANES
            psi_ref[:, at : at + LANES] = value.astype(jnp.bfloat16)

    channel = lax.broadcasted_iota(jnp.int32, (1, channels), 1).astype(jnp.float32)
    position = first_x + channel * (2.0 / receivers)
    spread = lax.rsqrt(position)
    nodes = consts_ref[:, 0:1]
    for s in range(sources):
        offset = position - (ranges_ref[s] + centre)
        cosine, sine = sincos_turns(nodes * offset * (1.0 / TWO_PI))
        even = jnp.zeros((half, channels), jnp.float32)
        odd = jnp.zeros((half, channels), jnp.float32)
        for j in range(half):
            even = even + consts_ref[:, 1 + j : 2 + j] * cosine[j : j + 1, :]
            odd = odd + consts_ref[:, 1 + half + j : 2 + half + j] * sine[j : j + 1, :]
        mid_c, mid_s = sincos_turns(offset * (K_MID / TWO_PI))
        mid_c, mid_s = mid_c * spread, mid_s * spread
        rows = jnp.concatenate([mid_c * even, -mid_s * odd, -mid_s * even, -mid_c * odd], axis=0)
        coef_ref[s] = rows.T.astype(jnp.bfloat16)

    chunk = 512

    def source(s, matched):
        z = depths_ref[s]
        terms = pl.ds(pl.multiple_of(z * (2 * TERMS), 2 * TERMS), 2 * TERMS)
        coef = coef_ref[s]
        total = jnp.zeros((channels, LANES), jnp.float32)
        for start in range(0, samples, chunk):
            series = jnp.dot(
                coef, psi_ref[terms, start : start + chunk], preferred_element_type=jnp.float32
            )
            product = jnp.tanh(series) * recorded_ref[:, start : start + chunk].astype(jnp.float32)
            for tile in range(chunk // LANES):
                total = total + product[:, tile * LANES : (tile + 1) * LANES]
        value = jnp.sum(total, axis=1, keepdims=True)
        lane = lax.broadcasted_iota(jnp.int32, (channels, LANES), 1)
        return jnp.where(lane % sources == s, value, matched)

    out_ref[...] = lax.fori_loop(
        0, sources, source, jnp.zeros((channels, LANES), jnp.float32)
    )


def exchange_kernel(sizes, block_ref, out_ref, held_ref, send_sem, recv_sem):
    freq_size, sub_size = sizes
    count = freq_size * sub_size
    me = lax.axis_index("freq") * sub_size + lax.axis_index("sub")
    barrier = pltpu.get_barrier_semaphore()

    def place(number):
        return {"freq": number // sub_size, "sub": number % sub_size}

    def greet(i, carry):
        pl.semaphore_signal(
            barrier,
            inc=1,
            device_id=place((me + i) % count),
            device_id_type=pl.DeviceIdType.MESH,
        )
        return carry

    lax.fori_loop(1, count, greet, 0)
    pl.semaphore_wait(barrier, count - 1)

    def copy_to(target, source):
        return pltpu.make_async_remote_copy(
            src_ref=block_ref.at[target],
            dst_ref=held_ref.at[source],
            send_sem=send_sem.at[target],
            recv_sem=recv_sem.at[source],
            device_id=place(target),
            device_id_type=pl.DeviceIdType.MESH,
        )

    def send(i, carry):
        copy_to((me + i) % count, me).start()
        return carry

    lax.fori_loop(1, count, send, 0)

    def receive(i, total):
        source = (me + count - i) % count
        copy_to(source, source).wait_recv()
        return total + held_ref[source]

    out_ref[...] = lax.fori_loop(1, count, receive, block_ref[me])

    def drain(i, carry):
        copy_to((me + i) % count, me).wait_send()
        return carry

    lax.fori_loop(1, count, drain, 0)

FAST_TERMS = 12
FAST_HALF = 8


def fast_constants():
    nodes = np.cos(np.pi * (np.arange(FAST_TERMS) + 0.5) / FAST_TERMS)[: FAST_TERMS // 2]
    order = np.arange(FAST_TERMS)
    table = np.cos(order[:, None] * np.arccos(nodes)[None, :])
    table *= (np.where(order == 0, 1.0, 2.0) * 2.0 / FAST_TERMS)[:, None]
    half = FAST_TERMS // 2
    out = np.zeros((FAST_HALF, LANES), np.float32)
    out[:half, 0] = K_HALF * nodes
    out[half, 0] = K_MID
    out[:half, 1 : 1 + half] = table[0::2]
    out[:half, 1 + half : 1 + 2 * half] = table[1::2]
    return out


def fast_place(n):
    return n // 2 if n % 2 == 0 else FAST_HALF + n // 2


def score_kernel(
    shape,
    depths_hbm,
    ranges_hbm,
    consts_hbm,
    sections_hbm,
    counts_hbm,
    wave_hbm,
    receiver_hbm,
    source_hbm,
    recorded_hbm,
    out_ref,
    depths_ref,
    ranges_ref,
    consts_ref,
    sections_ref,
    counts_ref,
    wave_ref,
    receiver_ref,
    source_ref,
    recorded_ref,
    left_ref,
    xi_ref,
    apart_ref,
    moment_ref,
    tab_ref,
    psi_ref,
    coef_ref,
    wave_t_ref,
    kept_ref,
    block_ref,
    held_ref,
    load_sem,
    send_sem,
    recv_sem,
):
    bins, modes, depth_grid, sources, channels, samples, sizes = shape
    freq_size, sub_size = sizes
    count = freq_size * sub_size
    receivers = channels * count
    quarter = bins // 4
    span = samples // 4
    half = FAST_TERMS // 2
    group = depth_grid * 4 * FAST_HALF
    me = lax.axis_index("freq") * sub_size + lax.axis_index("sub")
    barrier = pltpu.get_barrier_semaphore()

    loads = [
        pltpu.make_async_copy(source, target, load_sem.at[i])
        for i, (source, target) in enumerate(
            (
                (wave_hbm, wave_ref),
                (receiver_hbm, receiver_ref),
                (source_hbm, source_ref),
                (recorded_hbm, recorded_ref),
                (depths_hbm, depths_ref),
                (ranges_hbm, ranges_ref),
                (consts_hbm, consts_ref),
                (sections_hbm, sections_ref),
                (counts_hbm, counts_ref),
            )
        )
    ]
    for load in loads:
        load.start()

    my_freq = lax.axis_index("freq")
    my_sub = lax.axis_index("sub")
    partners = [(i, j) for i in range(freq_size) for j in range(sub_size) if i or j]

    def ahead(i, j):
        return lax.rem(my_freq + i, freq_size), lax.rem(my_sub + j, sub_size)

    for i, j in partners:
        freq, sub = ahead(i, j)
        pl.semaphore_signal(
            barrier,
            inc=1,
            device_id={"freq": freq, "sub": sub},
            device_id_type=pl.DeviceIdType.MESH,
        )

    reach = 2.0 * (channels - 1) / receivers
    first_x = 1.0 + (me * channels).astype(jnp.float32) * (2.0 / receivers)
    centre = first_x + 0.5 * (reach - R_TOP)

    lane = lax.broadcasted_iota(jnp.int32, (8, LANES), 1)
    row = lax.broadcasted_iota(jnp.int32, (8, LANES), 0)
    for r in range(4):
        number = F0 + 4 * lane + r
        whole = (number * row) % samples
        cosine, sine = sincos_turns(whole.astype(jnp.float32) * (1.0 / samples))
        turn = (number * 8) % samples
        step_c, step_s = sincos_turns(turn.astype(jnp.float32) * (1.0 / samples))
        for pair in range(span // 16):
            turned_c = cosine * step_c - sine * step_s
            turned_s = cosine * step_s + sine * step_c
            rows = slice(pair * 16, pair * 16 + 16)
            tab_ref[r, rows, :quarter] = jnp.concatenate([cosine, turned_c], axis=0).astype(jnp.bfloat16)
            tab_ref[r, rows, quarter:] = jnp.concatenate([sine, turned_s], axis=0).astype(jnp.bfloat16)
            cosine = turned_c * step_c - turned_s * step_s
            sine = turned_c * step_s + turned_s * step_c

    for load in loads[4:]:
        load.wait()

    channel = lax.broadcasted_iota(jnp.int32, (1, channels), 1).astype(jnp.float32)
    position = first_x + channel * (2.0 / receivers)
    spread = lax.rsqrt(position)
    nodes = consts_ref[:, 0:1]
    for s in range(sources):
        offset = position - (ranges_ref[s] + centre)
        cosine, sine = sincos_turns(nodes * offset * (1.0 / TWO_PI))
        even = jnp.zeros((FAST_HALF, channels), jnp.float32)
        odd = jnp.zeros((FAST_HALF, channels), jnp.float32)
        for j in range(half):
            even = even + consts_ref[:, 1 + j : 2 + j] * cosine[j : j + 1, :]
            odd = odd + consts_ref[:, 1 + half + j : 2 + half + j] * sine[j : j + 1, :]
        mid_c, mid_s = cosine[half : half + 1, :] * spread, sine[half : half + 1, :] * spread
        parts = jnp.concatenate([mid_c * even, -mid_s * odd, -mid_s * even, -mid_c * odd], axis=0)
        for z in range(depth_grid):
            here = jnp.where(depths_ref[s] == z, 1.0, 0.0)
            rows = slice(z * 4 * FAST_HALF, (z + 1) * 4 * FAST_HALF)
            coef_ref[rows, s * channels : (s + 1) * channels] = (parts * here).astype(jnp.bfloat16)

    def top_of(last):
        return min(modes, MMIN + (modes - MMIN) * last // max(bins - 1, 1) + SPREAD)

    loads[0].wait()
    loads[1].wait()
    loads[2].wait()
    padded = -(-modes // 16) * 16

    def filled(value, rows):
        lack = rows - value.shape[0]
        if lack == 0:
            return value
        return jnp.concatenate([value, jnp.zeros((lack, value.shape[1]), value.dtype)], axis=0)

    for first in range(0, bins, LANES):
        cols = slice(first, first + LANES)
        deep = -(-top_of(first + LANES - 1) // LANES) * LANES
        rows = min(-(-top_of(first + LANES - 1) // 16) * 16, modes)
        whole = -(-rows // 16) * 16
        wave = wave_ref[:rows, cols]
        cosine, sine = sincos_turns(wave * (centre * (1.0 / TWO_PI)))
        index = lax.broadcasted_iota(jnp.int32, (rows, LANES), 0)
        factor = receiver_ref[:rows, cols].astype(jnp.float32) * (8.0 / math.sqrt(bins * modes))
        factor = jnp.where(index < counts_ref[:, cols], factor * lax.rsqrt(wave), 0.0)
        xi = (wave - K_MID) * (1.0 / K_HALF)
        xi_ref[cols, :deep] = filled(filled(xi, whole), deep).T
        weights = (factor * cosine, factor * sine)
        source = jnp.transpose(source_ref[:rows, :, cols].astype(jnp.float32), (1, 0, 2))
        for z in range(depth_grid):
            for c in range(2):
                value = filled(source[z] * weights[c], whole).astype(jnp.bfloat16)
                left_ref[z * 2 + c, cols, :deep] = filled(value, deep).T

    loads[3].wait()
    for block in range(samples // LANES):
        rows = slice(block * LANES, (block + 1) * LANES)
        wave_t_ref[rows, :] = recorded_ref[:, rows].T

    across = (((1,), (1,)), ((), ()))
    terms = 2 * FAST_HALF
    kinds = 2 * depth_grid
    same_bin = (
        lax.broadcasted_iota(jnp.int32, (16, terms * 16), 0)
        == lax.broadcasted_iota(jnp.int32, (16, terms * 16), 1) % 16
    )
    for g in range(bins // 16):
        rows = slice(g * 16, g * 16 + 16)
        deep = -(-top_of(g * 16 + 15) // LANES) * LANES
        xi = xi_ref[rows, :deep]
        before, now = jnp.ones_like(xi), xi
        right = [before.astype(jnp.bfloat16)]
        for n in range(1, FAST_TERMS):
            right.append(now.astype(jnp.bfloat16))
            before, now = now, 2.0 * xi * now - before
        right = right + [jnp.zeros_like(right[0])] * (terms - FAST_TERMS)
        left = jnp.concatenate([left_ref[k, rows, :deep] for k in range(kinds)], axis=0)
        pairs = lax.dot_general(
            left, jnp.concatenate(right, axis=0), across, preferred_element_type=jnp.float32
        )
        for k in range(kinds):
            value = jnp.where(same_bin, pairs[k * 16 : k * 16 + 16], 0.0)
            apart_ref[rows, k * terms * 16 : (k + 1) * terms * 16] = value.astype(jnp.bfloat16)

    term = lax.broadcasted_iota(jnp.int32, (terms * 16, group), 0) // 16
    column = lax.broadcasted_iota(jnp.int32, (terms * 16, group), 1)
    column = column - (term // 2 + FAST_HALF * (term % 2))
    column = jnp.where(term < FAST_TERMS, column, -1)
    gathers = []
    for k in range(kinds):
        z, c = k // 2, k % 2
        plain = jnp.where(column == k * terms, 1.0, 0.0)
        turned = jnp.where(column == (z * 2 + 1 - c) * terms, 1.0 - 2.0 * c, 0.0)
        gathers.append(jnp.concatenate([plain, turned], axis=1).astype(jnp.bfloat16))
    moments = jnp.dot(
        apart_ref[...], jnp.concatenate(gathers, axis=0), preferred_element_type=jnp.float32
    )
    moment_ref[:bins, :] = moments[:, :group]
    moment_ref[bins:, :] = moments[:, group:]
    weights = []
    for r in range(4):
        plain = moment_ref[pl.ds(r, quarter, stride=4), :].astype(jnp.bfloat16)
        turned = moment_ref[pl.ds(bins + r, quarter, stride=4), :].astype(jnp.bfloat16)
        weight = jnp.concatenate([plain, turned], axis=0)
        if r % 2:
            weight = jnp.concatenate([weight, jnp.concatenate([turned, -plain], axis=0)], axis=1)
        weights.append(weight)
    piece = 128
    for start in range(0, span, piece):
        rows = slice(start, start + piece)
        p0, p1, p2, p3 = (
            jnp.dot(tab_ref[r, rows, :], weights[r], preferred_element_type=jnp.float32)
            for r in range(4)
        )
        odd, turned = p1[:, :group] + p3[:, :group], p1[:, group:] - p3[:, group:]
        even, gap = p0 + p2, p0 - p2
        for q, value in enumerate((even + odd, gap + turned, even - odd, gap - turned)):
            psi_ref[q * span + start : q * span + start + piece, :] = value.astype(jnp.bfloat16)

    width = 4 * channels
    section_row = sections_ref[...]
    lane_in_row = section_row % 8

    def quad(i, carry):
        cols = pl.ds(pl.multiple_of(i * width, width), width)
        series = jnp.dot(psi_ref[...], coef_ref[:, cols], preferred_element_type=jnp.float32)
        waveform = wave_t_ref[...].astype(jnp.float32)
        slot = lax.broadcasted_iota(jnp.int32, (8, channels), 0)
        for s in range(4):
            product = jnp.tanh(series[:, s * channels : (s + 1) * channels]) * waveform
            total = jnp.sum(product.reshape(samples // 8, 8, channels), axis=0)
            for shift in (4, 2, 1):
                total = total + pltpu.roll(total, shift, 0)
            rows = pl.ds(pl.multiple_of((sources - 1 - s - 4 * i) * 8, 8), 8)
            kept_ref[rows, :] = jnp.where(slot == lane_in_row, total, 0.0)
        return carry

    lax.fori_loop(0, sources // 4, quad, 0)

    own_rows = receivers // 4 // count // 8
    slots = lax.broadcasted_iota(jnp.int32, (count * 8, channels), 0)
    wanted = section_row // 8
    wanted = wanted // own_rows * 8 + wanted % own_rows
    member = (slots == wanted).astype(jnp.float32).astype(jnp.bfloat16)
    kept = kept_ref[...] * (1.0 / math.sqrt(samples * 4))
    high = kept.astype(jnp.bfloat16)
    low = (kept - high.astype(jnp.float32)).astype(jnp.bfloat16)
    blocks = lax.dot_general(
        jnp.concatenate([member, member], axis=1),
        jnp.concatenate([high, low], axis=1),
        across,
        preferred_element_type=jnp.float32,
    )
    block_ref[...] = blocks.reshape(count, 8, LANES)

    pl.semaphore_wait(barrier, count - 1)

    def copy_to(freq, sub, slot, source):
        return pltpu.make_async_remote_copy(
            src_ref=block_ref.at[freq * sub_size + sub],
            dst_ref=held_ref.at[source],
            send_sem=send_sem.at[slot],
            recv_sem=recv_sem.at[source],
            device_id={"freq": freq, "sub": sub},
            device_id_type=pl.DeviceIdType.MESH,
        )

    sends = []
    for slot, (i, j) in enumerate(partners):
        freq, sub = ahead(i, j)
        sends.append(copy_to(freq, sub, slot, me))
        sends[-1].start()
    total = block_ref[me]
    for slot, (i, j) in enumerate(partners):
        freq, sub = ahead(freq_size - i, sub_size - j)
        source = freq * sub_size + sub
        copy_to(freq, sub, slot, source).wait_recv()
        total = total + held_ref[source]

    halves = [jnp.zeros((8, LANES), jnp.float32)] * (sources // 8)
    for r in range(own_rows):
        spread_row = jnp.broadcast_to(total[r : r + 1, :], (8, LANES))
        moved = pltpu.roll(spread_row, 0, 1, stride=8, stride_axis=0)
        for h in range(sources // 8):
            placed = pltpu.roll(moved, (8 * r + 8 + 64 * h) % LANES, 1)
            halves[h] = jnp.where(lane // 8 == r, placed, halves[h])
    out_ref[...] = jnp.concatenate(halves, axis=0)[:, : own_rows * 8]

    for send in sends:
        send.wait_send()


def fast_fits(mesh_sizes, wavenumbers, source_shapes, source_depths, recorded):
    count = mesh_sizes[0] * mesh_sizes[1]
    bins = wavenumbers.shape[0]
    channels, samples = recorded.shape
    own = channels // 4
    return (
        channels == LANES
        and source_depths.shape[0] * 8 == LANES
        and source_shapes.shape[1] * 4 * FAST_HALF == LANES
        and bins == 4 * LANES
        and samples % (4 * LANES) == 0
        and own % 8 == 0
        and own // 8 <= 8
        and count * 8 % LANES == 0
    )


def per_device(
    mesh_sizes,
    wavenumbers,
    receiver_shapes,
    source_shapes,
    mode_counts,
    source_depths,
    source_ranges,
    sections,
    recorded,
):
    args = (
        wavenumbers,
        receiver_shapes,
        source_shapes,
        mode_counts,
        source_depths,
        source_ranges,
        sections,
        recorded,
    )
    if not fast_fits(mesh_sizes, wavenumbers, source_shapes, source_depths, recorded):
        return per_device_general(mesh_sizes, *args)
    freq_size, sub_size = mesh_sizes
    count = freq_size * sub_size
    bins, modes = wavenumbers.shape
    depth_grid = source_shapes.shape[1]
    sources = source_depths.shape[0]
    channels, samples = recorded.shape
    receivers = channels * count
    reach = 2.0 * (channels - 1) / receivers
    top_phase = K_HALF * 0.5 * (reach + R_TOP)
    assert 2.0 * (0.5 * top_phase) ** FAST_TERMS / math.factorial(FAST_TERMS) < 1e-6

    shape = (bins, modes, depth_grid, sources, channels, samples, mesh_sizes)
    group = depth_grid * 4 * FAST_HALF
    deep = -(-modes // LANES) * LANES
    own = channels // 4
    return pl.pallas_call(
        functools.partial(score_kernel, shape),
        out_shape=jax.ShapeDtypeStruct((sources, own), jnp.float32),
        in_specs=[pl.BlockSpec(memory_space=pltpu.HBM)] * 9,
        out_specs=pl.BlockSpec(memory_space=pltpu.VMEM),
        scratch_shapes=[
            pltpu.SMEM((sources,), jnp.int32),
            pltpu.SMEM((sources,), jnp.float32),
            pltpu.VMEM((FAST_HALF, LANES), jnp.float32),
            pltpu.VMEM((1, channels), jnp.int32),
            pltpu.VMEM((1, bins), jnp.int32),
            pltpu.VMEM((modes, bins), jnp.float32),
            pltpu.VMEM((modes, bins), jnp.bfloat16),
            pltpu.VMEM((modes, depth_grid, bins), jnp.bfloat16),
            pltpu.VMEM((channels, samples), jnp.bfloat16),
            pltpu.VMEM((2 * depth_grid, bins, deep), jnp.bfloat16),
            pltpu.VMEM((bins, deep), jnp.float32),
            pltpu.VMEM((bins, group * 2 * FAST_HALF), jnp.bfloat16),
            pltpu.VMEM((2 * bins, group), jnp.float32),
            pltpu.VMEM((4, samples // 4, bins // 2), jnp.bfloat16),
            pltpu.VMEM((samples, group), jnp.bfloat16),
            pltpu.VMEM((group, sources * channels), jnp.bfloat16),
            pltpu.VMEM((samples, channels), jnp.bfloat16),
            pltpu.VMEM((sources * 8, channels), jnp.float32),
            pltpu.VMEM((count, 8, LANES), jnp.float32),
            pltpu.VMEM((count, 8, LANES), jnp.float32),
            pltpu.SemaphoreType.DMA((9,)),
            pltpu.SemaphoreType.DMA((count - 1,)),
            pltpu.SemaphoreType.DMA((count,)),
        ],
        compiler_params=pltpu.CompilerParams(
            vmem_limit_bytes=48 * 1024 * 1024, collective_id=1, has_side_effects=True
        ),
        name="score",
    )(
        source_depths,
        source_ranges,
        jnp.asarray(fast_constants()),
        sections.reshape(1, channels),
        mode_counts.reshape(1, bins),
        wavenumbers.T,
        receiver_shapes.T,
        source_shapes.transpose(2, 1, 0),
        recorded,
    )


def per_device_general(
    mesh_sizes,
    wavenumbers,
    receiver_shapes,
    source_shapes,
    mode_counts,
    source_depths,
    source_ranges,
    sections,
    recorded,
):
    freq_size, sub_size = mesh_sizes
    count = freq_size * sub_size
    me = lax.axis_index("freq") * sub_size + lax.axis_index("sub")
    bins, modes = wavenumbers.shape
    depth_grid = source_shapes.shape[1]
    sources = source_depths.shape[0]
    channels, samples = recorded.shape
    receivers = channels * count

    first_x = 1.0 + 2.0 * (me * channels).astype(jnp.float32) / receivers
    reach = 2.0 * (channels - 1) / receivers
    centre = first_x + 0.5 * (reach - R_TOP)
    top_phase = K_HALF * 0.5 * (reach + R_TOP)
    assert 2.0 * (0.5 * top_phase) ** TERMS / math.factorial(TERMS) < 1e-9
    assert depth_grid * 2 * TERMS <= LANES

    extra = -modes % 8
    wave = wavenumbers.T
    live = jnp.arange(modes, dtype=jnp.int32)[:, None] < mode_counts[None, :]
    factor = receiver_shapes.T.astype(jnp.float32) * (8.0 / math.sqrt(bins))
    factor = jnp.where(live, factor / jnp.sqrt(wave * modes), 0.0)
    factor = jnp.pad(factor, ((0, extra), (0, 0)))
    wave = jnp.pad(wave, ((0, extra), (0, 0)), constant_values=K_MID)
    shape = (bins, modes, depth_grid, sources, channels, samples, receivers)
    matched = pl.pallas_call(
        functools.partial(replica_kernel, shape),
        out_shape=jax.ShapeDtypeStruct((channels, LANES), jnp.float32),
        in_specs=[pl.BlockSpec(memory_space=pltpu.SMEM)] * 3
        + [pl.BlockSpec(memory_space=pltpu.VMEM)] * 5,
        out_specs=pl.BlockSpec(memory_space=pltpu.VMEM),
        scratch_shapes=[
            pltpu.VMEM((depth_grid * 2 * TERMS, bins), jnp.float32),
            pltpu.VMEM((16, LANES), jnp.float32),
            pltpu.VMEM((TERMS * 8, LANES), jnp.float32),
            pltpu.VMEM((bins // 2, samples // 4), jnp.bfloat16),
            pltpu.VMEM((4, depth_grid * 2 * TERMS, samples // 4), jnp.float32),
            pltpu.VMEM((depth_grid * 2 * TERMS, samples), jnp.bfloat16),
            pltpu.VMEM((sources, channels, 2 * TERMS), jnp.bfloat16),
        ],
        compiler_params=pltpu.CompilerParams(vmem_limit_bytes=48 * 1024 * 1024),
        name="replica",
    )(
        source_depths,
        jnp.stack([first_x, centre]),
        source_ranges,
        jnp.asarray(term_constants()),
        wave,
        factor,
        source_shapes.transpose(2, 1, 0),
        recorded,
    )

    section_count = receivers // 4
    own = section_count // count
    per_row = min(LANES // sources, own)
    own_rows = own // per_row
    assert LANES % sources == 0 and own % per_row == 0
    padded = -(-own_rows // 8) * 8
    slot = jnp.arange(count * padded, dtype=jnp.int32)
    wanted = jnp.where(
        slot % padded < own_rows, slot // padded * own_rows + slot % padded, -1
    )
    member = (wanted[:, None] == (sections // per_row)[None, :]).astype(jnp.float32)
    lane_part = jnp.arange(LANES, dtype=jnp.int32) // sources
    kept = jnp.where((sections % per_row)[:, None] == lane_part[None, :], matched, 0.0)
    blocks = jnp.dot(member, kept, precision=lax.Precision.HIGHEST) * (
        1.0 / math.sqrt(samples * (receivers // section_count))
    )
    blocks = blocks.reshape(count, padded, LANES)
    total = pl.pallas_call(
        functools.partial(exchange_kernel, (freq_size, sub_size)),
        out_shape=jax.ShapeDtypeStruct((padded, LANES), jnp.float32),
        in_specs=[pl.BlockSpec(memory_space=pltpu.VMEM)],
        out_specs=pl.BlockSpec(memory_space=pltpu.VMEM),
        scratch_shapes=[
            pltpu.VMEM((count, padded, LANES), jnp.float32),
            pltpu.SemaphoreType.DMA((count,)),
            pltpu.SemaphoreType.DMA((count,)),
        ],
        compiler_params=pltpu.CompilerParams(collective_id=0, has_side_effects=True),
        name="exchange",
    )(blocks)
    total = total[:own_rows, : per_row * sources].reshape(own_rows, per_row, sources)
    return total.transpose(2, 0, 1).reshape(sources, own)


def solution(mesh):
    sizes = (mesh.shape["freq"], mesh.shape["sub"])
    in_specs = (
        P(),
        P(),
        P(),
        P(),
        P("groups"),
        P("groups"),
        P(("freq", "sub")),
        P(("freq", "sub"), None),
    )
    out_specs = P("groups", ("freq", "sub"))
    return jax.shard_map(
        functools.partial(per_device, sizes),
        mesh=mesh,
        in_specs=in_specs,
        out_specs=out_specs,
        check_vma=False,
    )
```

```python
import functools
import math

import jax
import jax.numpy as jnp
import numpy as np
from jax import lax
from jax.experimental import pallas as pl
from jax.experimental.pallas import tpu as pltpu
from jax.sharding import PartitionSpec as P

MMIN = 64
F0 = 256
SPREAD = 16
K_LOW, K_TOP = 1.0, 20.0
R_TOP = 0.5
K_MID, K_HALF = 0.5 * (K_LOW + K_TOP), 0.5 * (K_TOP - K_LOW)
LANES = 128
TERMS = 16
TWO_PI = 2.0 * math.pi


def sincos_turns(turns):
    part = turns - jnp.floor(turns + 0.5)
    sq = part * part
    p2 = math.pi * math.pi
    s = jnp.full_like(part, -(p2**5) / math.factorial(11))
    for n in (9, 7, 5, 3, 1):
        s = s * sq + ((-1) ** ((n - 1) // 2)) * p2 ** ((n - 1) // 2) / math.factorial(n)
    s = s * (part * math.pi)
    c = jnp.full_like(part, p2**6 / math.factorial(12))
    for n in (10, 8, 6, 4, 2, 0):
        c = c * sq + ((-1) ** (n // 2)) * p2 ** (n // 2) / math.factorial(n)
    return 1.0 - 2.0 * s * s, 2.0 * s * c


def term_constants():
    nodes = np.cos(np.pi * (np.arange(TERMS) + 0.5) / TERMS)[: TERMS // 2]
    order = np.arange(TERMS)
    table = np.cos(order[:, None] * np.arccos(nodes)[None, :])
    table *= (np.where(order == 0, 1.0, 2.0) * 2.0 / TERMS)[:, None]
    half = TERMS // 2
    out = np.zeros((half, LANES), np.float32)
    out[:, 0] = K_HALF * nodes
    out[:, 1 : 1 + half] = table[0::2]
    out[:, 1 + half : 1 + 2 * half] = table[1::2]
    return out


def place_of(n):
    return n // 2 if n % 2 == 0 else TERMS // 2 + n // 2


def replica_kernel(
    shape,
    depths_ref,
    place_ref,
    ranges_ref,
    consts_ref,
    wave_ref,
    factor_ref,
    source_ref,
    recorded_ref,
    out_ref,
    sum_ref,
    weight_ref,
    term_ref,
    tab_ref,
    part_ref,
    psi_ref,
    coef_ref,
):
    bins, modes, depth_grid, sources, channels, samples, receivers = shape
    quarter = bins // 4
    span = samples // 4
    half = TERMS // 2
    first_x = place_ref[0]
    centre = place_ref[1]

    for first in range(0, bins, LANES):
        last = first + LANES - 1
        top = min(modes, MMIN + (modes - MMIN) * last // max(bins - 1, 1) + SPREAD)
        cols = slice(first, first + LANES)

        def modal(step, sums, cols=cols):
            start = pl.multiple_of(step * 8, 8)
            rows = pl.ds(start, 8)
            wave = wave_ref[rows, cols]
            cosine, sine = sincos_turns(wave * (centre * (1.0 / TWO_PI)))
            factor = factor_ref[rows, cols]
            weight_ref[0:8, :] = factor * cosine
            weight_ref[8:16, :] = factor * sine
            xi = (wave - K_MID) * (1.0 / K_HALF)
            before, now = jnp.ones_like(xi), xi
            for n in range(1, TERMS):
                term_ref[n * 8 : n * 8 + 8, :] = now
                before, now = now, 2.0 * xi * now - before
            sums = list(sums)
            for i in range(8):
                source = source_ref[jnp.minimum(start + i, modes - 1), :, cols].astype(jnp.float32)
                value = jnp.concatenate(
                    [source * weight_ref[i : i + 1, :], source * weight_ref[8 + i : 9 + i, :]], axis=0
                )
                sums[0] = sums[0] + value
                for n in range(1, TERMS):
                    sums[n] = sums[n] + value * term_ref[n * 8 + i : n * 8 + i + 1, :]
            return tuple(sums)

        zero = jnp.zeros((2 * depth_grid, LANES), jnp.float32)
        sums = lax.fori_loop(0, -(-top // 8), modal, (zero,) * TERMS)
        for n in range(TERMS):
            for z in range(depth_grid):
                for c in range(2):
                    at = z * 2 * TERMS + c * TERMS + place_of(n)
                    row = c * depth_grid + z
                    sum_ref[at : at + 1, cols] = sums[n][row : row + 1, :]

    def times_i(value):
        blocks = []
        for z in range(depth_grid):
            base = z * 2 * TERMS
            blocks.append(-value[base + TERMS : base + 2 * TERMS])
            blocks.append(value[base : base + TERMS])
        return jnp.concatenate(blocks, axis=0)

    moments = sum_ref[...]
    moments = jnp.concatenate([moments, -times_i(moments)], axis=0).astype(jnp.bfloat16)
    group = depth_grid * 2 * TERMS

    for r in range(4):
        row = lax.broadcasted_iota(jnp.int32, (quarter, LANES), 0)
        column = lax.broadcasted_iota(jnp.int32, (quarter, LANES), 1)
        number = F0 + 4 * row + r
        whole = (number * column) % samples
        cosine, sine = sincos_turns(whole.astype(jnp.float32) * (1.0 / samples))
        turn = (number * LANES) % samples
        step_c, step_s = sincos_turns(turn.astype(jnp.float32) * (1.0 / samples))
        for block in range(span // LANES):
            cols = slice(block * LANES, (block + 1) * LANES)
            tab_ref[:quarter, cols] = cosine.astype(jnp.bfloat16)
            tab_ref[quarter:, cols] = (-sine).astype(jnp.bfloat16)
            cosine, sine = cosine * step_c - sine * step_s, cosine * step_s + sine * step_c
        bin_row = lax.broadcasted_iota(jnp.int32, (bins, quarter), 0)
        bin_column = lax.broadcasted_iota(jnp.int32, (bins, quarter), 1)
        chosen = (bin_row == 4 * bin_column + r).astype(jnp.float32).astype(jnp.bfloat16)
        picked = jnp.dot(moments, chosen, preferred_element_type=jnp.float32)
        left = jnp.concatenate([picked[:group], picked[group:]], axis=1)
        part_ref[r] = jnp.dot(
            left.astype(jnp.bfloat16), tab_ref[...], preferred_element_type=jnp.float32
        )

    for block in range(span // LANES):
        cols = slice(block * LANES, (block + 1) * LANES)
        p0, p1, p2, p3 = (part_ref[r, :, cols] for r in range(4))
        even, odd = p0 + p2, p1 + p3
        gap, turned = p0 - p2, times_i(p1 - p3)
        for q, value in enumerate((even + odd, gap + turned, even - odd, gap - turned)):
            at = q * span + block * LANES
            psi_ref[:, at : at + LANES] = value.astype(jnp.bfloat16)

    channel = lax.broadcasted_iota(jnp.int32, (1, channels), 1).astype(jnp.float32)
    position = first_x + channel * (2.0 / receivers)
    spread = lax.rsqrt(position)
    nodes = consts_ref[:, 0:1]
    for s in range(sources):
        offset = position - (ranges_ref[s] + centre)
        cosine, sine = sincos_turns(nodes * offset * (1.0 / TWO_PI))
        even = jnp.zeros((half, channels), jnp.float32)
        odd = jnp.zeros((half, channels), jnp.float32)
        for j in range(half):
            even = even + consts_ref[:, 1 + j : 2 + j] * cosine[j : j + 1, :]
            odd = odd + consts_ref[:, 1 + half + j : 2 + half + j] * sine[j : j + 1, :]
        mid_c, mid_s = sincos_turns(offset * (K_MID / TWO_PI))
        mid_c, mid_s = mid_c * spread, mid_s * spread
        rows = jnp.concatenate([mid_c * even, -mid_s * odd, -mid_s * even, -mid_c * odd], axis=0)
        coef_ref[s] = rows.T.astype(jnp.bfloat16)

    chunk = 512

    def source(s, matched):
        z = depths_ref[s]
        terms = pl.ds(pl.multiple_of(z * (2 * TERMS), 2 * TERMS), 2 * TERMS)
        coef = coef_ref[s]
        total = jnp.zeros((channels, LANES), jnp.float32)
        for start in range(0, samples, chunk):
            series = jnp.dot(
                coef, psi_ref[terms, start : start + chunk], preferred_element_type=jnp.float32
            )
            product = jnp.tanh(series) * recorded_ref[:, start : start + chunk].astype(jnp.float32)
            for tile in range(chunk // LANES):
                total = total + product[:, tile * LANES : (tile + 1) * LANES]
        value = jnp.sum(total, axis=1, keepdims=True)
        lane = lax.broadcasted_iota(jnp.int32, (channels, LANES), 1)
        return jnp.where(lane % sources == s, value, matched)

    out_ref[...] = lax.fori_loop(
        0, sources, source, jnp.zeros((channels, LANES), jnp.float32)
    )


def exchange_kernel(sizes, block_ref, out_ref, held_ref, send_sem, recv_sem):
    freq_size, sub_size = sizes
    count = freq_size * sub_size
    me = lax.axis_index("freq") * sub_size + lax.axis_index("sub")
    barrier = pltpu.get_barrier_semaphore()

    def place(number):
        return {"freq": number // sub_size, "sub": number % sub_size}

    def greet(i, carry):
        pl.semaphore_signal(
            barrier,
            inc=1,
            device_id=place((me + i) % count),
            device_id_type=pl.DeviceIdType.MESH,
        )
        return carry

    lax.fori_loop(1, count, greet, 0)
    pl.semaphore_wait(barrier, count - 1)

    def copy_to(target, source):
        return pltpu.make_async_remote_copy(
            src_ref=block_ref.at[target],
            dst_ref=held_ref.at[source],
            send_sem=send_sem.at[target],
            recv_sem=recv_sem.at[source],
            device_id=place(target),
            device_id_type=pl.DeviceIdType.MESH,
        )

    def send(i, carry):
        copy_to((me + i) % count, me).start()
        return carry

    lax.fori_loop(1, count, send, 0)

    def receive(i, total):
        source = (me + count - i) % count
        copy_to(source, source).wait_recv()
        return total + held_ref[source]

    out_ref[...] = lax.fori_loop(1, count, receive, block_ref[me])

    def drain(i, carry):
        copy_to((me + i) % count, me).wait_send()
        return carry

    lax.fori_loop(1, count, drain, 0)

FAST_TERMS = 12
FAST_HALF = 8


def fast_constants():
    nodes = np.cos(np.pi * (np.arange(FAST_TERMS) + 0.5) / FAST_TERMS)[: FAST_TERMS // 2]
    order = np.arange(FAST_TERMS)
    table = np.cos(order[:, None] * np.arccos(nodes)[None, :])
    table *= (np.where(order == 0, 1.0, 2.0) * 2.0 / FAST_TERMS)[:, None]
    half = FAST_TERMS // 2
    out = np.zeros((FAST_HALF, LANES), np.float32)
    out[:half, 0] = K_HALF * nodes
    out[half, 0] = K_MID
    out[:half, 1 : 1 + half] = table[0::2]
    out[:half, 1 + half : 1 + 2 * half] = table[1::2]
    return out


def fast_place(n):
    return n // 2 if n % 2 == 0 else FAST_HALF + n // 2


def score_kernel(
    shape,
    depths_hbm,
    ranges_hbm,
    consts_hbm,
    sections_hbm,
    counts_hbm,
    wave_hbm,
    receiver_hbm,
    source_hbm,
    recorded_hbm,
    out_ref,
    depths_ref,
    ranges_ref,
    consts_ref,
    sections_ref,
    counts_ref,
    wave_ref,
    receiver_ref,
    source_ref,
    recorded_ref,
    left_ref,
    xi_ref,
    apart_ref,
    moment_ref,
    tab_ref,
    psi_ref,
    coef_ref,
    wave_t_ref,
    kept_ref,
    block_ref,
    held_ref,
    load_sem,
    send_sem,
    recv_sem,
):
    bins, modes, depth_grid, sources, channels, samples, sizes = shape
    freq_size, sub_size = sizes
    count = freq_size * sub_size
    receivers = channels * count
    quarter = bins // 4
    span = samples // 4
    half = FAST_TERMS // 2
    group = depth_grid * 4 * FAST_HALF
    me = lax.axis_index("freq") * sub_size + lax.axis_index("sub")
    barrier = pltpu.get_barrier_semaphore()

    loads = [
        pltpu.make_async_copy(source, target, load_sem.at[i])
        for i, (source, target) in enumerate(
            (
                (wave_hbm, wave_ref),
                (receiver_hbm, receiver_ref),
                (source_hbm, source_ref),
                (recorded_hbm, recorded_ref),
                (depths_hbm, depths_ref),
                (ranges_hbm, ranges_ref),
                (consts_hbm, consts_ref),
                (sections_hbm, sections_ref),
                (counts_hbm, counts_ref),
            )
        )
    ]
    for load in loads:
        load.start()

    my_freq = lax.axis_index("freq")
    my_sub = lax.axis_index("sub")
    partners = [(i, j) for i in range(freq_size) for j in range(sub_size) if i or j]

    def ahead(i, j):
        return lax.rem(my_freq + i, freq_size), lax.rem(my_sub + j, sub_size)

    for i, j in partners:
        freq, sub = ahead(i, j)
        pl.semaphore_signal(
            barrier,
            inc=1,
            device_id={"freq": freq, "sub": sub},
            device_id_type=pl.DeviceIdType.MESH,
        )

    reach = 2.0 * (channels - 1) / receivers
    first_x = 1.0 + (me * channels).astype(jnp.float32) * (2.0 / receivers)
    centre = first_x + 0.5 * (reach - R_TOP)

    lane = lax.broadcasted_iota(jnp.int32, (8, LANES), 1)
    row = lax.broadcasted_iota(jnp.int32, (8, LANES), 0)
    for r in range(4):
        number = F0 + 4 * lane + r
        whole = (number * row) % samples
        cosine, sine = sincos_turns(whole.astype(jnp.float32) * (1.0 / samples))
        turn = (number * 8) % samples
        step_c, step_s = sincos_turns(turn.astype(jnp.float32) * (1.0 / samples))
        for pair in range(span // 16):
            turned_c = cosine * step_c - sine * step_s
            turned_s = cosine * step_s + sine * step_c
            rows = slice(pair * 16, pair * 16 + 16)
            tab_ref[r, rows, :quarter] = jnp.concatenate([cosine, turned_c], axis=0).astype(jnp.bfloat16)
            tab_ref[r, rows, quarter:] = jnp.concatenate([sine, turned_s], axis=0).astype(jnp.bfloat16)
            cosine = turned_c * step_c - turned_s * step_s
            sine = turned_c * step_s + turned_s * step_c

    for load in loads[4:]:
        load.wait()

    channel = lax.broadcasted_iota(jnp.int32, (1, channels), 1).astype(jnp.float32)
    position = first_x + channel * (2.0 / receivers)
    spread = lax.rsqrt(position)
    nodes = consts_ref[:, 0:1]
    for s in range(sources):
        offset = position - (ranges_ref[s] + centre)
        cosine, sine = sincos_turns(nodes * offset * (1.0 / TWO_PI))
        even = jnp.zeros((FAST_HALF, channels), jnp.float32)
        odd = jnp.zeros((FAST_HALF, channels), jnp.float32)
        for j in range(half):
            even = even + consts_ref[:, 1 + j : 2 + j] * cosine[j : j + 1, :]
            odd = odd + consts_ref[:, 1 + half + j : 2 + half + j] * sine[j : j + 1, :]
        mid_c, mid_s = cosine[half : half + 1, :] * spread, sine[half : half + 1, :] * spread
        parts = jnp.concatenate([mid_c * even, -mid_s * odd, -mid_s * even, -mid_c * odd], axis=0)
        for z in range(depth_grid):
            here = jnp.where(depths_ref[s] == z, 1.0, 0.0)
            rows = slice(z * 4 * FAST_HALF, (z + 1) * 4 * FAST_HALF)
            coef_ref[rows, s * channels : (s + 1) * channels] = (parts * here).astype(jnp.bfloat16)

    def top_of(last):
        return min(modes, MMIN + (modes - MMIN) * last // max(bins - 1, 1) + SPREAD)

    loads[0].wait()
    loads[1].wait()
    loads[2].wait()
    padded = -(-modes // 16) * 16

    def filled(value, rows):
        lack = rows - value.shape[0]
        if lack == 0:
            return value
        return jnp.concatenate([value, jnp.zeros((lack, value.shape[1]), value.dtype)], axis=0)

    for first in range(0, bins, LANES):
        cols = slice(first, first + LANES)
        deep = -(-top_of(first + LANES - 1) // LANES) * LANES
        rows = min(-(-top_of(first + LANES - 1) // 16) * 16, modes)
        whole = -(-rows // 16) * 16
        wave = wave_ref[:rows, cols]
        cosine, sine = sincos_turns(wave * (centre * (1.0 / TWO_PI)))
        index = lax.broadcasted_iota(jnp.int32, (rows, LANES), 0)
        factor = receiver_ref[:rows, cols].astype(jnp.float32) * (8.0 / math.sqrt(bins * modes))
        factor = jnp.where(index < counts_ref[:, cols], factor * lax.rsqrt(wave), 0.0)
        xi = (wave - K_MID) * (1.0 / K_HALF)
        xi_ref[cols, :deep] = filled(filled(xi, whole), deep).T
        weights = (factor * cosine, factor * sine)
        source = jnp.transpose(source_ref[:rows, :, cols].astype(jnp.float32), (1, 0, 2))
        for z in range(depth_grid):
            for c in range(2):
                value = filled(source[z] * weights[c], whole).astype(jnp.bfloat16)
                left_ref[z * 2 + c, cols, :deep] = filled(value, deep).T

    loads[3].wait()
    for block in range(samples // LANES):
        rows = slice(block * LANES, (block + 1) * LANES)
        wave_t_ref[rows, :] = recorded_ref[:, rows].T

    across = (((1,), (1,)), ((), ()))
    terms = 2 * FAST_HALF
    kinds = 2 * depth_grid
    same_bin = (
        lax.broadcasted_iota(jnp.int32, (16, terms * 16), 0)
        == lax.broadcasted_iota(jnp.int32, (16, terms * 16), 1) % 16
    )
    for g in range(bins // 16):
        rows = slice(g * 16, g * 16 + 16)
        deep = -(-top_of(g * 16 + 15) // LANES) * LANES
        xi = xi_ref[rows, :deep]
        before, now = jnp.ones_like(xi), xi
        right = [before.astype(jnp.bfloat16)]
        for n in range(1, FAST_TERMS):
            right.append(now.astype(jnp.bfloat16))
            before, now = now, 2.0 * xi * now - before
        right = right + [jnp.zeros_like(right[0])] * (terms - FAST_TERMS)
        left = jnp.concatenate([left_ref[k, rows, :deep] for k in range(kinds)], axis=0)
        pairs = lax.dot_general(
            left, jnp.concatenate(right, axis=0), across, preferred_element_type=jnp.float32
        )
        for k in range(kinds):
            value = jnp.where(same_bin, pairs[k * 16 : k * 16 + 16], 0.0)
            apart_ref[rows, k * terms * 16 : (k + 1) * terms * 16] = value.astype(jnp.bfloat16)

    term = lax.broadcasted_iota(jnp.int32, (terms * 16, group), 0) // 16
    column = lax.broadcasted_iota(jnp.int32, (terms * 16, group), 1)
    column = column - (term // 2 + FAST_HALF * (term % 2))
    column = jnp.where(term < FAST_TERMS, column, -1)
    gathers = []
    for k in range(kinds):
        z, c = k // 2, k % 2
        plain = jnp.where(column == k * terms, 1.0, 0.0)
        turned = jnp.where(column == (z * 2 + 1 - c) * terms, 1.0 - 2.0 * c, 0.0)
        gathers.append(jnp.concatenate([plain, turned], axis=1).astype(jnp.bfloat16))
    moments = jnp.dot(
        apart_ref[...], jnp.concatenate(gathers, axis=0), preferred_element_type=jnp.float32
    )
    moment_ref[:bins, :] = moments[:, :group]
    moment_ref[bins:, :] = moments[:, group:]
    weights = []
    for r in range(4):
        plain = moment_ref[pl.ds(r, quarter, stride=4), :].astype(jnp.bfloat16)
        turned = moment_ref[pl.ds(bins + r, quarter, stride=4), :].astype(jnp.bfloat16)
        weight = jnp.concatenate([plain, turned], axis=0)
        if r % 2:
            weight = jnp.concatenate([weight, jnp.concatenate([turned, -plain], axis=0)], axis=1)
        weights.append(weight)
    piece = 128
    for start in range(0, span, piece):
        rows = slice(start, start + piece)
        p0, p1, p2, p3 = (
            jnp.dot(tab_ref[r, rows, :], weights[r], preferred_element_type=jnp.float32)
            for r in range(4)
        )
        odd, turned = p1[:, :group] + p3[:, :group], p1[:, group:] - p3[:, group:]
        even, gap = p0 + p2, p0 - p2
        for q, value in enumerate((even + odd, gap + turned, even - odd, gap - turned)):
            psi_ref[q * span + start : q * span + start + piece, :] = value.astype(jnp.bfloat16)

    width = 4 * channels
    section_row = sections_ref[...]
    lane_in_row = section_row % 8

    def quad(i, carry):
        cols = pl.ds(pl.multiple_of(i * width, width), width)
        series = jnp.dot(psi_ref[...], coef_ref[:, cols], preferred_element_type=jnp.float32)
        waveform = wave_t_ref[...].astype(jnp.float32)
        slot = lax.broadcasted_iota(jnp.int32, (8, channels), 0)
        for s in range(4):
            product = jnp.tanh(series[:, s * channels : (s + 1) * channels]) * waveform
            total = jnp.sum(product.reshape(samples // 8, 8, channels), axis=0)
            for shift in (4, 2, 1):
                total = total + pltpu.roll(total, shift, 0)
            rows = pl.ds(pl.multiple_of((sources - 1 - s - 4 * i) * 8, 8), 8)
            kept_ref[rows, :] = jnp.where(slot == lane_in_row, total, 0.0)
        return carry

    lax.fori_loop(0, sources // 4, quad, 0)

    own_rows = receivers // 4 // count // 8
    slots = lax.broadcasted_iota(jnp.int32, (count * 8, channels), 0)
    wanted = section_row // 8
    wanted = wanted // own_rows * 8 + wanted % own_rows
    member = (slots == wanted).astype(jnp.float32).astype(jnp.bfloat16)
    kept = kept_ref[...] * (1.0 / math.sqrt(samples * 4))
    high = kept.astype(jnp.bfloat16)
    low = (kept - high.astype(jnp.float32)).astype(jnp.bfloat16)
    blocks = lax.dot_general(
        jnp.concatenate([member, member], axis=1),
        jnp.concatenate([high, low], axis=1),
        across,
        preferred_element_type=jnp.float32,
    )
    block_ref[...] = blocks.reshape(count, 8, LANES)

    pl.semaphore_wait(barrier, count - 1)

    def copy_to(freq, sub, slot, source):
        return pltpu.make_async_remote_copy(
            src_ref=block_ref.at[freq * sub_size + sub],
            dst_ref=held_ref.at[source],
            send_sem=send_sem.at[slot],
            recv_sem=recv_sem.at[source],
            device_id={"freq": freq, "sub": sub},
            device_id_type=pl.DeviceIdType.MESH,
        )

    sends = []
    for slot, (i, j) in enumerate(partners):
        freq, sub = ahead(i, j)
        sends.append(copy_to(freq, sub, slot, me))
        sends[-1].start()
    total = block_ref[me]
    for slot, (i, j) in enumerate(partners):
        freq, sub = ahead(freq_size - i, sub_size - j)
        source = freq * sub_size + sub
        copy_to(freq, sub, slot, source).wait_recv()
        total = total + held_ref[source]

    halves = [jnp.zeros((8, LANES), jnp.float32)] * (sources // 8)
    for r in range(own_rows):
        spread_row = jnp.broadcast_to(total[r : r + 1, :], (8, LANES))
        moved = pltpu.roll(spread_row, 0, 1, stride=8, stride_axis=0)
        for h in range(sources // 8):
            placed = pltpu.roll(moved, (8 * r + 8 + 64 * h) % LANES, 1)
            halves[h] = jnp.where(lane // 8 == r, placed, halves[h])
    out_ref[...] = jnp.concatenate(halves, axis=0)[:, : own_rows * 8]

    for send in sends:
        send.wait_send()


def fast_fits(mesh_sizes, wavenumbers, source_shapes, source_depths, recorded):
    count = mesh_sizes[0] * mesh_sizes[1]
    bins = wavenumbers.shape[0]
    channels, samples = recorded.shape
    own = channels // 4
    return (
        channels == LANES
        and source_depths.shape[0] * 8 == LANES
        and source_shapes.shape[1] * 4 * FAST_HALF == LANES
        and bins == 4 * LANES
        and samples % (4 * LANES) == 0
        and own % 8 == 0
        and own // 8 <= 8
        and count * 8 % LANES == 0
    )


def per_device(
    mesh_sizes,
    wavenumbers,
    receiver_shapes,
    source_shapes,
    mode_counts,
    source_depths,
    source_ranges,
    sections,
    recorded,
):
    args = (
        wavenumbers,
        receiver_shapes,
        source_shapes,
        mode_counts,
        source_depths,
        source_ranges,
        sections,
        recorded,
    )
    if not fast_fits(mesh_sizes, wavenumbers, source_shapes, source_depths, recorded):
        return per_device_general(mesh_sizes, *args)
    freq_size, sub_size = mesh_sizes
    count = freq_size * sub_size
    bins, modes = wavenumbers.shape
    depth_grid = source_shapes.shape[1]
    sources = source_depths.shape[0]
    channels, samples = recorded.shape
    receivers = channels * count
    reach = 2.0 * (channels - 1) / receivers
    top_phase = K_HALF * 0.5 * (reach + R_TOP)
    assert 2.0 * (0.5 * top_phase) ** FAST_TERMS / math.factorial(FAST_TERMS) < 1e-6

    shape = (bins, modes, depth_grid, sources, channels, samples, mesh_sizes)
    group = depth_grid * 4 * FAST_HALF
    deep = -(-modes // LANES) * LANES
    own = channels // 4
    return pl.pallas_call(
        functools.partial(score_kernel, shape),
        out_shape=jax.ShapeDtypeStruct((sources, own), jnp.float32),
        in_specs=[pl.BlockSpec(memory_space=pl.ANY)] * 9,
        out_specs=pl.BlockSpec(memory_space=pltpu.VMEM),
        scratch_shapes=[
            pltpu.SMEM((sources,), jnp.int32),
            pltpu.SMEM((sources,), jnp.float32),
            pltpu.VMEM((FAST_HALF, LANES), jnp.float32),
            pltpu.VMEM((1, channels), jnp.int32),
            pltpu.VMEM((1, bins), jnp.int32),
            pltpu.VMEM((modes, bins), jnp.float32),
            pltpu.VMEM((modes, bins), jnp.bfloat16),
            pltpu.VMEM((modes, depth_grid, bins), jnp.bfloat16),
            pltpu.VMEM((channels, samples), jnp.bfloat16),
            pltpu.VMEM((2 * depth_grid, bins, deep), jnp.bfloat16),
            pltpu.VMEM((bins, deep), jnp.float32),
            pltpu.VMEM((bins, group * 2 * FAST_HALF), jnp.bfloat16),
            pltpu.VMEM((2 * bins, group), jnp.float32),
            pltpu.VMEM((4, samples // 4, bins // 2), jnp.bfloat16),
            pltpu.VMEM((samples, group), jnp.bfloat16),
            pltpu.VMEM((group, sources * channels), jnp.bfloat16),
            pltpu.VMEM((samples, channels), jnp.bfloat16),
            pltpu.VMEM((sources * 8, channels), jnp.float32),
            pltpu.VMEM((count, 8, LANES), jnp.float32),
            pltpu.VMEM((count, 8, LANES), jnp.float32),
            pltpu.SemaphoreType.DMA((9,)),
            pltpu.SemaphoreType.DMA((count - 1,)),
            pltpu.SemaphoreType.DMA((count,)),
        ],
        compiler_params=pltpu.CompilerParams(
            vmem_limit_bytes=60 * 1024 * 1024, collective_id=1, has_side_effects=True
        ),
        name="score",
    )(
        source_depths,
        source_ranges,
        jnp.asarray(fast_constants()),
        sections.reshape(1, channels),
        mode_counts.reshape(1, bins),
        wavenumbers.T,
        receiver_shapes.T,
        source_shapes.transpose(2, 1, 0),
        recorded,
    )


def per_device_general(
    mesh_sizes,
    wavenumbers,
    receiver_shapes,
    source_shapes,
    mode_counts,
    source_depths,
    source_ranges,
    sections,
    recorded,
):
    freq_size, sub_size = mesh_sizes
    count = freq_size * sub_size
    me = lax.axis_index("freq") * sub_size + lax.axis_index("sub")
    bins, modes = wavenumbers.shape
    depth_grid = source_shapes.shape[1]
    sources = source_depths.shape[0]
    channels, samples = recorded.shape
    receivers = channels * count

    first_x = 1.0 + 2.0 * (me * channels).astype(jnp.float32) / receivers
    reach = 2.0 * (channels - 1) / receivers
    centre = first_x + 0.5 * (reach - R_TOP)
    top_phase = K_HALF * 0.5 * (reach + R_TOP)
    assert 2.0 * (0.5 * top_phase) ** TERMS / math.factorial(TERMS) < 1e-9
    assert depth_grid * 2 * TERMS <= LANES

    extra = -modes % 8
    wave = wavenumbers.T
    live = jnp.arange(modes, dtype=jnp.int32)[:, None] < mode_counts[None, :]
    factor = receiver_shapes.T.astype(jnp.float32) * (8.0 / math.sqrt(bins))
    factor = jnp.where(live, factor / jnp.sqrt(wave * modes), 0.0)
    factor = jnp.pad(factor, ((0, extra), (0, 0)))
    wave = jnp.pad(wave, ((0, extra), (0, 0)), constant_values=K_MID)
    shape = (bins, modes, depth_grid, sources, channels, samples, receivers)
    matched = pl.pallas_call(
        functools.partial(replica_kernel, shape),
        out_shape=jax.ShapeDtypeStruct((channels, LANES), jnp.float32),
        in_specs=[pl.BlockSpec(memory_space=pltpu.SMEM)] * 3
        + [pl.BlockSpec(memory_space=pltpu.VMEM)] * 5,
        out_specs=pl.BlockSpec(memory_space=pltpu.VMEM),
        scratch_shapes=[
            pltpu.VMEM((depth_grid * 2 * TERMS, bins), jnp.float32),
            pltpu.VMEM((16, LANES), jnp.float32),
            pltpu.VMEM((TERMS * 8, LANES), jnp.float32),
            pltpu.VMEM((bins // 2, samples // 4), jnp.bfloat16),
            pltpu.VMEM((4, depth_grid * 2 * TERMS, samples // 4), jnp.float32),
            pltpu.VMEM((depth_grid * 2 * TERMS, samples), jnp.bfloat16),
            pltpu.VMEM((sources, channels, 2 * TERMS), jnp.bfloat16),
        ],
        compiler_params=pltpu.CompilerParams(vmem_limit_bytes=48 * 1024 * 1024),
        name="replica",
    )(
        source_depths,
        jnp.stack([first_x, centre]),
        source_ranges,
        jnp.asarray(term_constants()),
        wave,
        factor,
        source_shapes.transpose(2, 1, 0),
        recorded,
    )

    section_count = receivers // 4
    own = section_count // count
    per_row = min(LANES // sources, own)
    own_rows = own // per_row
    assert LANES % sources == 0 and own % per_row == 0
    padded = -(-own_rows // 8) * 8
    slot = jnp.arange(count * padded, dtype=jnp.int32)
    wanted = jnp.where(
        slot % padded < own_rows, slot // padded * own_rows + slot % padded, -1
    )
    member = (wanted[:, None] == (sections // per_row)[None, :]).astype(jnp.float32)
    lane_part = jnp.arange(LANES, dtype=jnp.int32) // sources
    kept = jnp.where((sections % per_row)[:, None] == lane_part[None, :], matched, 0.0)
    blocks = jnp.dot(member, kept, precision=lax.Precision.HIGHEST) * (
        1.0 / math.sqrt(samples * (receivers // section_count))
    )
    blocks = blocks.reshape(count, padded, LANES)
    total = pl.pallas_call(
        functools.partial(exchange_kernel, (freq_size, sub_size)),
        out_shape=jax.ShapeDtypeStruct((padded, LANES), jnp.float32),
        in_specs=[pl.BlockSpec(memory_space=pltpu.VMEM)],
        out_specs=pl.BlockSpec(memory_space=pltpu.VMEM),
        scratch_shapes=[
            pltpu.VMEM((count, padded, LANES), jnp.float32),
            pltpu.SemaphoreType.DMA((count,)),
            pltpu.SemaphoreType.DMA((count,)),
        ],
        compiler_params=pltpu.CompilerParams(collective_id=0, has_side_effects=True),
        name="exchange",
    )(blocks)
    total = total[:own_rows, : per_row * sources].reshape(own_rows, per_row, sources)
    return total.transpose(2, 0, 1).reshape(sources, own)


def solution(mesh):
    sizes = (mesh.shape["freq"], mesh.shape["sub"])
    in_specs = (
        P(),
        P(),
        P(),
        P(),
        P("groups"),
        P("groups"),
        P(("freq", "sub")),
        P(("freq", "sub"), None),
    )
    out_specs = P("groups", ("freq", "sub"))
    return jax.shard_map(
        functools.partial(per_device, sizes),
        mesh=mesh,
        in_specs=in_specs,
        out_specs=out_specs,
        check_vma=False,
    )
```

```python
import functools
import math

import jax
import jax.numpy as jnp
import numpy as np
from jax import lax
from jax.experimental import pallas as pl
from jax.experimental.pallas import tpu as pltpu
from jax.sharding import PartitionSpec as P

MMIN = 64
F0 = 256
SPREAD = 16
K_LOW, K_TOP = 1.0, 20.0
R_TOP = 0.5
K_MID, K_HALF = 0.5 * (K_LOW + K_TOP), 0.5 * (K_TOP - K_LOW)
LANES = 128
TERMS = 16
TWO_PI = 2.0 * math.pi


def fitted(function, count):
    angle = np.pi * (np.arange(200) + 0.5) / 200
    square = 0.125 * (1.0 + np.cos(angle))
    series = np.polynomial.chebyshev.Chebyshev.fit(
        square, function(np.sqrt(square)), count - 1, domain=[0.0, 0.25]
    )
    return [float(c) for c in series.convert(kind=np.polynomial.Polynomial).coef]


SINE = fitted(lambda x: np.sin(np.pi * x) / x, 5)
COSINE = fitted(lambda x: np.cos(np.pi * x), 5)


def horner(coefficients, x):
    value = coefficients[-1] * x + coefficients[-2]
    for c in coefficients[-3::-1]:
        value = value * x + c
    return value


def sincos_turns(turns):
    part = turns - jnp.floor(turns + 0.5)
    square = part * part
    s = horner(SINE, square) * part
    c = horner(COSINE, square)
    twice = s + s
    return 1.0 - twice * s, twice * c


def term_constants():
    nodes = np.cos(np.pi * (np.arange(TERMS) + 0.5) / TERMS)[: TERMS // 2]
    order = np.arange(TERMS)
    table = np.cos(order[:, None] * np.arccos(nodes)[None, :])
    table *= (np.where(order == 0, 1.0, 2.0) * 2.0 / TERMS)[:, None]
    half = TERMS // 2
    out = np.zeros((half, LANES), np.float32)
    out[:, 0] = K_HALF * nodes
    out[:, 1 : 1 + half] = table[0::2]
    out[:, 1 + half : 1 + 2 * half] = table[1::2]
    return out


def place_of(n):
    return n // 2 if n % 2 == 0 else TERMS // 2 + n // 2


def replica_kernel(
    shape,
    depths_ref,
    place_ref,
    ranges_ref,
    consts_ref,
    wave_ref,
    factor_ref,
    source_ref,
    recorded_ref,
    out_ref,
    sum_ref,
    weight_ref,
    term_ref,
    tab_ref,
    part_ref,
    psi_ref,
    coef_ref,
):
    bins, modes, depth_grid, sources, channels, samples, receivers = shape
    quarter = bins // 4
    span = samples // 4
    half = TERMS // 2
    first_x = place_ref[0]
    centre = place_ref[1]

    for first in range(0, bins, LANES):
        last = first + LANES - 1
        top = min(modes, MMIN + (modes - MMIN) * last // max(bins - 1, 1) + SPREAD)
        cols = slice(first, first + LANES)

        def modal(step, sums, cols=cols):
            start = pl.multiple_of(step * 8, 8)
            rows = pl.ds(start, 8)
            wave = wave_ref[rows, cols]
            cosine, sine = sincos_turns(wave * (centre * (1.0 / TWO_PI)))
            factor = factor_ref[rows, cols]
            weight_ref[0:8, :] = factor * cosine
            weight_ref[8:16, :] = factor * sine
            xi = (wave - K_MID) * (1.0 / K_HALF)
            before, now = jnp.ones_like(xi), xi
            for n in range(1, TERMS):
                term_ref[n * 8 : n * 8 + 8, :] = now
                before, now = now, 2.0 * xi * now - before
            sums = list(sums)
            for i in range(8):
                source = source_ref[jnp.minimum(start + i, modes - 1), :, cols].astype(jnp.float32)
                value = jnp.concatenate(
                    [source * weight_ref[i : i + 1, :], source * weight_ref[8 + i : 9 + i, :]], axis=0
                )
                sums[0] = sums[0] + value
                for n in range(1, TERMS):
                    sums[n] = sums[n] + value * term_ref[n * 8 + i : n * 8 + i + 1, :]
            return tuple(sums)

        zero = jnp.zeros((2 * depth_grid, LANES), jnp.float32)
        sums = lax.fori_loop(0, -(-top // 8), modal, (zero,) * TERMS)
        for n in range(TERMS):
            for z in range(depth_grid):
                for c in range(2):
                    at = z * 2 * TERMS + c * TERMS + place_of(n)
                    row = c * depth_grid + z
                    sum_ref[at : at + 1, cols] = sums[n][row : row + 1, :]

    def times_i(value):
        blocks = []
        for z in range(depth_grid):
            base = z * 2 * TERMS
            blocks.append(-value[base + TERMS : base + 2 * TERMS])
            blocks.append(value[base : base + TERMS])
        return jnp.concatenate(blocks, axis=0)

    moments = sum_ref[...]
    moments = jnp.concatenate([moments, -times_i(moments)], axis=0).astype(jnp.bfloat16)
    group = depth_grid * 2 * TERMS

    for r in range(4):
        row = lax.broadcasted_iota(jnp.int32, (quarter, LANES), 0)
        column = lax.broadcasted_iota(jnp.int32, (quarter, LANES), 1)
        number = F0 + 4 * row + r
        whole = (number * column) % samples
        cosine, sine = sincos_turns(whole.astype(jnp.float32) * (1.0 / samples))
        turn = (number * LANES) % samples
        step_c, step_s = sincos_turns(turn.astype(jnp.float32) * (1.0 / samples))
        for block in range(span // LANES):
            cols = slice(block * LANES, (block + 1) * LANES)
            tab_ref[:quarter, cols] = cosine.astype(jnp.bfloat16)
            tab_ref[quarter:, cols] = (-sine).astype(jnp.bfloat16)
            cosine, sine = cosine * step_c - sine * step_s, cosine * step_s + sine * step_c
        bin_row = lax.broadcasted_iota(jnp.int32, (bins, quarter), 0)
        bin_column = lax.broadcasted_iota(jnp.int32, (bins, quarter), 1)
        chosen = (bin_row == 4 * bin_column + r).astype(jnp.float32).astype(jnp.bfloat16)
        picked = jnp.dot(moments, chosen, preferred_element_type=jnp.float32)
        left = jnp.concatenate([picked[:group], picked[group:]], axis=1)
        part_ref[r] = jnp.dot(
            left.astype(jnp.bfloat16), tab_ref[...], preferred_element_type=jnp.float32
        )

    for block in range(span // LANES):
        cols = slice(block * LANES, (block + 1) * LANES)
        p0, p1, p2, p3 = (part_ref[r, :, cols] for r in range(4))
        even, odd = p0 + p2, p1 + p3
        gap, turned = p0 - p2, times_i(p1 - p3)
        for q, value in enumerate((even + odd, gap + turned, even - odd, gap - turned)):
            at = q * span + block * LANES
            psi_ref[:, at : at + LANES] = value.astype(jnp.bfloat16)

    channel = lax.broadcasted_iota(jnp.int32, (1, channels), 1).astype(jnp.float32)
    position = first_x + channel * (2.0 / receivers)
    spread = lax.rsqrt(position)
    nodes = consts_ref[:, 0:1]
    for s in range(sources):
        offset = position - (ranges_ref[s] + centre)
        cosine, sine = sincos_turns(nodes * offset * (1.0 / TWO_PI))
        even = jnp.zeros((half, channels), jnp.float32)
        odd = jnp.zeros((half, channels), jnp.float32)
        for j in range(half):
            even = even + consts_ref[:, 1 + j : 2 + j] * cosine[j : j + 1, :]
            odd = odd + consts_ref[:, 1 + half + j : 2 + half + j] * sine[j : j + 1, :]
        mid_c, mid_s = sincos_turns(offset * (K_MID / TWO_PI))
        mid_c, mid_s = mid_c * spread, mid_s * spread
        rows = jnp.concatenate([mid_c * even, -mid_s * odd, -mid_s * even, -mid_c * odd], axis=0)
        coef_ref[s] = rows.T.astype(jnp.bfloat16)

    chunk = 512

    def source(s, matched):
        z = depths_ref[s]
        terms = pl.ds(pl.multiple_of(z * (2 * TERMS), 2 * TERMS), 2 * TERMS)
        coef = coef_ref[s]
        total = jnp.zeros((channels, LANES), jnp.float32)
        for start in range(0, samples, chunk):
            series = jnp.dot(
                coef, psi_ref[terms, start : start + chunk], preferred_element_type=jnp.float32
            )
            product = jnp.tanh(series) * recorded_ref[:, start : start + chunk].astype(jnp.float32)
            for tile in range(chunk // LANES):
                total = total + product[:, tile * LANES : (tile + 1) * LANES]
        value = jnp.sum(total, axis=1, keepdims=True)
        lane = lax.broadcasted_iota(jnp.int32, (channels, LANES), 1)
        return jnp.where(lane % sources == s, value, matched)

    out_ref[...] = lax.fori_loop(
        0, sources, source, jnp.zeros((channels, LANES), jnp.float32)
    )


def exchange_kernel(sizes, block_ref, out_ref, held_ref, send_sem, recv_sem):
    freq_size, sub_size = sizes
    count = freq_size * sub_size
    me = lax.axis_index("freq") * sub_size + lax.axis_index("sub")
    barrier = pltpu.get_barrier_semaphore()

    def place(number):
        return {"freq": number // sub_size, "sub": number % sub_size}

    def greet(i, carry):
        pl.semaphore_signal(
            barrier,
            inc=1,
            device_id=place((me + i) % count),
            device_id_type=pl.DeviceIdType.MESH,
        )
        return carry

    lax.fori_loop(1, count, greet, 0)
    pl.semaphore_wait(barrier, count - 1)

    def copy_to(target, source):
        return pltpu.make_async_remote_copy(
            src_ref=block_ref.at[target],
            dst_ref=held_ref.at[source],
            send_sem=send_sem.at[target],
            recv_sem=recv_sem.at[source],
            device_id=place(target),
            device_id_type=pl.DeviceIdType.MESH,
        )

    def send(i, carry):
        copy_to((me + i) % count, me).start()
        return carry

    lax.fori_loop(1, count, send, 0)

    def receive(i, total):
        source = (me + count - i) % count
        copy_to(source, source).wait_recv()
        return total + held_ref[source]

    out_ref[...] = lax.fori_loop(1, count, receive, block_ref[me])

    def drain(i, carry):
        copy_to((me + i) % count, me).wait_send()
        return carry

    lax.fori_loop(1, count, drain, 0)

FAST_TERMS = 12
FAST_HALF = 8


def fast_constants():
    nodes = np.cos(np.pi * (np.arange(FAST_TERMS) + 0.5) / FAST_TERMS)[: FAST_TERMS // 2]
    order = np.arange(FAST_TERMS)
    table = np.cos(order[:, None] * np.arccos(nodes)[None, :])
    table *= (np.where(order == 0, 1.0, 2.0) * 2.0 / FAST_TERMS)[:, None]
    half = FAST_TERMS // 2
    out = np.zeros((FAST_HALF, LANES), np.float32)
    out[:half, 0] = K_HALF * nodes
    out[half, 0] = K_MID
    out[:half, 1 : 1 + half] = table[0::2]
    out[:half, 1 + half : 1 + 2 * half] = table[1::2]
    return out


def fast_place(n):
    return n // 2 if n % 2 == 0 else FAST_HALF + n // 2


def score_kernel(
    shape,
    depths_hbm,
    ranges_hbm,
    consts_hbm,
    sections_hbm,
    counts_hbm,
    wave_hbm,
    receiver_hbm,
    source_hbm,
    recorded_hbm,
    out_ref,
    depths_ref,
    ranges_ref,
    consts_ref,
    sections_ref,
    counts_ref,
    wave_ref,
    receiver_ref,
    source_ref,
    recorded_ref,
    left_ref,
    xi_ref,
    apart_ref,
    moment_ref,
    weights_ref,
    tab_ref,
    psi_ref,
    coef_ref,
    wave_t_ref,
    kept_ref,
    block_ref,
    held_ref,
    load_sem,
    send_sem,
    recv_sem,
):
    bins, modes, depth_grid, sources, channels, samples, sizes = shape
    freq_size, sub_size = sizes
    count = freq_size * sub_size
    receivers = channels * count
    quarter = bins // 4
    span = samples // 4
    half = FAST_TERMS // 2
    group = depth_grid * 4 * FAST_HALF
    me = lax.axis_index("freq") * sub_size + lax.axis_index("sub")
    barrier = pltpu.get_barrier_semaphore()

    loads = [
        pltpu.make_async_copy(source, target, load_sem.at[i])
        for i, (source, target) in enumerate(
            (
                (depths_hbm, depths_ref),
                (ranges_hbm, ranges_ref),
                (consts_hbm, consts_ref),
                (sections_hbm, sections_ref),
                (counts_hbm, counts_ref),
                (wave_hbm, wave_ref),
                (receiver_hbm, receiver_ref),
                (source_hbm, source_ref),
                (recorded_hbm, recorded_ref),
            )
        )
    ]
    for load in loads:
        load.start()

    my_freq = lax.axis_index("freq")
    my_sub = lax.axis_index("sub")
    partners = [(i, j) for i in range(freq_size) for j in range(sub_size) if i or j]

    def ahead(i, j):
        return lax.rem(my_freq + i, freq_size), lax.rem(my_sub + j, sub_size)

    for i, j in partners:
        freq, sub = ahead(i, j)
        pl.semaphore_signal(
            barrier,
            inc=1,
            device_id={"freq": freq, "sub": sub},
            device_id_type=pl.DeviceIdType.MESH,
        )

    reach = 2.0 * (channels - 1) / receivers
    first_x = 1.0 + (me * channels).astype(jnp.float32) * (2.0 / receivers)
    centre = first_x + 0.5 * (reach - R_TOP)

    lane = lax.broadcasted_iota(jnp.int32, (8, LANES), 1)
    row = lax.broadcasted_iota(jnp.int32, (8, LANES), 0)
    for r in range(4):
        number = F0 + 4 * lane + r
        whole = (number * row) % samples
        cosine, sine = sincos_turns(whole.astype(jnp.float32) * (1.0 / samples))
        turn = (number * 8) % samples
        step_c, step_s = sincos_turns(turn.astype(jnp.float32) * (1.0 / samples))
        for pair in range(span // 16):
            turned_c = cosine * step_c - sine * step_s
            turned_s = cosine * step_s + sine * step_c
            rows = slice(pair * 16, pair * 16 + 16)
            tab_ref[r, rows, :quarter] = jnp.concatenate([cosine, turned_c], axis=0).astype(jnp.bfloat16)
            tab_ref[r, rows, quarter:] = jnp.concatenate([sine, turned_s], axis=0).astype(jnp.bfloat16)
            cosine = turned_c * step_c - turned_s * step_s
            sine = turned_c * step_s + turned_s * step_c

    for load in loads[:5]:
        load.wait()

    channel = lax.broadcasted_iota(jnp.int32, (1, channels), 1).astype(jnp.float32)
    position = first_x + channel * (2.0 / receivers)
    spread = lax.rsqrt(position)
    nodes = consts_ref[:, 0:1]
    for s in range(sources):
        offset = position - (ranges_ref[s] + centre)
        cosine, sine = sincos_turns(nodes * offset * (1.0 / TWO_PI))
        even = jnp.zeros((FAST_HALF, channels), jnp.float32)
        odd = jnp.zeros((FAST_HALF, channels), jnp.float32)
        for j in range(half):
            even = even + consts_ref[:, 1 + j : 2 + j] * cosine[j : j + 1, :]
            odd = odd + consts_ref[:, 1 + half + j : 2 + half + j] * sine[j : j + 1, :]
        mid_c, mid_s = cosine[half : half + 1, :] * spread, sine[half : half + 1, :] * spread
        parts = jnp.concatenate([mid_c * even, -mid_s * odd, -mid_s * even, -mid_c * odd], axis=0)
        for z in range(depth_grid):
            here = jnp.where(depths_ref[s] == z, 1.0, 0.0)
            rows = slice(z * 4 * FAST_HALF, (z + 1) * 4 * FAST_HALF)
            coef_ref[rows, s * channels : (s + 1) * channels] = (parts * here).astype(jnp.bfloat16)

    def top_of(last):
        return min(modes, MMIN + (modes - MMIN) * last // max(bins - 1, 1) + SPREAD)

    for load in loads[5:8]:
        load.wait()
    padded = -(-modes // 16) * 16

    def filled(value, rows):
        lack = rows - value.shape[0]
        if lack == 0:
            return value
        return jnp.concatenate([value, jnp.zeros((lack, value.shape[1]), value.dtype)], axis=0)

    for first in range(0, bins, LANES):
        cols = slice(first, first + LANES)
        deep = -(-top_of(first + LANES - 1) // LANES) * LANES
        rows = min(-(-top_of(first + LANES - 1) // 16) * 16, modes)
        whole = -(-rows // 16) * 16
        wave = wave_ref[:rows, cols]
        cosine, sine = sincos_turns(wave * (centre * (1.0 / TWO_PI)))
        index = lax.broadcasted_iota(jnp.int32, (rows, LANES), 0)
        factor = receiver_ref[:rows, cols].astype(jnp.float32) * (8.0 / math.sqrt(bins * modes))
        factor = jnp.where(index < counts_ref[:, cols], factor * lax.rsqrt(wave), 0.0)
        xi = (wave - K_MID) * (1.0 / K_HALF)
        xi_ref[cols, :deep] = filled(filled(xi, whole), deep).T
        weights = (factor * cosine, factor * sine)
        source = jnp.transpose(source_ref[:rows, :, cols].astype(jnp.float32), (1, 0, 2))
        for z in range(depth_grid):
            for c in range(2):
                value = filled(source[z] * weights[c], whole).astype(jnp.bfloat16)
                left_ref[z * 2 + c, cols, :deep] = filled(value, deep).T

    loads[8].wait()
    for block in range(samples // LANES):
        rows = slice(block * LANES, (block + 1) * LANES)
        wave_t_ref[rows, :] = recorded_ref[:, rows].T

    across = (((1,), (1,)), ((), ()))
    terms = 2 * FAST_HALF
    kinds = 2 * depth_grid
    same_bin = (
        lax.broadcasted_iota(jnp.int32, (16, terms * 16), 0)
        == lax.broadcasted_iota(jnp.int32, (16, terms * 16), 1) % 16
    )
    for g in range(bins // 16):
        rows = slice(g * 16, g * 16 + 16)
        deep = -(-top_of(g * 16 + 15) // LANES) * LANES
        xi = xi_ref[rows, :deep]
        before, now = jnp.ones_like(xi), xi
        right = [before.astype(jnp.bfloat16)]
        for n in range(1, FAST_TERMS):
            right.append(now.astype(jnp.bfloat16))
            before, now = now, 2.0 * xi * now - before
        right = right + [jnp.zeros_like(right[0])] * (terms - FAST_TERMS)
        left = jnp.concatenate([left_ref[k, rows, :deep] for k in range(kinds)], axis=0)
        pairs = lax.dot_general(
            left, jnp.concatenate(right, axis=0), across, preferred_element_type=jnp.float32
        )
        for k in range(kinds):
            value = jnp.where(same_bin, pairs[k * 16 : k * 16 + 16], 0.0)
            apart_ref[rows, k * terms * 16 : (k + 1) * terms * 16] = value.astype(jnp.bfloat16)

    term = lax.broadcasted_iota(jnp.int32, (terms * 16, group), 0) // 16
    column = lax.broadcasted_iota(jnp.int32, (terms * 16, group), 1)
    column = column - (term // 2 + FAST_HALF * (term % 2))
    column = jnp.where(term < FAST_TERMS, column, -1)
    gathers = []
    for k in range(kinds):
        z, c = k // 2, k % 2
        plain = jnp.where(column == k * terms, 1.0, 0.0)
        turned = jnp.where(column == (z * 2 + 1 - c) * terms, 1.0 - 2.0 * c, 0.0)
        gathers.append(jnp.concatenate([plain, turned], axis=1).astype(jnp.bfloat16))
    gather = jnp.concatenate(gathers, axis=0)
    middle = bins // 2
    moments = jnp.concatenate(
        [
            jnp.dot(apart_ref[:middle, :], gather, preferred_element_type=jnp.float32),
            jnp.dot(apart_ref[middle:, :], gather, preferred_element_type=jnp.float32),
        ],
        axis=0,
    )
    moment_ref[:bins, :] = moments[:, :group]
    moment_ref[bins:, :] = moments[:, group:]
    weights = []
    for r in range(4):
        plain = moment_ref[pl.ds(r, quarter, stride=4), :].astype(jnp.bfloat16)
        turned = moment_ref[pl.ds(bins + r, quarter, stride=4), :].astype(jnp.bfloat16)
        weight = jnp.concatenate([plain, turned], axis=0)
        if r % 2:
            weight = jnp.concatenate([weight, jnp.concatenate([turned, -plain], axis=0)], axis=1)
        weights.append(weight)
    piece = 512
    for r in range(4):
        sides = weights[r].shape[1]
        weights_ref[r, :, :sides] = weights[r]

    def transform(i, carry):
        start = pl.multiple_of(i * piece, piece)
        rows = pl.ds(start, piece)
        p0, p1, p2, p3 = (
            jnp.dot(
                tab_ref[r, rows, :],
                weights_ref[r, :, : group * (1 + r % 2)],
                preferred_element_type=jnp.float32,
            )
            for r in range(4)
        )
        odd, turned = p1[:, :group] + p3[:, :group], p1[:, group:] - p3[:, group:]
        even, gap = p0 + p2, p0 - p2
        for q, value in enumerate((even + odd, gap + turned, even - odd, gap - turned)):
            psi_ref[pl.ds(q * span + start, piece), :] = value.astype(jnp.bfloat16)
        return carry

    lax.fori_loop(0, span // piece, transform, 0)

    width = 4 * channels
    section_row = sections_ref[...]
    lane_in_row = section_row % 8

    def quad(i, carry):
        cols = pl.ds(pl.multiple_of(i * width, width), width)
        series = jnp.dot(psi_ref[...], coef_ref[:, cols], preferred_element_type=jnp.float32)
        waveform = wave_t_ref[...].astype(jnp.float32)
        slot = lax.broadcasted_iota(jnp.int32, (8, channels), 0)
        for s in range(4):
            product = jnp.tanh(series[:, s * channels : (s + 1) * channels]) * waveform
            total = jnp.sum(product.reshape(samples // 8, 8, channels), axis=0)
            for shift in (4, 2, 1):
                total = total + pltpu.roll(total, shift, 0)
            rows = pl.ds(pl.multiple_of((sources - 1 - s - 4 * i) * 8, 8), 8)
            kept_ref[rows, :] = jnp.where(slot == lane_in_row, total, 0.0)
        return carry

    lax.fori_loop(0, sources // 4, quad, 0)

    own_rows = receivers // 4 // count // 8
    slots = lax.broadcasted_iota(jnp.int32, (count * 8, channels), 0)
    wanted = section_row // 8
    wanted = wanted // own_rows * 8 + wanted % own_rows
    member = (slots == wanted).astype(jnp.float32).astype(jnp.bfloat16)
    kept = kept_ref[...] * (1.0 / math.sqrt(samples * 4))
    high = kept.astype(jnp.bfloat16)
    low = (kept - high.astype(jnp.float32)).astype(jnp.bfloat16)
    blocks = lax.dot_general(
        jnp.concatenate([member, member], axis=1),
        jnp.concatenate([high, low], axis=1),
        across,
        preferred_element_type=jnp.float32,
    )
    block_ref[...] = blocks.reshape(count, 8, LANES)

    pl.semaphore_wait(barrier, count - 1)

    def copy_to(freq, sub, slot, source):
        return pltpu.make_async_remote_copy(
            src_ref=block_ref.at[freq * sub_size + sub],
            dst_ref=held_ref.at[source],
            send_sem=send_sem.at[slot],
            recv_sem=recv_sem.at[source],
            device_id={"freq": freq, "sub": sub},
            device_id_type=pl.DeviceIdType.MESH,
        )

    sends = []
    for slot, (i, j) in enumerate(partners):
        freq, sub = ahead(i, j)
        sends.append(copy_to(freq, sub, slot, me))
        sends[-1].start()
    total = block_ref[me]
    for slot, (i, j) in enumerate(partners):
        freq, sub = ahead(freq_size - i, sub_size - j)
        source = freq * sub_size + sub
        copy_to(freq, sub, slot, source).wait_recv()
        total = total + held_ref[source]

    halves = [jnp.zeros((8, LANES), jnp.float32)] * (sources // 8)
    for r in range(own_rows):
        spread_row = jnp.broadcast_to(total[r : r + 1, :], (8, LANES))
        moved = pltpu.roll(spread_row, 0, 1, stride=8, stride_axis=0)
        for h in range(sources // 8):
            placed = pltpu.roll(moved, (8 * r + 8 + 64 * h) % LANES, 1)
            halves[h] = jnp.where(lane // 8 == r, placed, halves[h])
    out_ref[...] = jnp.concatenate(halves, axis=0)[:, : own_rows * 8]

    for send in sends:
        send.wait_send()


def fast_fits(mesh_sizes, wavenumbers, source_shapes, source_depths, recorded):
    count = mesh_sizes[0] * mesh_sizes[1]
    bins = wavenumbers.shape[0]
    channels, samples = recorded.shape
    own = channels // 4
    return (
        channels == LANES
        and source_depths.shape[0] * 8 == LANES
        and source_shapes.shape[1] * 4 * FAST_HALF == LANES
        and bins == 4 * LANES
        and samples % (4 * LANES) == 0
        and own % 8 == 0
        and own // 8 <= 8
        and count * 8 % LANES == 0
    )


def per_device(
    mesh_sizes,
    wavenumbers,
    receiver_shapes,
    source_shapes,
    mode_counts,
    source_depths,
    source_ranges,
    sections,
    recorded,
):
    args = (
        wavenumbers,
        receiver_shapes,
        source_shapes,
        mode_counts,
        source_depths,
        source_ranges,
        sections,
        recorded,
    )
    if not fast_fits(mesh_sizes, wavenumbers, source_shapes, source_depths, recorded):
        return per_device_general(mesh_sizes, *args)
    freq_size, sub_size = mesh_sizes
    count = freq_size * sub_size
    bins, modes = wavenumbers.shape
    depth_grid = source_shapes.shape[1]
    sources = source_depths.shape[0]
    channels, samples = recorded.shape
    receivers = channels * count
    reach = 2.0 * (channels - 1) / receivers
    top_phase = K_HALF * 0.5 * (reach + R_TOP)
    assert 2.0 * (0.5 * top_phase) ** FAST_TERMS / math.factorial(FAST_TERMS) < 1e-6

    shape = (bins, modes, depth_grid, sources, channels, samples, mesh_sizes)
    group = depth_grid * 4 * FAST_HALF
    deep = -(-modes // LANES) * LANES
    own = channels // 4
    return pl.pallas_call(
        functools.partial(score_kernel, shape),
        out_shape=jax.ShapeDtypeStruct((sources, own), jnp.float32),
        in_specs=[pl.BlockSpec(memory_space=pl.ANY)] * 9,
        out_specs=pl.BlockSpec(memory_space=pltpu.VMEM),
        scratch_shapes=[
            pltpu.SMEM((sources,), jnp.int32),
            pltpu.SMEM((sources,), jnp.float32),
            pltpu.VMEM((FAST_HALF, LANES), jnp.float32),
            pltpu.VMEM((1, channels), jnp.int32),
            pltpu.VMEM((1, bins), jnp.int32),
            pltpu.VMEM((modes, bins), jnp.float32),
            pltpu.VMEM((modes, bins), jnp.bfloat16),
            pltpu.VMEM((modes, depth_grid, bins), jnp.bfloat16),
            pltpu.VMEM((channels, samples), jnp.bfloat16),
            pltpu.VMEM((2 * depth_grid, bins, deep), jnp.bfloat16),
            pltpu.VMEM((bins, deep), jnp.float32),
            pltpu.VMEM((bins, group * 2 * FAST_HALF), jnp.bfloat16),
            pltpu.VMEM((2 * bins, group), jnp.float32),
            pltpu.VMEM((4, bins // 2, 2 * group), jnp.bfloat16),
            pltpu.VMEM((4, samples // 4, bins // 2), jnp.bfloat16),
            pltpu.VMEM((samples, group), jnp.bfloat16),
            pltpu.VMEM((group, sources * channels), jnp.bfloat16),
            pltpu.VMEM((samples, channels), jnp.bfloat16),
            pltpu.VMEM((sources * 8, channels), jnp.float32),
            pltpu.VMEM((count, 8, LANES), jnp.float32),
            pltpu.VMEM((count, 8, LANES), jnp.float32),
            pltpu.SemaphoreType.DMA((9,)),
            pltpu.SemaphoreType.DMA((count - 1,)),
            pltpu.SemaphoreType.DMA((count,)),
        ],
        compiler_params=pltpu.CompilerParams(
            vmem_limit_bytes=60 * 1024 * 1024, collective_id=1, has_side_effects=True
        ),
        name="score",
    )(
        source_depths,
        source_ranges,
        jnp.asarray(fast_constants()),
        sections.reshape(1, channels),
        mode_counts.reshape(1, bins),
        wavenumbers.T,
        receiver_shapes.T,
        source_shapes.transpose(2, 1, 0),
        recorded,
    )


def per_device_general(
    mesh_sizes,
    wavenumbers,
    receiver_shapes,
    source_shapes,
    mode_counts,
    source_depths,
    source_ranges,
    sections,
    recorded,
):
    freq_size, sub_size = mesh_sizes
    count = freq_size * sub_size
    me = lax.axis_index("freq") * sub_size + lax.axis_index("sub")
    bins, modes = wavenumbers.shape
    depth_grid = source_shapes.shape[1]
    sources = source_depths.shape[0]
    channels, samples = recorded.shape
    receivers = channels * count

    first_x = 1.0 + 2.0 * (me * channels).astype(jnp.float32) / receivers
    reach = 2.0 * (channels - 1) / receivers
    centre = first_x + 0.5 * (reach - R_TOP)
    top_phase = K_HALF * 0.5 * (reach + R_TOP)
    assert 2.0 * (0.5 * top_phase) ** TERMS / math.factorial(TERMS) < 1e-9
    assert depth_grid * 2 * TERMS <= LANES

    extra = -modes % 8
    wave = wavenumbers.T
    live = jnp.arange(modes, dtype=jnp.int32)[:, None] < mode_counts[None, :]
    factor = receiver_shapes.T.astype(jnp.float32) * (8.0 / math.sqrt(bins))
    factor = jnp.where(live, factor / jnp.sqrt(wave * modes), 0.0)
    factor = jnp.pad(factor, ((0, extra), (0, 0)))
    wave = jnp.pad(wave, ((0, extra), (0, 0)), constant_values=K_MID)
    shape = (bins, modes, depth_grid, sources, channels, samples, receivers)
    matched = pl.pallas_call(
        functools.partial(replica_kernel, shape),
        out_shape=jax.ShapeDtypeStruct((channels, LANES), jnp.float32),
        in_specs=[pl.BlockSpec(memory_space=pltpu.SMEM)] * 3
        + [pl.BlockSpec(memory_space=pltpu.VMEM)] * 5,
        out_specs=pl.BlockSpec(memory_space=pltpu.VMEM),
        scratch_shapes=[
            pltpu.VMEM((depth_grid * 2 * TERMS, bins), jnp.float32),
            pltpu.VMEM((16, LANES), jnp.float32),
            pltpu.VMEM((TERMS * 8, LANES), jnp.float32),
            pltpu.VMEM((bins // 2, samples // 4), jnp.bfloat16),
            pltpu.VMEM((4, depth_grid * 2 * TERMS, samples // 4), jnp.float32),
            pltpu.VMEM((depth_grid * 2 * TERMS, samples), jnp.bfloat16),
            pltpu.VMEM((sources, channels, 2 * TERMS), jnp.bfloat16),
        ],
        compiler_params=pltpu.CompilerParams(vmem_limit_bytes=48 * 1024 * 1024),
        name="replica",
    )(
        source_depths,
        jnp.stack([first_x, centre]),
        source_ranges,
        jnp.asarray(term_constants()),
        wave,
        factor,
        source_shapes.transpose(2, 1, 0),
        recorded,
    )

    section_count = receivers // 4
    own = section_count // count
    per_row = min(LANES // sources, own)
    own_rows = own // per_row
    assert LANES % sources == 0 and own % per_row == 0
    padded = -(-own_rows // 8) * 8
    slot = jnp.arange(count * padded, dtype=jnp.int32)
    wanted = jnp.where(
        slot % padded < own_rows, slot // padded * own_rows + slot % padded, -1
    )
    member = (wanted[:, None] == (sections // per_row)[None, :]).astype(jnp.float32)
    lane_part = jnp.arange(LANES, dtype=jnp.int32) // sources
    kept = jnp.where((sections % per_row)[:, None] == lane_part[None, :], matched, 0.0)
    blocks = jnp.dot(member, kept, precision=lax.Precision.HIGHEST) * (
        1.0 / math.sqrt(samples * (receivers // section_count))
    )
    blocks = blocks.reshape(count, padded, LANES)
    total = pl.pallas_call(
        functools.partial(exchange_kernel, (freq_size, sub_size)),
        out_shape=jax.ShapeDtypeStruct((padded, LANES), jnp.float32),
        in_specs=[pl.BlockSpec(memory_space=pltpu.VMEM)],
        out_specs=pl.BlockSpec(memory_space=pltpu.VMEM),
        scratch_shapes=[
            pltpu.VMEM((count, padded, LANES), jnp.float32),
            pltpu.SemaphoreType.DMA((count,)),
            pltpu.SemaphoreType.DMA((count,)),
        ],
        compiler_params=pltpu.CompilerParams(collective_id=0, has_side_effects=True),
        name="exchange",
    )(blocks)
    total = total[:own_rows, : per_row * sources].reshape(own_rows, per_row, sources)
    return total.transpose(2, 0, 1).reshape(sources, own)


def solution(mesh):
    sizes = (mesh.shape["freq"], mesh.shape["sub"])
    in_specs = (
        P(),
        P(),
        P(),
        P(),
        P("groups"),
        P("groups"),
        P(("freq", "sub")),
        P(("freq", "sub"), None),
    )
    out_specs = P("groups", ("freq", "sub"))
    return jax.shard_map(
        functools.partial(per_device, sizes),
        mesh=mesh,
        in_specs=in_specs,
        out_specs=out_specs,
        check_vma=False,
    )
```

```python
import functools
import math

import jax
import jax.numpy as jnp
import numpy as np
from jax import lax
from jax.experimental import pallas as pl
from jax.experimental.pallas import tpu as pltpu
from jax.sharding import PartitionSpec as P

MMIN = 64
F0 = 256
SPREAD = 16
K_LOW, K_TOP = 1.0, 20.0
R_TOP = 0.5
K_MID, K_HALF = 0.5 * (K_LOW + K_TOP), 0.5 * (K_TOP - K_LOW)
LANES = 128
TERMS = 16
TWO_PI = 2.0 * math.pi


def fitted(function, count):
    angle = np.pi * (np.arange(200) + 0.5) / 200
    square = 0.125 * (1.0 + np.cos(angle))
    series = np.polynomial.chebyshev.Chebyshev.fit(
        square, function(np.sqrt(square)), count - 1, domain=[0.0, 0.25]
    )
    return [float(c) for c in series.convert(kind=np.polynomial.Polynomial).coef]


SINE = fitted(lambda x: np.sin(np.pi * x) / x, 5)
COSINE = fitted(lambda x: np.cos(np.pi * x), 5)


def horner(coefficients, x):
    value = coefficients[-1] * x + coefficients[-2]
    for c in coefficients[-3::-1]:
        value = value * x + c
    return value


def sincos_turns(turns):
    part = turns - jnp.floor(turns + 0.5)
    square = part * part
    s = horner(SINE, square) * part
    c = horner(COSINE, square)
    twice = s + s
    return 1.0 - twice * s, twice * c


def term_constants():
    nodes = np.cos(np.pi * (np.arange(TERMS) + 0.5) / TERMS)[: TERMS // 2]
    order = np.arange(TERMS)
    table = np.cos(order[:, None] * np.arccos(nodes)[None, :])
    table *= (np.where(order == 0, 1.0, 2.0) * 2.0 / TERMS)[:, None]
    half = TERMS // 2
    out = np.zeros((half, LANES), np.float32)
    out[:, 0] = K_HALF * nodes
    out[:, 1 : 1 + half] = table[0::2]
    out[:, 1 + half : 1 + 2 * half] = table[1::2]
    return out


def place_of(n):
    return n // 2 if n % 2 == 0 else TERMS // 2 + n // 2


def replica_kernel(
    shape,
    depths_ref,
    place_ref,
    ranges_ref,
    consts_ref,
    wave_ref,
    factor_ref,
    source_ref,
    recorded_ref,
    out_ref,
    sum_ref,
    weight_ref,
    term_ref,
    tab_ref,
    part_ref,
    psi_ref,
    coef_ref,
):
    bins, modes, depth_grid, sources, channels, samples, receivers = shape
    quarter = bins // 4
    span = samples // 4
    half = TERMS // 2
    first_x = place_ref[0]
    centre = place_ref[1]

    for first in range(0, bins, LANES):
        last = first + LANES - 1
        top = min(modes, MMIN + (modes - MMIN) * last // max(bins - 1, 1) + SPREAD)
        cols = slice(first, first + LANES)

        def modal(step, sums, cols=cols):
            start = pl.multiple_of(step * 8, 8)
            rows = pl.ds(start, 8)
            wave = wave_ref[rows, cols]
            cosine, sine = sincos_turns(wave * (centre * (1.0 / TWO_PI)))
            factor = factor_ref[rows, cols]
            weight_ref[0:8, :] = factor * cosine
            weight_ref[8:16, :] = factor * sine
            xi = (wave - K_MID) * (1.0 / K_HALF)
            before, now = jnp.ones_like(xi), xi
            for n in range(1, TERMS):
                term_ref[n * 8 : n * 8 + 8, :] = now
                before, now = now, 2.0 * xi * now - before
            sums = list(sums)
            for i in range(8):
                source = source_ref[jnp.minimum(start + i, modes - 1), :, cols].astype(jnp.float32)
                value = jnp.concatenate(
                    [source * weight_ref[i : i + 1, :], source * weight_ref[8 + i : 9 + i, :]], axis=0
                )
                sums[0] = sums[0] + value
                for n in range(1, TERMS):
                    sums[n] = sums[n] + value * term_ref[n * 8 + i : n * 8 + i + 1, :]
            return tuple(sums)

        zero = jnp.zeros((2 * depth_grid, LANES), jnp.float32)
        sums = lax.fori_loop(0, -(-top // 8), modal, (zero,) * TERMS)
        for n in range(TERMS):
            for z in range(depth_grid):
                for c in range(2):
                    at = z * 2 * TERMS + c * TERMS + place_of(n)
                    row = c * depth_grid + z
                    sum_ref[at : at + 1, cols] = sums[n][row : row + 1, :]

    def times_i(value):
        blocks = []
        for z in range(depth_grid):
            base = z * 2 * TERMS
            blocks.append(-value[base + TERMS : base + 2 * TERMS])
            blocks.append(value[base : base + TERMS])
        return jnp.concatenate(blocks, axis=0)

    moments = sum_ref[...]
    moments = jnp.concatenate([moments, -times_i(moments)], axis=0).astype(jnp.bfloat16)
    group = depth_grid * 2 * TERMS

    for r in range(4):
        row = lax.broadcasted_iota(jnp.int32, (quarter, LANES), 0)
        column = lax.broadcasted_iota(jnp.int32, (quarter, LANES), 1)
        number = F0 + 4 * row + r
        whole = (number * column) % samples
        cosine, sine = sincos_turns(whole.astype(jnp.float32) * (1.0 / samples))
        turn = (number * LANES) % samples
        step_c, step_s = sincos_turns(turn.astype(jnp.float32) * (1.0 / samples))
        for block in range(span // LANES):
            cols = slice(block * LANES, (block + 1) * LANES)
            tab_ref[:quarter, cols] = cosine.astype(jnp.bfloat16)
            tab_ref[quarter:, cols] = (-sine).astype(jnp.bfloat16)
            cosine, sine = cosine * step_c - sine * step_s, cosine * step_s + sine * step_c
        bin_row = lax.broadcasted_iota(jnp.int32, (bins, quarter), 0)
        bin_column = lax.broadcasted_iota(jnp.int32, (bins, quarter), 1)
        chosen = (bin_row == 4 * bin_column + r).astype(jnp.float32).astype(jnp.bfloat16)
        picked = jnp.dot(moments, chosen, preferred_element_type=jnp.float32)
        left = jnp.concatenate([picked[:group], picked[group:]], axis=1)
        part_ref[r] = jnp.dot(
            left.astype(jnp.bfloat16), tab_ref[...], preferred_element_type=jnp.float32
        )

    for block in range(span // LANES):
        cols = slice(block * LANES, (block + 1) * LANES)
        p0, p1, p2, p3 = (part_ref[r, :, cols] for r in range(4))
        even, odd = p0 + p2, p1 + p3
        gap, turned = p0 - p2, times_i(p1 - p3)
        for q, value in enumerate((even + odd, gap + turned, even - odd, gap - turned)):
            at = q * span + block * LANES
            psi_ref[:, at : at + LANES] = value.astype(jnp.bfloat16)

    channel = lax.broadcasted_iota(jnp.int32, (1, channels), 1).astype(jnp.float32)
    position = first_x + channel * (2.0 / receivers)
    spread = lax.rsqrt(position)
    nodes = consts_ref[:, 0:1]
    for s in range(sources):
        offset = position - (ranges_ref[s] + centre)
        cosine, sine = sincos_turns(nodes * offset * (1.0 / TWO_PI))
        even = jnp.zeros((half, channels), jnp.float32)
        odd = jnp.zeros((half, channels), jnp.float32)
        for j in range(half):
            even = even + consts_ref[:, 1 + j : 2 + j] * cosine[j : j + 1, :]
            odd = odd + consts_ref[:, 1 + half + j : 2 + half + j] * sine[j : j + 1, :]
        mid_c, mid_s = sincos_turns(offset * (K_MID / TWO_PI))
        mid_c, mid_s = mid_c * spread, mid_s * spread
        rows = jnp.concatenate([mid_c * even, -mid_s * odd, -mid_s * even, -mid_c * odd], axis=0)
        coef_ref[s] = rows.T.astype(jnp.bfloat16)

    chunk = 512

    def source(s, matched):
        z = depths_ref[s]
        terms = pl.ds(pl.multiple_of(z * (2 * TERMS), 2 * TERMS), 2 * TERMS)
        coef = coef_ref[s]
        total = jnp.zeros((channels, LANES), jnp.float32)
        for start in range(0, samples, chunk):
            series = jnp.dot(
                coef, psi_ref[terms, start : start + chunk], preferred_element_type=jnp.float32
            )
            product = jnp.tanh(series) * recorded_ref[:, start : start + chunk].astype(jnp.float32)
            for tile in range(chunk // LANES):
                total = total + product[:, tile * LANES : (tile + 1) * LANES]
        value = jnp.sum(total, axis=1, keepdims=True)
        lane = lax.broadcasted_iota(jnp.int32, (channels, LANES), 1)
        return jnp.where(lane % sources == s, value, matched)

    out_ref[...] = lax.fori_loop(
        0, sources, source, jnp.zeros((channels, LANES), jnp.float32)
    )


def exchange_kernel(sizes, block_ref, out_ref, held_ref, send_sem, recv_sem):
    freq_size, sub_size = sizes
    count = freq_size * sub_size
    me = lax.axis_index("freq") * sub_size + lax.axis_index("sub")
    barrier = pltpu.get_barrier_semaphore()

    def place(number):
        return {"freq": number // sub_size, "sub": number % sub_size}

    def greet(i, carry):
        pl.semaphore_signal(
            barrier,
            inc=1,
            device_id=place((me + i) % count),
            device_id_type=pl.DeviceIdType.MESH,
        )
        return carry

    lax.fori_loop(1, count, greet, 0)
    pl.semaphore_wait(barrier, count - 1)

    def copy_to(target, source):
        return pltpu.make_async_remote_copy(
            src_ref=block_ref.at[target],
            dst_ref=held_ref.at[source],
            send_sem=send_sem.at[target],
            recv_sem=recv_sem.at[source],
            device_id=place(target),
            device_id_type=pl.DeviceIdType.MESH,
        )

    def send(i, carry):
        copy_to((me + i) % count, me).start()
        return carry

    lax.fori_loop(1, count, send, 0)

    def receive(i, total):
        source = (me + count - i) % count
        copy_to(source, source).wait_recv()
        return total + held_ref[source]

    out_ref[...] = lax.fori_loop(1, count, receive, block_ref[me])

    def drain(i, carry):
        copy_to((me + i) % count, me).wait_send()
        return carry

    lax.fori_loop(1, count, drain, 0)

FAST_TERMS = 12
FAST_HALF = 8


def fast_constants():
    nodes = np.cos(np.pi * (np.arange(FAST_TERMS) + 0.5) / FAST_TERMS)[: FAST_TERMS // 2]
    order = np.arange(FAST_TERMS)
    table = np.cos(order[:, None] * np.arccos(nodes)[None, :])
    table *= (np.where(order == 0, 1.0, 2.0) * 2.0 / FAST_TERMS)[:, None]
    half = FAST_TERMS // 2
    out = np.zeros((FAST_HALF, LANES), np.float32)
    out[:half, 0] = K_HALF * nodes
    out[half, 0] = K_MID
    out[:half, 1 : 1 + half] = table[0::2]
    out[:half, 1 + half : 1 + 2 * half] = table[1::2]
    return out


def fast_place(n):
    return n // 2 if n % 2 == 0 else FAST_HALF + n // 2


def score_kernel(
    shape,
    depths_hbm,
    ranges_hbm,
    consts_hbm,
    sections_hbm,
    counts_hbm,
    wave_hbm,
    receiver_hbm,
    source_hbm,
    recorded_hbm,
    out_ref,
    depths_ref,
    ranges_ref,
    consts_ref,
    sections_ref,
    counts_ref,
    wave_ref,
    receiver_ref,
    source_ref,
    recorded_ref,
    left_ref,
    xi_ref,
    apart_ref,
    moment_ref,
    weights_ref,
    tab_ref,
    psi_ref,
    coef_ref,
    wave_t_ref,
    kept_ref,
    block_ref,
    held_ref,
    load_sem,
    send_sem,
    recv_sem,
):
    bins, modes, depth_grid, sources, channels, samples, sizes = shape
    freq_size, sub_size = sizes
    count = freq_size * sub_size
    receivers = channels * count
    quarter = bins // 4
    span = samples // 4
    half = FAST_TERMS // 2
    group = depth_grid * 4 * FAST_HALF
    me = lax.axis_index("freq") * sub_size + lax.axis_index("sub")
    barrier = pltpu.get_barrier_semaphore()

    def top_of(last):
        return min(modes, MMIN + (modes - MMIN) * last // max(bins - 1, 1) + SPREAD)

    pairs = [
        (depths_hbm, depths_ref),
        (ranges_hbm, ranges_ref),
        (consts_hbm, consts_ref),
        (sections_hbm, sections_ref),
        (counts_hbm, counts_ref),
    ]
    for first in range(0, bins, LANES):
        cols = slice(first, first + LANES)
        rows = min(-(-top_of(first + LANES - 1) // 16) * 16, modes)
        pairs.append((wave_hbm.at[:rows, cols], wave_ref.at[:rows, cols]))
        pairs.append((receiver_hbm.at[:rows, cols], receiver_ref.at[:rows, cols]))
        pairs.append((source_hbm.at[:rows, :, cols], source_ref.at[:rows, :, cols]))
    pairs.append((recorded_hbm, recorded_ref))
    loads = [
        pltpu.make_async_copy(source, target, load_sem.at[i])
        for i, (source, target) in enumerate(pairs)
    ]
    for load in loads:
        load.start()

    my_freq = lax.axis_index("freq")
    my_sub = lax.axis_index("sub")
    partners = [(i, j) for i in range(freq_size) for j in range(sub_size) if i or j]

    def ahead(i, j):
        return lax.rem(my_freq + i, freq_size), lax.rem(my_sub + j, sub_size)

    for i, j in partners:
        freq, sub = ahead(i, j)
        pl.semaphore_signal(
            barrier,
            inc=1,
            device_id={"freq": freq, "sub": sub},
            device_id_type=pl.DeviceIdType.MESH,
        )

    reach = 2.0 * (channels - 1) / receivers
    first_x = 1.0 + (me * channels).astype(jnp.float32) * (2.0 / receivers)
    centre = first_x + 0.5 * (reach - R_TOP)

    lane = lax.broadcasted_iota(jnp.int32, (8, LANES), 1)
    row = lax.broadcasted_iota(jnp.int32, (8, LANES), 0)
    for r in range(4):
        number = F0 + 4 * lane + r
        whole = (number * row) % samples
        cosine, sine = sincos_turns(whole.astype(jnp.float32) * (1.0 / samples))
        turn = (number * 8) % samples
        step_c, step_s = sincos_turns(turn.astype(jnp.float32) * (1.0 / samples))
        for pair in range(span // 16):
            turned_c = cosine * step_c - sine * step_s
            turned_s = cosine * step_s + sine * step_c
            rows = slice(pair * 16, pair * 16 + 16)
            tab_ref[r, rows, :quarter] = jnp.concatenate([cosine, turned_c], axis=0).astype(jnp.bfloat16)
            tab_ref[r, rows, quarter:] = jnp.concatenate([sine, turned_s], axis=0).astype(jnp.bfloat16)
            cosine = turned_c * step_c - turned_s * step_s
            sine = turned_c * step_s + turned_s * step_c

    for load in loads[:5]:
        load.wait()

    channel = lax.broadcasted_iota(jnp.int32, (1, channels), 1).astype(jnp.float32)
    position = first_x + channel * (2.0 / receivers)
    spread = lax.rsqrt(position)
    nodes = consts_ref[:, 0:1]
    for s in range(sources):
        offset = position - (ranges_ref[s] + centre)
        cosine, sine = sincos_turns(nodes * offset * (1.0 / TWO_PI))
        even = jnp.zeros((FAST_HALF, channels), jnp.float32)
        odd = jnp.zeros((FAST_HALF, channels), jnp.float32)
        for j in range(half):
            even = even + consts_ref[:, 1 + j : 2 + j] * cosine[j : j + 1, :]
            odd = odd + consts_ref[:, 1 + half + j : 2 + half + j] * sine[j : j + 1, :]
        mid_c, mid_s = cosine[half : half + 1, :] * spread, sine[half : half + 1, :] * spread
        parts = jnp.concatenate([mid_c * even, -mid_s * odd, -mid_s * even, -mid_c * odd], axis=0)
        for z in range(depth_grid):
            here = jnp.where(depths_ref[s] == z, 1.0, 0.0)
            rows = slice(z * 4 * FAST_HALF, (z + 1) * 4 * FAST_HALF)
            coef_ref[rows, s * channels : (s + 1) * channels] = (parts * here).astype(jnp.bfloat16)

    def filled(value, rows):
        lack = rows - value.shape[0]
        if lack == 0:
            return value
        return jnp.concatenate([value, jnp.zeros((lack, value.shape[1]), value.dtype)], axis=0)

    for block, first in enumerate(range(0, bins, LANES)):
        for load in loads[5 + 3 * block : 8 + 3 * block]:
            load.wait()
        cols = slice(first, first + LANES)
        deep = -(-top_of(first + LANES - 1) // LANES) * LANES
        rows = min(-(-top_of(first + LANES - 1) // 16) * 16, modes)
        whole = -(-rows // 16) * 16
        wave = wave_ref[:rows, cols]
        cosine, sine = sincos_turns(wave * (centre * (1.0 / TWO_PI)))
        index = lax.broadcasted_iota(jnp.int32, (rows, LANES), 0)
        factor = receiver_ref[:rows, cols].astype(jnp.float32) * (8.0 / math.sqrt(bins * modes))
        factor = jnp.where(index < counts_ref[:, cols], factor * lax.rsqrt(wave), 0.0)
        xi = (wave - K_MID) * (1.0 / K_HALF)
        xi_ref[cols, :deep] = filled(filled(xi, whole), deep).T
        weights = (factor * cosine, factor * sine)
        source = jnp.transpose(source_ref[:rows, :, cols].astype(jnp.float32), (1, 0, 2))
        for z in range(depth_grid):
            for c in range(2):
                value = filled(source[z] * weights[c], whole).astype(jnp.bfloat16)
                left_ref[z * 2 + c, cols, :deep] = filled(value, deep).T

    loads[-1].wait()
    for block in range(samples // LANES):
        rows = slice(block * LANES, (block + 1) * LANES)
        wave_t_ref[rows, :] = recorded_ref[:, rows].T

    across = (((1,), (1,)), ((), ()))
    terms = 2 * FAST_HALF
    kinds = 2 * depth_grid
    same_bin = (
        lax.broadcasted_iota(jnp.int32, (16, terms * 16), 0)
        == lax.broadcasted_iota(jnp.int32, (16, terms * 16), 1) % 16
    )
    for g in range(bins // 16):
        rows = slice(g * 16, g * 16 + 16)
        deep = -(-top_of(g * 16 + 15) // LANES) * LANES
        xi = xi_ref[rows, :deep]
        before, now = jnp.ones_like(xi), xi
        right = [before.astype(jnp.bfloat16)]
        for n in range(1, FAST_TERMS):
            right.append(now.astype(jnp.bfloat16))
            before, now = now, 2.0 * xi * now - before
        right = right + [jnp.zeros_like(right[0])] * (terms - FAST_TERMS)
        left = jnp.concatenate([left_ref[k, rows, :deep] for k in range(kinds)], axis=0)
        pairs = lax.dot_general(
            left, jnp.concatenate(right, axis=0), across, preferred_element_type=jnp.float32
        )
        for k in range(kinds):
            value = jnp.where(same_bin, pairs[k * 16 : k * 16 + 16], 0.0)
            apart_ref[rows, k * terms * 16 : (k + 1) * terms * 16] = value.astype(jnp.bfloat16)

    term = lax.broadcasted_iota(jnp.int32, (terms * 16, group), 0) // 16
    column = lax.broadcasted_iota(jnp.int32, (terms * 16, group), 1)
    column = column - (term // 2 + FAST_HALF * (term % 2))
    column = jnp.where(term < FAST_TERMS, column, -1)
    gathers = []
    for k in range(kinds):
        z, c = k // 2, k % 2
        plain = jnp.where(column == k * terms, 1.0, 0.0)
        turned = jnp.where(column == (z * 2 + 1 - c) * terms, 1.0 - 2.0 * c, 0.0)
        gathers.append(jnp.concatenate([plain, turned], axis=1).astype(jnp.bfloat16))
    gather = jnp.concatenate(gathers, axis=0)
    middle = bins // 2
    moments = jnp.concatenate(
        [
            jnp.dot(apart_ref[:middle, :], gather, preferred_element_type=jnp.float32),
            jnp.dot(apart_ref[middle:, :], gather, preferred_element_type=jnp.float32),
        ],
        axis=0,
    )
    moment_ref[:bins, :] = moments[:, :group]
    moment_ref[bins:, :] = moments[:, group:]
    weights = []
    for r in range(4):
        plain = moment_ref[pl.ds(r, quarter, stride=4), :].astype(jnp.bfloat16)
        turned = moment_ref[pl.ds(bins + r, quarter, stride=4), :].astype(jnp.bfloat16)
        weight = jnp.concatenate([plain, turned], axis=0)
        if r % 2:
            weight = jnp.concatenate([weight, jnp.concatenate([turned, -plain], axis=0)], axis=1)
        weights.append(weight)
    piece = 512
    for r in range(4):
        sides = weights[r].shape[1]
        weights_ref[r, :, :sides] = weights[r]

    def transform(i, carry):
        start = pl.multiple_of(i * piece, piece)
        rows = pl.ds(start, piece)
        p0, p1, p2, p3 = (
            jnp.dot(
                tab_ref[r, rows, :],
                weights_ref[r, :, : group * (1 + r % 2)],
                preferred_element_type=jnp.float32,
            )
            for r in range(4)
        )
        odd, turned = p1[:, :group] + p3[:, :group], p1[:, group:] - p3[:, group:]
        even, gap = p0 + p2, p0 - p2
        for q, value in enumerate((even + odd, gap + turned, even - odd, gap - turned)):
            psi_ref[pl.ds(q * span + start, piece), :] = value.astype(jnp.bfloat16)
        return carry

    lax.fori_loop(0, span // piece, transform, 0)

    width = 4 * channels
    section_row = sections_ref[...]
    lane_in_row = section_row % 8

    def quad(i, carry):
        cols = pl.ds(pl.multiple_of(i * width, width), width)
        series = jnp.dot(psi_ref[...], coef_ref[:, cols], preferred_element_type=jnp.float32)
        waveform = wave_t_ref[...].astype(jnp.float32)
        slot = lax.broadcasted_iota(jnp.int32, (8, channels), 0)
        for s in range(4):
            product = jnp.tanh(series[:, s * channels : (s + 1) * channels]) * waveform
            total = jnp.sum(product.reshape(samples // 8, 8, channels), axis=0)
            for shift in (4, 2, 1):
                total = total + pltpu.roll(total, shift, 0)
            rows = pl.ds(pl.multiple_of((sources - 1 - s - 4 * i) * 8, 8), 8)
            kept_ref[rows, :] = jnp.where(slot == lane_in_row, total, 0.0)
        return carry

    lax.fori_loop(0, sources // 4, quad, 0)

    own_rows = receivers // 4 // count // 8
    slots = lax.broadcasted_iota(jnp.int32, (count * 8, channels), 0)
    wanted = section_row // 8
    wanted = wanted // own_rows * 8 + wanted % own_rows
    member = (slots == wanted).astype(jnp.float32).astype(jnp.bfloat16)
    kept = kept_ref[...] * (1.0 / math.sqrt(samples * 4))
    high = kept.astype(jnp.bfloat16)
    low = (kept - high.astype(jnp.float32)).astype(jnp.bfloat16)
    blocks = lax.dot_general(
        jnp.concatenate([member, member], axis=1),
        jnp.concatenate([high, low], axis=1),
        across,
        preferred_element_type=jnp.float32,
    )
    block_ref[...] = blocks.reshape(count, 8, LANES)

    pl.semaphore_wait(barrier, count - 1)

    def copy_to(freq, sub, slot, source):
        return pltpu.make_async_remote_copy(
            src_ref=block_ref.at[freq * sub_size + sub],
            dst_ref=held_ref.at[source],
            send_sem=send_sem.at[slot],
            recv_sem=recv_sem.at[source],
            device_id={"freq": freq, "sub": sub},
            device_id_type=pl.DeviceIdType.MESH,
        )

    sends = []
    for slot, (i, j) in enumerate(partners):
        freq, sub = ahead(i, j)
        sends.append(copy_to(freq, sub, slot, me))
        sends[-1].start()
    total = block_ref[me]
    for slot, (i, j) in enumerate(partners):
        freq, sub = ahead(freq_size - i, sub_size - j)
        source = freq * sub_size + sub
        copy_to(freq, sub, slot, source).wait_recv()
        total = total + held_ref[source]

    halves = [jnp.zeros((8, LANES), jnp.float32)] * (sources // 8)
    for r in range(own_rows):
        spread_row = jnp.broadcast_to(total[r : r + 1, :], (8, LANES))
        moved = pltpu.roll(spread_row, 0, 1, stride=8, stride_axis=0)
        for h in range(sources // 8):
            placed = pltpu.roll(moved, (8 * r + 8 + 64 * h) % LANES, 1)
            halves[h] = jnp.where(lane // 8 == r, placed, halves[h])
    out_ref[...] = jnp.concatenate(halves, axis=0)[:, : own_rows * 8]

    for send in sends:
        send.wait_send()


def fast_fits(mesh_sizes, wavenumbers, source_shapes, source_depths, recorded):
    count = mesh_sizes[0] * mesh_sizes[1]
    bins = wavenumbers.shape[0]
    channels, samples = recorded.shape
    own = channels // 4
    return (
        channels == LANES
        and source_depths.shape[0] * 8 == LANES
        and source_shapes.shape[1] * 4 * FAST_HALF == LANES
        and bins == 4 * LANES
        and samples % (4 * LANES) == 0
        and own % 8 == 0
        and own // 8 <= 8
        and count * 8 % LANES == 0
    )


def per_device(
    mesh_sizes,
    wavenumbers,
    receiver_shapes,
    source_shapes,
    mode_counts,
    source_depths,
    source_ranges,
    sections,
    recorded,
):
    args = (
        wavenumbers,
        receiver_shapes,
        source_shapes,
        mode_counts,
        source_depths,
        source_ranges,
        sections,
        recorded,
    )
    if not fast_fits(mesh_sizes, wavenumbers, source_shapes, source_depths, recorded):
        return per_device_general(mesh_sizes, *args)
    freq_size, sub_size = mesh_sizes
    count = freq_size * sub_size
    bins, modes = wavenumbers.shape
    depth_grid = source_shapes.shape[1]
    sources = source_depths.shape[0]
    channels, samples = recorded.shape
    receivers = channels * count
    reach = 2.0 * (channels - 1) / receivers
    top_phase = K_HALF * 0.5 * (reach + R_TOP)
    assert 2.0 * (0.5 * top_phase) ** FAST_TERMS / math.factorial(FAST_TERMS) < 1e-6

    shape = (bins, modes, depth_grid, sources, channels, samples, mesh_sizes)
    group = depth_grid * 4 * FAST_HALF
    deep = -(-modes // LANES) * LANES
    own = channels // 4
    return pl.pallas_call(
        functools.partial(score_kernel, shape),
        out_shape=pltpu.VMEM((sources, own), jnp.float32),
        in_specs=[pl.BlockSpec(memory_space=pl.ANY)] * 9,
        out_specs=pl.BlockSpec(memory_space=pltpu.VMEM),
        scratch_shapes=[
            pltpu.SMEM((sources,), jnp.int32),
            pltpu.SMEM((sources,), jnp.float32),
            pltpu.VMEM((FAST_HALF, LANES), jnp.float32),
            pltpu.VMEM((1, channels), jnp.int32),
            pltpu.VMEM((1, bins), jnp.int32),
            pltpu.VMEM((modes, bins), jnp.float32),
            pltpu.VMEM((modes, bins), jnp.bfloat16),
            pltpu.VMEM((modes, depth_grid, bins), jnp.bfloat16),
            pltpu.VMEM((channels, samples), jnp.bfloat16),
            pltpu.VMEM((2 * depth_grid, bins, deep), jnp.bfloat16),
            pltpu.VMEM((bins, deep), jnp.float32),
            pltpu.VMEM((bins, group * 2 * FAST_HALF), jnp.bfloat16),
            pltpu.VMEM((2 * bins, group), jnp.float32),
            pltpu.VMEM((4, bins // 2, 2 * group), jnp.bfloat16),
            pltpu.VMEM((4, samples // 4, bins // 2), jnp.bfloat16),
            pltpu.VMEM((samples, group), jnp.bfloat16),
            pltpu.VMEM((group, sources * channels), jnp.bfloat16),
            pltpu.VMEM((samples, channels), jnp.bfloat16),
            pltpu.VMEM((sources * 8, channels), jnp.float32),
            pltpu.VMEM((count, 8, LANES), jnp.float32),
            pltpu.VMEM((count, 8, LANES), jnp.float32),
            pltpu.SemaphoreType.DMA((6 + 3 * bins // LANES,)),
            pltpu.SemaphoreType.DMA((count - 1,)),
            pltpu.SemaphoreType.DMA((count,)),
        ],
        compiler_params=pltpu.CompilerParams(
            vmem_limit_bytes=60 * 1024 * 1024, collective_id=1, has_side_effects=True
        ),
        name="score",
    )(
        source_depths,
        source_ranges,
        jnp.asarray(fast_constants()),
        sections.reshape(1, channels),
        mode_counts.reshape(1, bins),
        wavenumbers.T,
        receiver_shapes.T,
        source_shapes.transpose(2, 1, 0),
        recorded,
    )


def per_device_general(
    mesh_sizes,
    wavenumbers,
    receiver_shapes,
    source_shapes,
    mode_counts,
    source_depths,
    source_ranges,
    sections,
    recorded,
):
    freq_size, sub_size = mesh_sizes
    count = freq_size * sub_size
    me = lax.axis_index("freq") * sub_size + lax.axis_index("sub")
    bins, modes = wavenumbers.shape
    depth_grid = source_shapes.shape[1]
    sources = source_depths.shape[0]
    channels, samples = recorded.shape
    receivers = channels * count

    first_x = 1.0 + 2.0 * (me * channels).astype(jnp.float32) / receivers
    reach = 2.0 * (channels - 1) / receivers
    centre = first_x + 0.5 * (reach - R_TOP)
    top_phase = K_HALF * 0.5 * (reach + R_TOP)
    assert 2.0 * (0.5 * top_phase) ** TERMS / math.factorial(TERMS) < 1e-9
    assert depth_grid * 2 * TERMS <= LANES

    extra = -modes % 8
    wave = wavenumbers.T
    live = jnp.arange(modes, dtype=jnp.int32)[:, None] < mode_counts[None, :]
    factor = receiver_shapes.T.astype(jnp.float32) * (8.0 / math.sqrt(bins))
    factor = jnp.where(live, factor / jnp.sqrt(wave * modes), 0.0)
    factor = jnp.pad(factor, ((0, extra), (0, 0)))
    wave = jnp.pad(wave, ((0, extra), (0, 0)), constant_values=K_MID)
    shape = (bins, modes, depth_grid, sources, channels, samples, receivers)
    matched = pl.pallas_call(
        functools.partial(replica_kernel, shape),
        out_shape=jax.ShapeDtypeStruct((channels, LANES), jnp.float32),
        in_specs=[pl.BlockSpec(memory_space=pltpu.SMEM)] * 3
        + [pl.BlockSpec(memory_space=pltpu.VMEM)] * 5,
        out_specs=pl.BlockSpec(memory_space=pltpu.VMEM),
        scratch_shapes=[
            pltpu.VMEM((depth_grid * 2 * TERMS, bins), jnp.float32),
            pltpu.VMEM((16, LANES), jnp.float32),
            pltpu.VMEM((TERMS * 8, LANES), jnp.float32),
            pltpu.VMEM((bins // 2, samples // 4), jnp.bfloat16),
            pltpu.VMEM((4, depth_grid * 2 * TERMS, samples // 4), jnp.float32),
            pltpu.VMEM((depth_grid * 2 * TERMS, samples), jnp.bfloat16),
            pltpu.VMEM((sources, channels, 2 * TERMS), jnp.bfloat16),
        ],
        compiler_params=pltpu.CompilerParams(vmem_limit_bytes=48 * 1024 * 1024),
        name="replica",
    )(
        source_depths,
        jnp.stack([first_x, centre]),
        source_ranges,
        jnp.asarray(term_constants()),
        wave,
        factor,
        source_shapes.transpose(2, 1, 0),
        recorded,
    )

    section_count = receivers // 4
    own = section_count // count
    per_row = min(LANES // sources, own)
    own_rows = own // per_row
    assert LANES % sources == 0 and own % per_row == 0
    padded = -(-own_rows // 8) * 8
    slot = jnp.arange(count * padded, dtype=jnp.int32)
    wanted = jnp.where(
        slot % padded < own_rows, slot // padded * own_rows + slot % padded, -1
    )
    member = (wanted[:, None] == (sections // per_row)[None, :]).astype(jnp.float32)
    lane_part = jnp.arange(LANES, dtype=jnp.int32) // sources
    kept = jnp.where((sections % per_row)[:, None] == lane_part[None, :], matched, 0.0)
    blocks = jnp.dot(member, kept, precision=lax.Precision.HIGHEST) * (
        1.0 / math.sqrt(samples * (receivers // section_count))
    )
    blocks = blocks.reshape(count, padded, LANES)
    total = pl.pallas_call(
        functools.partial(exchange_kernel, (freq_size, sub_size)),
        out_shape=jax.ShapeDtypeStruct((padded, LANES), jnp.float32),
        in_specs=[pl.BlockSpec(memory_space=pltpu.VMEM)],
        out_specs=pl.BlockSpec(memory_space=pltpu.VMEM),
        scratch_shapes=[
            pltpu.VMEM((count, padded, LANES), jnp.float32),
            pltpu.SemaphoreType.DMA((count,)),
            pltpu.SemaphoreType.DMA((count,)),
        ],
        compiler_params=pltpu.CompilerParams(collective_id=0, has_side_effects=True),
        name="exchange",
    )(blocks)
    total = total[:own_rows, : per_row * sources].reshape(own_rows, per_row, sources)
    return total.transpose(2, 0, 1).reshape(sources, own)


def solution(mesh):
    sizes = (mesh.shape["freq"], mesh.shape["sub"])
    in_specs = (
        P(),
        P(),
        P(),
        P(),
        P("groups"),
        P("groups"),
        P(("freq", "sub")),
        P(("freq", "sub"), None),
    )
    out_specs = P("groups", ("freq", "sub"))
    return jax.shard_map(
        functools.partial(per_device, sizes),
        mesh=mesh,
        in_specs=in_specs,
        out_specs=out_specs,
        check_vma=False,
    )
```

```python
import functools
import math

import jax
import jax.numpy as jnp
import numpy as np
from jax import lax
from jax.experimental import pallas as pl
from jax.experimental.pallas import tpu as pltpu
from jax.sharding import PartitionSpec as P

MMIN = 64
F0 = 256
SPREAD = 16
K_LOW, K_TOP = 1.0, 20.0
R_TOP = 0.5
K_MID, K_HALF = 0.5 * (K_LOW + K_TOP), 0.5 * (K_TOP - K_LOW)
LANES = 128
TERMS = 16
TWO_PI = 2.0 * math.pi


def fitted(function, count):
    angle = np.pi * (np.arange(200) + 0.5) / 200
    square = 0.125 * (1.0 + np.cos(angle))
    series = np.polynomial.chebyshev.Chebyshev.fit(
        square, function(np.sqrt(square)), count - 1, domain=[0.0, 0.25]
    )
    return [float(c) for c in series.convert(kind=np.polynomial.Polynomial).coef]


SINE = fitted(lambda x: np.sin(np.pi * x) / x, 5)
COSINE = fitted(lambda x: np.cos(np.pi * x), 5)


def horner(coefficients, x):
    value = coefficients[-1] * x + coefficients[-2]
    for c in coefficients[-3::-1]:
        value = value * x + c
    return value


def sincos_turns(turns):
    part = turns - jnp.floor(turns + 0.5)
    square = part * part
    s = horner(SINE, square) * part
    c = horner(COSINE, square)
    twice = s + s
    return 1.0 - twice * s, twice * c


def term_constants():
    nodes = np.cos(np.pi * (np.arange(TERMS) + 0.5) / TERMS)[: TERMS // 2]
    order = np.arange(TERMS)
    table = np.cos(order[:, None] * np.arccos(nodes)[None, :])
    table *= (np.where(order == 0, 1.0, 2.0) * 2.0 / TERMS)[:, None]
    half = TERMS // 2
    out = np.zeros((half, LANES), np.float32)
    out[:, 0] = K_HALF * nodes
    out[:, 1 : 1 + half] = table[0::2]
    out[:, 1 + half : 1 + 2 * half] = table[1::2]
    return out


def place_of(n):
    return n // 2 if n % 2 == 0 else TERMS // 2 + n // 2


def replica_kernel(
    shape,
    depths_ref,
    place_ref,
    ranges_ref,
    consts_ref,
    wave_ref,
    factor_ref,
    source_ref,
    recorded_ref,
    out_ref,
    sum_ref,
    weight_ref,
    term_ref,
    tab_ref,
    part_ref,
    psi_ref,
    coef_ref,
):
    bins, modes, depth_grid, sources, channels, samples, receivers = shape
    quarter = bins // 4
    span = samples // 4
    half = TERMS // 2
    first_x = place_ref[0]
    centre = place_ref[1]

    for first in range(0, bins, LANES):
        last = first + LANES - 1
        top = min(modes, MMIN + (modes - MMIN) * last // max(bins - 1, 1) + SPREAD)
        cols = slice(first, first + LANES)

        def modal(step, sums, cols=cols):
            start = pl.multiple_of(step * 8, 8)
            rows = pl.ds(start, 8)
            wave = wave_ref[rows, cols]
            cosine, sine = sincos_turns(wave * (centre * (1.0 / TWO_PI)))
            factor = factor_ref[rows, cols]
            weight_ref[0:8, :] = factor * cosine
            weight_ref[8:16, :] = factor * sine
            xi = (wave - K_MID) * (1.0 / K_HALF)
            before, now = jnp.ones_like(xi), xi
            for n in range(1, TERMS):
                term_ref[n * 8 : n * 8 + 8, :] = now
                before, now = now, 2.0 * xi * now - before
            sums = list(sums)
            for i in range(8):
                source = source_ref[jnp.minimum(start + i, modes - 1), :, cols].astype(jnp.float32)
                value = jnp.concatenate(
                    [source * weight_ref[i : i + 1, :], source * weight_ref[8 + i : 9 + i, :]], axis=0
                )
                sums[0] = sums[0] + value
                for n in range(1, TERMS):
                    sums[n] = sums[n] + value * term_ref[n * 8 + i : n * 8 + i + 1, :]
            return tuple(sums)

        zero = jnp.zeros((2 * depth_grid, LANES), jnp.float32)
        sums = lax.fori_loop(0, -(-top // 8), modal, (zero,) * TERMS)
        for n in range(TERMS):
            for z in range(depth_grid):
                for c in range(2):
                    at = z * 2 * TERMS + c * TERMS + place_of(n)
                    row = c * depth_grid + z
                    sum_ref[at : at + 1, cols] = sums[n][row : row + 1, :]

    def times_i(value):
        blocks = []
        for z in range(depth_grid):
            base = z * 2 * TERMS
            blocks.append(-value[base + TERMS : base + 2 * TERMS])
            blocks.append(value[base : base + TERMS])
        return jnp.concatenate(blocks, axis=0)

    moments = sum_ref[...]
    moments = jnp.concatenate([moments, -times_i(moments)], axis=0).astype(jnp.bfloat16)
    group = depth_grid * 2 * TERMS

    for r in range(4):
        row = lax.broadcasted_iota(jnp.int32, (quarter, LANES), 0)
        column = lax.broadcasted_iota(jnp.int32, (quarter, LANES), 1)
        number = F0 + 4 * row + r
        whole = (number * column) % samples
        cosine, sine = sincos_turns(whole.astype(jnp.float32) * (1.0 / samples))
        turn = (number * LANES) % samples
        step_c, step_s = sincos_turns(turn.astype(jnp.float32) * (1.0 / samples))
        for block in range(span // LANES):
            cols = slice(block * LANES, (block + 1) * LANES)
            tab_ref[:quarter, cols] = cosine.astype(jnp.bfloat16)
            tab_ref[quarter:, cols] = (-sine).astype(jnp.bfloat16)
            cosine, sine = cosine * step_c - sine * step_s, cosine * step_s + sine * step_c
        bin_row = lax.broadcasted_iota(jnp.int32, (bins, quarter), 0)
        bin_column = lax.broadcasted_iota(jnp.int32, (bins, quarter), 1)
        chosen = (bin_row == 4 * bin_column + r).astype(jnp.float32).astype(jnp.bfloat16)
        picked = jnp.dot(moments, chosen, preferred_element_type=jnp.float32)
        left = jnp.concatenate([picked[:group], picked[group:]], axis=1)
        part_ref[r] = jnp.dot(
            left.astype(jnp.bfloat16), tab_ref[...], preferred_element_type=jnp.float32
        )

    for block in range(span // LANES):
        cols = slice(block * LANES, (block + 1) * LANES)
        p0, p1, p2, p3 = (part_ref[r, :, cols] for r in range(4))
        even, odd = p0 + p2, p1 + p3
        gap, turned = p0 - p2, times_i(p1 - p3)
        for q, value in enumerate((even + odd, gap + turned, even - odd, gap - turned)):
            at = q * span + block * LANES
            psi_ref[:, at : at + LANES] = value.astype(jnp.bfloat16)

    channel = lax.broadcasted_iota(jnp.int32, (1, channels), 1).astype(jnp.float32)
    position = first_x + channel * (2.0 / receivers)
    spread = lax.rsqrt(position)
    nodes = consts_ref[:, 0:1]
    for s in range(sources):
        offset = position - (ranges_ref[s] + centre)
        cosine, sine = sincos_turns(nodes * offset * (1.0 / TWO_PI))
        even = jnp.zeros((half, channels), jnp.float32)
        odd = jnp.zeros((half, channels), jnp.float32)
        for j in range(half):
            even = even + consts_ref[:, 1 + j : 2 + j] * cosine[j : j + 1, :]
            odd = odd + consts_ref[:, 1 + half + j : 2 + half + j] * sine[j : j + 1, :]
        mid_c, mid_s = sincos_turns(offset * (K_MID / TWO_PI))
        mid_c, mid_s = mid_c * spread, mid_s * spread
        rows = jnp.concatenate([mid_c * even, -mid_s * odd, -mid_s * even, -mid_c * odd], axis=0)
        coef_ref[s] = rows.T.astype(jnp.bfloat16)

    chunk = 512

    def source(s, matched):
        z = depths_ref[s]
        terms = pl.ds(pl.multiple_of(z * (2 * TERMS), 2 * TERMS), 2 * TERMS)
        coef = coef_ref[s]
        total = jnp.zeros((channels, LANES), jnp.float32)
        for start in range(0, samples, chunk):
            series = jnp.dot(
                coef, psi_ref[terms, start : start + chunk], preferred_element_type=jnp.float32
            )
            product = jnp.tanh(series) * recorded_ref[:, start : start + chunk].astype(jnp.float32)
            for tile in range(chunk // LANES):
                total = total + product[:, tile * LANES : (tile + 1) * LANES]
        value = jnp.sum(total, axis=1, keepdims=True)
        lane = lax.broadcasted_iota(jnp.int32, (channels, LANES), 1)
        return jnp.where(lane % sources == s, value, matched)

    out_ref[...] = lax.fori_loop(
        0, sources, source, jnp.zeros((channels, LANES), jnp.float32)
    )


def exchange_kernel(sizes, block_ref, out_ref, held_ref, send_sem, recv_sem):
    freq_size, sub_size = sizes
    count = freq_size * sub_size
    me = lax.axis_index("freq") * sub_size + lax.axis_index("sub")
    barrier = pltpu.get_barrier_semaphore()

    def place(number):
        return {"freq": number // sub_size, "sub": number % sub_size}

    def greet(i, carry):
        pl.semaphore_signal(
            barrier,
            inc=1,
            device_id=place((me + i) % count),
            device_id_type=pl.DeviceIdType.MESH,
        )
        return carry

    lax.fori_loop(1, count, greet, 0)
    pl.semaphore_wait(barrier, count - 1)

    def copy_to(target, source):
        return pltpu.make_async_remote_copy(
            src_ref=block_ref.at[target],
            dst_ref=held_ref.at[source],
            send_sem=send_sem.at[target],
            recv_sem=recv_sem.at[source],
            device_id=place(target),
            device_id_type=pl.DeviceIdType.MESH,
        )

    def send(i, carry):
        copy_to((me + i) % count, me).start()
        return carry

    lax.fori_loop(1, count, send, 0)

    def receive(i, total):
        source = (me + count - i) % count
        copy_to(source, source).wait_recv()
        return total + held_ref[source]

    out_ref[...] = lax.fori_loop(1, count, receive, block_ref[me])

    def drain(i, carry):
        copy_to((me + i) % count, me).wait_send()
        return carry

    lax.fori_loop(1, count, drain, 0)

FAST_TERMS = 12
FAST_HALF = 8


def fast_constants():
    nodes = np.cos(np.pi * (np.arange(FAST_TERMS) + 0.5) / FAST_TERMS)[: FAST_TERMS // 2]
    order = np.arange(FAST_TERMS)
    table = np.cos(order[:, None] * np.arccos(nodes)[None, :])
    table *= (np.where(order == 0, 1.0, 2.0) * 2.0 / FAST_TERMS)[:, None]
    half = FAST_TERMS // 2
    out = np.zeros((FAST_HALF, LANES), np.float32)
    out[:half, 0] = K_HALF * nodes
    out[half, 0] = K_MID
    out[:half, 1 : 1 + half] = table[0::2]
    out[:half, 1 + half : 1 + 2 * half] = table[1::2]
    return out


def fast_place(n):
    return n // 2 if n % 2 == 0 else FAST_HALF + n // 2


def score_kernel(
    shape,
    depths_hbm,
    ranges_hbm,
    consts_hbm,
    sections_hbm,
    counts_hbm,
    wave_hbm,
    receiver_hbm,
    source_hbm,
    recorded_hbm,
    out_ref,
    depths_ref,
    ranges_ref,
    consts_ref,
    sections_ref,
    counts_ref,
    wave_ref,
    receiver_ref,
    source_ref,
    recorded_ref,
    flat_ref,
    left_ref,
    xi_ref,
    apart_ref,
    moment_ref,
    weights_ref,
    tab_ref,
    psi_ref,
    coef_ref,
    wave_t_ref,
    kept_ref,
    member_ref,
    block_ref,
    held_ref,
    load_sem,
    send_sem,
    recv_sem,
):
    bins, modes, depth_grid, sources, channels, samples, sizes = shape
    freq_size, sub_size = sizes
    count = freq_size * sub_size
    receivers = channels * count
    quarter = bins // 4
    span = samples // 4
    half = FAST_TERMS // 2
    group = depth_grid * 4 * FAST_HALF
    me = lax.axis_index("freq") * sub_size + lax.axis_index("sub")
    barrier = pltpu.get_barrier_semaphore()

    def top_of(last):
        return min(modes, MMIN + (modes - MMIN) * last // max(bins - 1, 1) + SPREAD)

    pairs = [
        (depths_hbm, depths_ref),
        (ranges_hbm, ranges_ref),
        (consts_hbm, consts_ref),
        (sections_hbm, sections_ref),
        (counts_hbm, counts_ref),
    ]
    for first in range(0, bins, LANES):
        cols = slice(first, first + LANES)
        rows = min(-(-top_of(first + LANES - 1) // 16) * 16, modes)
        pairs.append((wave_hbm.at[:rows, cols], wave_ref.at[:rows, cols]))
        pairs.append((receiver_hbm.at[:rows, cols], receiver_ref.at[:rows, cols]))
        pairs.append((source_hbm.at[:rows, :, cols], source_ref.at[:rows, :, cols]))
    pairs.append((recorded_hbm, recorded_ref))
    loads = [
        pltpu.make_async_copy(source, target, load_sem.at[i])
        for i, (source, target) in enumerate(pairs)
    ]
    for load in loads:
        load.start()

    my_freq = lax.axis_index("freq")
    my_sub = lax.axis_index("sub")
    partners = [(i, j) for i in range(1, freq_size) for j in range(sub_size)]
    partners += [(0, j) for j in range(1, sub_size)]

    def ahead(i, j):
        return lax.rem(my_freq + i, freq_size), lax.rem(my_sub + j, sub_size)

    reach = 2.0 * (channels - 1) / receivers
    first_x = 1.0 + (me * channels).astype(jnp.float32) * (2.0 / receivers)
    centre = first_x + 0.5 * (reach - R_TOP)

    lane = lax.broadcasted_iota(jnp.int32, (8, LANES), 1)
    row = lax.broadcasted_iota(jnp.int32, (8, LANES), 0)
    for r in range(4):
        number = F0 + 4 * lane + r
        whole = (number * row) % samples
        cosine, sine = sincos_turns(whole.astype(jnp.float32) * (1.0 / samples))
        turn = (number * 8) % samples
        step_c, step_s = sincos_turns(turn.astype(jnp.float32) * (1.0 / samples))
        for pair in range(span // 16):
            turned_c = cosine * step_c - sine * step_s
            turned_s = cosine * step_s + sine * step_c
            rows = slice(pair * 16, pair * 16 + 16)
            tab_ref[r, rows, :quarter] = jnp.concatenate([cosine, turned_c], axis=0).astype(jnp.bfloat16)
            tab_ref[r, rows, quarter:] = jnp.concatenate([sine, turned_s], axis=0).astype(jnp.bfloat16)
            cosine = turned_c * step_c - turned_s * step_s
            sine = turned_c * step_s + turned_s * step_c

    for load in loads[:5]:
        load.wait()

    channel = lax.broadcasted_iota(jnp.int32, (1, channels), 1).astype(jnp.float32)
    position = first_x + channel * (2.0 / receivers)
    spread = lax.rsqrt(position)
    for i, j in partners:
        freq, sub = ahead(i, j)
        pl.semaphore_signal(
            barrier,
            inc=1,
            device_id={"freq": freq, "sub": sub},
            device_id_type=pl.DeviceIdType.MESH,
        )

    nodes = consts_ref[:, 0:1]

    def coefficients(i):
        for s in range(4):
            number = i * 4 + s
            offset = position - (ranges_ref[number] + centre)
            cosine, sine = sincos_turns(nodes * offset * (1.0 / TWO_PI))
            even = jnp.zeros((FAST_HALF, channels), jnp.float32)
            odd = jnp.zeros((FAST_HALF, channels), jnp.float32)
            for j in range(half):
                even = even + consts_ref[:, 1 + j : 2 + j] * cosine[j : j + 1, :]
                odd = odd + consts_ref[:, 1 + half + j : 2 + half + j] * sine[j : j + 1, :]
            mid_c, mid_s = cosine[half : half + 1, :] * spread, sine[half : half + 1, :] * spread
            parts = jnp.concatenate([mid_c * even, -mid_s * odd, -mid_s * even, -mid_c * odd], axis=0)
            for z in range(depth_grid):
                here = jnp.where(depths_ref[number] == z, 1.0, 0.0)
                rows = slice(z * 4 * FAST_HALF, (z + 1) * 4 * FAST_HALF)
                cols = slice(s * channels, (s + 1) * channels)
                coef_ref[i, rows, cols] = (parts * here).astype(jnp.bfloat16)

    coefficients(0)

    def filled(value, rows):
        lack = rows - value.shape[0]
        if lack == 0:
            return value
        return jnp.concatenate([value, jnp.zeros((lack, value.shape[1]), value.dtype)], axis=0)

    for block, first in enumerate(range(0, bins, LANES)):
        for load in loads[5 + 3 * block : 8 + 3 * block]:
            load.wait()
        cols = slice(first, first + LANES)
        deep = -(-top_of(first + LANES - 1) // LANES) * LANES
        rows = min(-(-top_of(first + LANES - 1) // 16) * 16, modes)
        whole = -(-rows // 16) * 16
        wave = wave_ref[:rows, cols]
        cosine, sine = sincos_turns(wave * (centre * (1.0 / TWO_PI)))
        index = lax.broadcasted_iota(jnp.int32, (rows, LANES), 0)
        factor = receiver_ref[:rows, cols].astype(jnp.float32) * (8.0 / math.sqrt(bins * modes))
        factor = jnp.where(index < counts_ref[:, cols], factor * lax.rsqrt(wave), 0.0)
        xi = (wave - K_MID) * (1.0 / K_HALF)
        xi_ref[cols, :deep] = filled(filled(xi, whole), deep).T
        weights = (factor * cosine, factor * sine)
        base = block * modes * depth_grid
        flat_ref[base : base + rows * depth_grid, :] = (
            source_ref[:rows, :, cols].astype(jnp.float32).reshape(rows * depth_grid, LANES)
        )
        for z in range(depth_grid):
            source = flat_ref[pl.ds(base + z, rows, stride=depth_grid), :]
            for c in range(2):
                value = filled(source * weights[c], whole).astype(jnp.bfloat16)
                left_ref[z * 2 + c, cols, :deep] = filled(value, deep).T

    loads[-1].wait()
    for block in range(samples // LANES):
        rows = slice(block * LANES, (block + 1) * LANES)
        wave_t_ref[rows, :] = recorded_ref[:, rows].T

    across = (((1,), (1,)), ((), ()))
    terms = 2 * FAST_HALF
    kinds = 2 * depth_grid
    same_bin = (
        lax.broadcasted_iota(jnp.int32, (16, terms * 16), 0)
        == lax.broadcasted_iota(jnp.int32, (16, terms * 16), 1) % 16
    )
    for g in range(bins // 16):
        rows = slice(g * 16, g * 16 + 16)
        deep = -(-top_of(g * 16 + 15) // LANES) * LANES
        xi = xi_ref[rows, :deep]
        double = xi + xi
        before, now = jnp.ones_like(xi), xi
        right = [before.astype(jnp.bfloat16)]
        for n in range(1, FAST_TERMS):
            right.append(now.astype(jnp.bfloat16))
            before, now = now, double * now - before
        right = right + [jnp.zeros_like(right[0])] * (terms - FAST_TERMS)
        left = jnp.concatenate([left_ref[k, rows, :deep] for k in range(kinds)], axis=0)
        pairs = lax.dot_general(
            left, jnp.concatenate(right, axis=0), across, preferred_element_type=jnp.float32
        )
        for k in range(kinds):
            value = jnp.where(same_bin, pairs[k * 16 : k * 16 + 16], 0.0)
            apart_ref[rows, k * terms * 16 : (k + 1) * terms * 16] = value.astype(jnp.bfloat16)

    term = lax.broadcasted_iota(jnp.int32, (terms * 16, group), 0) // 16
    column = lax.broadcasted_iota(jnp.int32, (terms * 16, group), 1)
    column = column - (term // 2 + FAST_HALF * (term % 2))
    column = jnp.where(term < FAST_TERMS, column, -1)
    gathers = []
    for k in range(kinds):
        z, c = k // 2, k % 2
        plain = jnp.where(column == k * terms, 1.0, 0.0)
        turned = jnp.where(column == (z * 2 + 1 - c) * terms, 1.0 - 2.0 * c, 0.0)
        gathers.append(jnp.concatenate([plain, turned], axis=1).astype(jnp.bfloat16))
    gather = jnp.concatenate(gathers, axis=0)
    middle = bins // 2
    moments = jnp.concatenate(
        [
            jnp.dot(apart_ref[:middle, :], gather, preferred_element_type=jnp.float32),
            jnp.dot(apart_ref[middle:, :], gather, preferred_element_type=jnp.float32),
        ],
        axis=0,
    )
    moment_ref[:bins, :] = moments[:, :group]
    moment_ref[bins:, :] = moments[:, group:]
    weights = []
    for r in range(4):
        plain = moment_ref[pl.ds(r, quarter, stride=4), :].astype(jnp.bfloat16)
        turned = moment_ref[pl.ds(bins + r, quarter, stride=4), :].astype(jnp.bfloat16)
        weight = jnp.concatenate([plain, turned], axis=0)
        if r % 2:
            weight = jnp.concatenate([weight, jnp.concatenate([turned, -plain], axis=0)], axis=1)
        weights.append(weight)
    piece = 512
    for r in range(4):
        sides = weights[r].shape[1]
        weights_ref[r, :, :sides] = weights[r]

    def transform(i, carry):
        start = pl.multiple_of(i * piece, piece)
        rows = pl.ds(start, piece)
        p0, p1, p2, p3 = (
            jnp.dot(
                tab_ref[r, rows, :],
                weights_ref[r, :, : group * (1 + r % 2)],
                preferred_element_type=jnp.float32,
            )
            for r in range(4)
        )
        odd, turned = p1[:, :group] + p3[:, :group], p1[:, group:] - p3[:, group:]
        even, gap = p0 + p2, p0 - p2
        for q, value in enumerate((even + odd, gap + turned, even - odd, gap - turned)):
            psi_ref[pl.ds(q * span + start, piece), :] = value.astype(jnp.bfloat16)
        return carry

    lax.fori_loop(0, span // piece, transform, 0)

    section_row = sections_ref[...]
    lane_in_row = section_row % 8
    own_rows = receivers // 4 // count // 8
    slots = lax.broadcasted_iota(jnp.int32, (count * 8, channels), 0)
    wanted = section_row // 8
    wanted = wanted // own_rows * 8 + wanted % own_rows
    member_ref[...] = (slots == wanted).astype(jnp.float32).astype(jnp.bfloat16)

    def quad(i, carry):
        series = jnp.dot(psi_ref[...], coef_ref[i], preferred_element_type=jnp.float32)
        waveform = wave_t_ref[...].astype(jnp.float32)
        slot = lax.broadcasted_iota(jnp.int32, (8, channels), 0)
        for s in range(4):
            product = jnp.tanh(series[:, s * channels : (s + 1) * channels]) * waveform
            total = jnp.sum(product.reshape(samples // 8, 8, channels), axis=0)
            for shift in (4, 2, 1):
                total = total + pltpu.roll(total, shift, 0)
            rows = pl.ds((sources - 1 - s - 4 * i) * 8, 8)
            kept_ref[rows, :] = jnp.where(slot == lane_in_row, total, 0.0)
        if i + 1 < sources // 4:
            coefficients(i + 1)
        return carry

    for i in range(sources // 4):
        quad(i, 0)

    member = member_ref[...]
    kept = kept_ref[...] * (1.0 / math.sqrt(samples * 4))
    high = kept.astype(jnp.bfloat16)
    low = (kept - high.astype(jnp.float32)).astype(jnp.bfloat16)
    blocks = lax.dot_general(
        jnp.concatenate([member, member], axis=1),
        jnp.concatenate([high, low], axis=1),
        across,
        preferred_element_type=jnp.float32,
    )
    block_ref[...] = blocks.reshape(count, 8, LANES)

    pl.semaphore_wait(barrier, count - 1)

    def copy_to(freq, sub, slot, source):
        return pltpu.make_async_remote_copy(
            src_ref=block_ref.at[freq * sub_size + sub],
            dst_ref=held_ref.at[source],
            send_sem=send_sem.at[slot],
            recv_sem=recv_sem.at[source],
            device_id={"freq": freq, "sub": sub},
            device_id_type=pl.DeviceIdType.MESH,
        )

    sends = []
    for slot, (i, j) in enumerate(partners):
        freq, sub = ahead(i, j)
        sends.append(copy_to(freq, sub, slot, me))
        sends[-1].start()
    total = block_ref[me]
    for slot, (i, j) in enumerate(partners):
        freq, sub = ahead(freq_size - i, sub_size - j)
        source = freq * sub_size + sub
        copy_to(freq, sub, slot, source).wait_recv()
        total = total + held_ref[source]

    halves = [jnp.zeros((8, LANES), jnp.float32)] * (sources // 8)
    for r in range(own_rows):
        spread_row = jnp.broadcast_to(total[r : r + 1, :], (8, LANES))
        moved = pltpu.roll(spread_row, 0, 1, stride=8, stride_axis=0)
        for h in range(sources // 8):
            placed = pltpu.roll(moved, (8 * r + 8 + 64 * h) % LANES, 1)
            halves[h] = jnp.where(lane // 8 == r, placed, halves[h])
    out_ref[...] = jnp.concatenate(halves, axis=0)[:, : own_rows * 8]

    for send in sends:
        send.wait_send()


def fast_fits(mesh_sizes, wavenumbers, source_shapes, source_depths, recorded):
    count = mesh_sizes[0] * mesh_sizes[1]
    bins = wavenumbers.shape[0]
    channels, samples = recorded.shape
    own = channels // 4
    return (
        channels == LANES
        and source_depths.shape[0] * 8 == LANES
        and source_shapes.shape[1] * 4 * FAST_HALF == LANES
        and bins == 4 * LANES
        and samples % (4 * LANES) == 0
        and own % 8 == 0
        and own // 8 <= 8
        and count * 8 % LANES == 0
    )


def per_device(
    mesh_sizes,
    wavenumbers,
    receiver_shapes,
    source_shapes,
    mode_counts,
    source_depths,
    source_ranges,
    sections,
    recorded,
):
    args = (
        wavenumbers,
        receiver_shapes,
        source_shapes,
        mode_counts,
        source_depths,
        source_ranges,
        sections,
        recorded,
    )
    if not fast_fits(mesh_sizes, wavenumbers, source_shapes, source_depths, recorded):
        return per_device_general(mesh_sizes, *args)
    freq_size, sub_size = mesh_sizes
    count = freq_size * sub_size
    bins, modes = wavenumbers.shape
    depth_grid = source_shapes.shape[1]
    sources = source_depths.shape[0]
    channels, samples = recorded.shape
    receivers = channels * count
    reach = 2.0 * (channels - 1) / receivers
    top_phase = K_HALF * 0.5 * (reach + R_TOP)
    assert 2.0 * (0.5 * top_phase) ** FAST_TERMS / math.factorial(FAST_TERMS) < 1e-6

    shape = (bins, modes, depth_grid, sources, channels, samples, mesh_sizes)
    group = depth_grid * 4 * FAST_HALF
    deep = -(-modes // LANES) * LANES
    own = channels // 4
    return pl.pallas_call(
        functools.partial(score_kernel, shape),
        out_shape=pltpu.VMEM((sources, own), jnp.float32),
        in_specs=[pl.BlockSpec(memory_space=pl.ANY)] * 9,
        out_specs=pl.BlockSpec(memory_space=pltpu.VMEM),
        scratch_shapes=[
            pltpu.SMEM((sources,), jnp.int32),
            pltpu.SMEM((sources,), jnp.float32),
            pltpu.VMEM((FAST_HALF, LANES), jnp.float32),
            pltpu.VMEM((1, channels), jnp.int32),
            pltpu.VMEM((1, bins), jnp.int32),
            pltpu.VMEM((modes, bins), jnp.float32),
            pltpu.VMEM((modes, bins), jnp.bfloat16),
            pltpu.VMEM((modes, depth_grid, bins), jnp.bfloat16),
            pltpu.VMEM((channels, samples), jnp.bfloat16),
            pltpu.VMEM((bins // LANES * modes * depth_grid, LANES), jnp.float32),
            pltpu.VMEM((2 * depth_grid, bins, deep), jnp.bfloat16),
            pltpu.VMEM((bins, deep), jnp.float32),
            pltpu.VMEM((bins, group * 2 * FAST_HALF), jnp.bfloat16),
            pltpu.VMEM((2 * bins, group), jnp.float32),
            pltpu.VMEM((4, bins // 2, 2 * group), jnp.bfloat16),
            pltpu.VMEM((4, samples // 4, bins // 2), jnp.bfloat16),
            pltpu.VMEM((samples, group), jnp.bfloat16),
            pltpu.VMEM((sources // 4 + 1, group, 4 * channels), jnp.bfloat16),
            pltpu.VMEM((samples, channels), jnp.bfloat16),
            pltpu.VMEM((sources * 8, channels), jnp.float32),
            pltpu.VMEM((count * 8, channels), jnp.bfloat16),
            pltpu.VMEM((count, 8, LANES), jnp.float32),
            pltpu.VMEM((count, 8, LANES), jnp.float32),
            pltpu.SemaphoreType.DMA((6 + 3 * bins // LANES,)),
            pltpu.SemaphoreType.DMA((count - 1,)),
            pltpu.SemaphoreType.DMA((count,)),
        ],
        compiler_params=pltpu.CompilerParams(
            vmem_limit_bytes=60 * 1024 * 1024, collective_id=1, has_side_effects=True
        ),
        name="score",
    )(
        source_depths,
        source_ranges,
        jnp.asarray(fast_constants()),
        sections.reshape(1, channels),
        mode_counts.reshape(1, bins),
        wavenumbers.T,
        receiver_shapes.T,
        source_shapes.transpose(2, 1, 0),
        recorded,
    )


def per_device_general(
    mesh_sizes,
    wavenumbers,
    receiver_shapes,
    source_shapes,
    mode_counts,
    source_depths,
    source_ranges,
    sections,
    recorded,
):
    freq_size, sub_size = mesh_sizes
    count = freq_size * sub_size
    me = lax.axis_index("freq") * sub_size + lax.axis_index("sub")
    bins, modes = wavenumbers.shape
    depth_grid = source_shapes.shape[1]
    sources = source_depths.shape[0]
    channels, samples = recorded.shape
    receivers = channels * count

    first_x = 1.0 + 2.0 * (me * channels).astype(jnp.float32) / receivers
    reach = 2.0 * (channels - 1) / receivers
    centre = first_x + 0.5 * (reach - R_TOP)
    top_phase = K_HALF * 0.5 * (reach + R_TOP)
    assert 2.0 * (0.5 * top_phase) ** TERMS / math.factorial(TERMS) < 1e-9
    assert depth_grid * 2 * TERMS <= LANES

    extra = -modes % 8
    wave = wavenumbers.T
    live = jnp.arange(modes, dtype=jnp.int32)[:, None] < mode_counts[None, :]
    factor = receiver_shapes.T.astype(jnp.float32) * (8.0 / math.sqrt(bins))
    factor = jnp.where(live, factor / jnp.sqrt(wave * modes), 0.0)
    factor = jnp.pad(factor, ((0, extra), (0, 0)))
    wave = jnp.pad(wave, ((0, extra), (0, 0)), constant_values=K_MID)
    shape = (bins, modes, depth_grid, sources, channels, samples, receivers)
    matched = pl.pallas_call(
        functools.partial(replica_kernel, shape),
        out_shape=jax.ShapeDtypeStruct((channels, LANES), jnp.float32),
        in_specs=[pl.BlockSpec(memory_space=pltpu.SMEM)] * 3
        + [pl.BlockSpec(memory_space=pltpu.VMEM)] * 5,
        out_specs=pl.BlockSpec(memory_space=pltpu.VMEM),
        scratch_shapes=[
            pltpu.VMEM((depth_grid * 2 * TERMS, bins), jnp.float32),
            pltpu.VMEM((16, LANES), jnp.float32),
            pltpu.VMEM((TERMS * 8, LANES), jnp.float32),
            pltpu.VMEM((bins // 2, samples // 4), jnp.bfloat16),
            pltpu.VMEM((4, depth_grid * 2 * TERMS, samples // 4), jnp.float32),
            pltpu.VMEM((depth_grid * 2 * TERMS, samples), jnp.bfloat16),
            pltpu.VMEM((sources, channels, 2 * TERMS), jnp.bfloat16),
        ],
        compiler_params=pltpu.CompilerParams(vmem_limit_bytes=48 * 1024 * 1024),
        name="replica",
    )(
        source_depths,
        jnp.stack([first_x, centre]),
        source_ranges,
        jnp.asarray(term_constants()),
        wave,
        factor,
        source_shapes.transpose(2, 1, 0),
        recorded,
    )

    section_count = receivers // 4
    own = section_count // count
    per_row = min(LANES // sources, own)
    own_rows = own // per_row
    assert LANES % sources == 0 and own % per_row == 0
    padded = -(-own_rows // 8) * 8
    slot = jnp.arange(count * padded, dtype=jnp.int32)
    wanted = jnp.where(
        slot % padded < own_rows, slot // padded * own_rows + slot % padded, -1
    )
    member = (wanted[:, None] == (sections // per_row)[None, :]).astype(jnp.float32)
    lane_part = jnp.arange(LANES, dtype=jnp.int32) // sources
    kept = jnp.where((sections % per_row)[:, None] == lane_part[None, :], matched, 0.0)
    blocks = jnp.dot(member, kept, precision=lax.Precision.HIGHEST) * (
        1.0 / math.sqrt(samples * (receivers // section_count))
    )
    blocks = blocks.reshape(count, padded, LANES)
    total = pl.pallas_call(
        functools.partial(exchange_kernel, (freq_size, sub_size)),
        out_shape=jax.ShapeDtypeStruct((padded, LANES), jnp.float32),
        in_specs=[pl.BlockSpec(memory_space=pltpu.VMEM)],
        out_specs=pl.BlockSpec(memory_space=pltpu.VMEM),
        scratch_shapes=[
            pltpu.VMEM((count, padded, LANES), jnp.float32),
            pltpu.SemaphoreType.DMA((count,)),
            pltpu.SemaphoreType.DMA((count,)),
        ],
        compiler_params=pltpu.CompilerParams(collective_id=0, has_side_effects=True),
        name="exchange",
    )(blocks)
    total = total[:own_rows, : per_row * sources].reshape(own_rows, per_row, sources)
    return total.transpose(2, 0, 1).reshape(sources, own)


def solution(mesh):
    sizes = (mesh.shape["freq"], mesh.shape["sub"])
    in_specs = (
        P(),
        P(),
        P(),
        P(),
        P("groups"),
        P("groups"),
        P(("freq", "sub")),
        P(("freq", "sub"), None),
    )
    out_specs = P("groups", ("freq", "sub"))
    return jax.shard_map(
        functools.partial(per_device, sizes),
        mesh=mesh,
        in_specs=in_specs,
        out_specs=out_specs,
        check_vma=False,
    )
```

```python
import functools
import math

import jax
import jax.numpy as jnp
import numpy as np
from jax import lax
from jax.experimental import pallas as pl
from jax.experimental.pallas import tpu as pltpu
from jax.sharding import PartitionSpec as P

MMIN = 64
F0 = 256
SPREAD = 16
K_LOW, K_TOP = 1.0, 20.0
R_TOP = 0.5
K_MID, K_HALF = 0.5 * (K_LOW + K_TOP), 0.5 * (K_TOP - K_LOW)
LANES = 128
TERMS = 16
TWO_PI = 2.0 * math.pi


def fitted(function, count):
    angle = np.pi * (np.arange(200) + 0.5) / 200
    square = 0.125 * (1.0 + np.cos(angle))
    series = np.polynomial.chebyshev.Chebyshev.fit(
        square, function(np.sqrt(square)), count - 1, domain=[0.0, 0.25]
    )
    return [float(c) for c in series.convert(kind=np.polynomial.Polynomial).coef]


SINE = fitted(lambda x: np.sin(np.pi * x) / x, 5)
COSINE = fitted(lambda x: np.cos(np.pi * x), 5)


def horner(coefficients, x):
    value = coefficients[-1] * x + coefficients[-2]
    for c in coefficients[-3::-1]:
        value = value * x + c
    return value


def sincos_turns(turns):
    part = turns - jnp.floor(turns + 0.5)
    square = part * part
    s = horner(SINE, square) * part
    c = horner(COSINE, square)
    twice = s + s
    return 1.0 - twice * s, twice * c


def term_constants():
    nodes = np.cos(np.pi * (np.arange(TERMS) + 0.5) / TERMS)[: TERMS // 2]
    order = np.arange(TERMS)
    table = np.cos(order[:, None] * np.arccos(nodes)[None, :])
    table *= (np.where(order == 0, 1.0, 2.0) * 2.0 / TERMS)[:, None]
    half = TERMS // 2
    out = np.zeros((half, LANES), np.float32)
    out[:, 0] = K_HALF * nodes
    out[:, 1 : 1 + half] = table[0::2]
    out[:, 1 + half : 1 + 2 * half] = table[1::2]
    return out


def place_of(n):
    return n // 2 if n % 2 == 0 else TERMS // 2 + n // 2


def replica_kernel(
    shape,
    depths_ref,
    place_ref,
    ranges_ref,
    consts_ref,
    wave_ref,
    factor_ref,
    source_ref,
    recorded_ref,
    out_ref,
    sum_ref,
    weight_ref,
    term_ref,
    tab_ref,
    part_ref,
    psi_ref,
    coef_ref,
):
    bins, modes, depth_grid, sources, channels, samples, receivers = shape
    quarter = bins // 4
    span = samples // 4
    half = TERMS // 2
    first_x = place_ref[0]
    centre = place_ref[1]

    for first in range(0, bins, LANES):
        last = first + LANES - 1
        top = min(modes, MMIN + (modes - MMIN) * last // max(bins - 1, 1) + SPREAD)
        cols = slice(first, first + LANES)

        def modal(step, sums, cols=cols):
            start = pl.multiple_of(step * 8, 8)
            rows = pl.ds(start, 8)
            wave = wave_ref[rows, cols]
            cosine, sine = sincos_turns(wave * (centre * (1.0 / TWO_PI)))
            factor = factor_ref[rows, cols]
            weight_ref[0:8, :] = factor * cosine
            weight_ref[8:16, :] = factor * sine
            xi = (wave - K_MID) * (1.0 / K_HALF)
            before, now = jnp.ones_like(xi), xi
            for n in range(1, TERMS):
                term_ref[n * 8 : n * 8 + 8, :] = now
                before, now = now, 2.0 * xi * now - before
            sums = list(sums)
            for i in range(8):
                source = source_ref[jnp.minimum(start + i, modes - 1), :, cols].astype(jnp.float32)
                value = jnp.concatenate(
                    [source * weight_ref[i : i + 1, :], source * weight_ref[8 + i : 9 + i, :]], axis=0
                )
                sums[0] = sums[0] + value
                for n in range(1, TERMS):
                    sums[n] = sums[n] + value * term_ref[n * 8 + i : n * 8 + i + 1, :]
            return tuple(sums)

        zero = jnp.zeros((2 * depth_grid, LANES), jnp.float32)
        sums = lax.fori_loop(0, -(-top // 8), modal, (zero,) * TERMS)
        for n in range(TERMS):
            for z in range(depth_grid):
                for c in range(2):
                    at = z * 2 * TERMS + c * TERMS + place_of(n)
                    row = c * depth_grid + z
                    sum_ref[at : at + 1, cols] = sums[n][row : row + 1, :]

    def times_i(value):
        blocks = []
        for z in range(depth_grid):
            base = z * 2 * TERMS
            blocks.append(-value[base + TERMS : base + 2 * TERMS])
            blocks.append(value[base : base + TERMS])
        return jnp.concatenate(blocks, axis=0)

    moments = sum_ref[...]
    moments = jnp.concatenate([moments, -times_i(moments)], axis=0).astype(jnp.bfloat16)
    group = depth_grid * 2 * TERMS

    for r in range(4):
        row = lax.broadcasted_iota(jnp.int32, (quarter, LANES), 0)
        column = lax.broadcasted_iota(jnp.int32, (quarter, LANES), 1)
        number = F0 + 4 * row + r
        whole = (number * column) % samples
        cosine, sine = sincos_turns(whole.astype(jnp.float32) * (1.0 / samples))
        turn = (number * LANES) % samples
        step_c, step_s = sincos_turns(turn.astype(jnp.float32) * (1.0 / samples))
        for block in range(span // LANES):
            cols = slice(block * LANES, (block + 1) * LANES)
            tab_ref[:quarter, cols] = cosine.astype(jnp.bfloat16)
            tab_ref[quarter:, cols] = (-sine).astype(jnp.bfloat16)
            cosine, sine = cosine * step_c - sine * step_s, cosine * step_s + sine * step_c
        bin_row = lax.broadcasted_iota(jnp.int32, (bins, quarter), 0)
        bin_column = lax.broadcasted_iota(jnp.int32, (bins, quarter), 1)
        chosen = (bin_row == 4 * bin_column + r).astype(jnp.float32).astype(jnp.bfloat16)
        picked = jnp.dot(moments, chosen, preferred_element_type=jnp.float32)
        left = jnp.concatenate([picked[:group], picked[group:]], axis=1)
        part_ref[r] = jnp.dot(
            left.astype(jnp.bfloat16), tab_ref[...], preferred_element_type=jnp.float32
        )

    for block in range(span // LANES):
        cols = slice(block * LANES, (block + 1) * LANES)
        p0, p1, p2, p3 = (part_ref[r, :, cols] for r in range(4))
        even, odd = p0 + p2, p1 + p3
        gap, turned = p0 - p2, times_i(p1 - p3)
        for q, value in enumerate((even + odd, gap + turned, even - odd, gap - turned)):
            at = q * span + block * LANES
            psi_ref[:, at : at + LANES] = value.astype(jnp.bfloat16)

    channel = lax.broadcasted_iota(jnp.int32, (1, channels), 1).astype(jnp.float32)
    position = first_x + channel * (2.0 / receivers)
    spread = lax.rsqrt(position)
    nodes = consts_ref[:, 0:1]
    for s in range(sources):
        offset = position - (ranges_ref[s] + centre)
        cosine, sine = sincos_turns(nodes * offset * (1.0 / TWO_PI))
        even = jnp.zeros((half, channels), jnp.float32)
        odd = jnp.zeros((half, channels), jnp.float32)
        for j in range(half):
            even = even + consts_ref[:, 1 + j : 2 + j] * cosine[j : j + 1, :]
            odd = odd + consts_ref[:, 1 + half + j : 2 + half + j] * sine[j : j + 1, :]
        mid_c, mid_s = sincos_turns(offset * (K_MID / TWO_PI))
        mid_c, mid_s = mid_c * spread, mid_s * spread
        rows = jnp.concatenate([mid_c * even, -mid_s * odd, -mid_s * even, -mid_c * odd], axis=0)
        coef_ref[s] = rows.T.astype(jnp.bfloat16)

    chunk = 512

    def source(s, matched):
        z = depths_ref[s]
        terms = pl.ds(pl.multiple_of(z * (2 * TERMS), 2 * TERMS), 2 * TERMS)
        coef = coef_ref[s]
        total = jnp.zeros((channels, LANES), jnp.float32)
        for start in range(0, samples, chunk):
            series = jnp.dot(
                coef, psi_ref[terms, start : start + chunk], preferred_element_type=jnp.float32
            )
            product = jnp.tanh(series) * recorded_ref[:, start : start + chunk].astype(jnp.float32)
            for tile in range(chunk // LANES):
                total = total + product[:, tile * LANES : (tile + 1) * LANES]
        value = jnp.sum(total, axis=1, keepdims=True)
        lane = lax.broadcasted_iota(jnp.int32, (channels, LANES), 1)
        return jnp.where(lane % sources == s, value, matched)

    out_ref[...] = lax.fori_loop(
        0, sources, source, jnp.zeros((channels, LANES), jnp.float32)
    )


def exchange_kernel(sizes, block_ref, out_ref, held_ref, send_sem, recv_sem):
    freq_size, sub_size = sizes
    count = freq_size * sub_size
    me = lax.axis_index("freq") * sub_size + lax.axis_index("sub")
    barrier = pltpu.get_barrier_semaphore()

    def place(number):
        return {"freq": number // sub_size, "sub": number % sub_size}

    def greet(i, carry):
        pl.semaphore_signal(
            barrier,
            inc=1,
            device_id=place((me + i) % count),
            device_id_type=pl.DeviceIdType.MESH,
        )
        return carry

    lax.fori_loop(1, count, greet, 0)
    pl.semaphore_wait(barrier, count - 1)

    def copy_to(target, source):
        return pltpu.make_async_remote_copy(
            src_ref=block_ref.at[target],
            dst_ref=held_ref.at[source],
            send_sem=send_sem.at[target],
            recv_sem=recv_sem.at[source],
            device_id=place(target),
            device_id_type=pl.DeviceIdType.MESH,
        )

    def send(i, carry):
        copy_to((me + i) % count, me).start()
        return carry

    lax.fori_loop(1, count, send, 0)

    def receive(i, total):
        source = (me + count - i) % count
        copy_to(source, source).wait_recv()
        return total + held_ref[source]

    out_ref[...] = lax.fori_loop(1, count, receive, block_ref[me])

    def drain(i, carry):
        copy_to((me + i) % count, me).wait_send()
        return carry

    lax.fori_loop(1, count, drain, 0)

FAST_TERMS = 12
FAST_HALF = 8


def fast_constants():
    nodes = np.cos(np.pi * (np.arange(FAST_TERMS) + 0.5) / FAST_TERMS)[: FAST_TERMS // 2]
    order = np.arange(FAST_TERMS)
    table = np.cos(order[:, None] * np.arccos(nodes)[None, :])
    table *= (np.where(order == 0, 1.0, 2.0) * 2.0 / FAST_TERMS)[:, None]
    half = FAST_TERMS // 2
    out = np.zeros((FAST_HALF, LANES), np.float32)
    out[:half, 0] = K_HALF * nodes
    out[half, 0] = K_MID
    out[:half, 1 : 1 + half] = table[0::2]
    out[:half, 1 + half : 1 + 2 * half] = table[1::2]
    return out


def fast_place(n):
    return n // 2 if n % 2 == 0 else FAST_HALF + n // 2


def score_kernel(
    shape,
    depths_hbm,
    ranges_hbm,
    consts_hbm,
    sections_hbm,
    counts_hbm,
    wave_hbm,
    receiver_hbm,
    source_hbm,
    recorded_hbm,
    out_ref,
    depths_ref,
    ranges_ref,
    consts_ref,
    sections_ref,
    counts_ref,
    wave_ref,
    receiver_ref,
    source_ref,
    recorded_ref,
    flat_ref,
    left_ref,
    xi_ref,
    apart_ref,
    moment_ref,
    weights_ref,
    tab_ref,
    psi_ref,
    coef_ref,
    wave_t_ref,
    kept_ref,
    member_ref,
    block_ref,
    held_ref,
    load_sem,
    send_sem,
    recv_sem,
):
    bins, modes, depth_grid, sources, channels, samples, sizes = shape
    freq_size, sub_size = sizes
    count = freq_size * sub_size
    receivers = channels * count
    quarter = bins // 4
    span = samples // 4
    half = FAST_TERMS // 2
    group = depth_grid * 4 * FAST_HALF
    me = lax.axis_index("freq") * sub_size + lax.axis_index("sub")
    barrier = pltpu.get_barrier_semaphore()

    def top_of(last):
        return min(modes, MMIN + (modes - MMIN) * last // max(bins - 1, 1) + SPREAD)

    pairs = [
        (depths_hbm, depths_ref),
        (ranges_hbm, ranges_ref),
        (consts_hbm, consts_ref),
        (sections_hbm, sections_ref),
        (counts_hbm, counts_ref),
    ]
    for first in range(0, bins, LANES):
        cols = slice(first, first + LANES)
        rows = min(-(-top_of(first + LANES - 1) // 16) * 16, modes)
        pairs.append((wave_hbm.at[:rows, cols], wave_ref.at[:rows, cols]))
        pairs.append((receiver_hbm.at[:rows, cols], receiver_ref.at[:rows, cols]))
        pairs.append((source_hbm.at[:rows, :, cols], source_ref.at[:rows, :, cols]))
    pairs.append((recorded_hbm, recorded_ref))
    loads = [
        pltpu.make_async_copy(source, target, load_sem.at[i])
        for i, (source, target) in enumerate(pairs)
    ]
    for load in loads:
        load.start()

    my_freq = lax.axis_index("freq")
    my_sub = lax.axis_index("sub")
    partners = [(i, j) for i in range(1, freq_size) for j in range(sub_size)]
    partners += [(0, j) for j in range(1, sub_size)]

    def ahead(i, j):
        return lax.rem(my_freq + i, freq_size), lax.rem(my_sub + j, sub_size)

    reach = 2.0 * (channels - 1) / receivers
    first_x = 1.0 + (me * channels).astype(jnp.float32) * (2.0 / receivers)
    centre = first_x + 0.5 * (reach - R_TOP)

    lane = lax.broadcasted_iota(jnp.int32, (8, LANES), 1)
    row = lax.broadcasted_iota(jnp.int32, (8, LANES), 0)
    for r in range(4):
        number = F0 + 4 * lane + r
        whole = (number * row) % samples
        cosine, sine = sincos_turns(whole.astype(jnp.float32) * (1.0 / samples))
        turn = (number * 8) % samples
        step_c, step_s = sincos_turns(turn.astype(jnp.float32) * (1.0 / samples))
        for pair in range(span // 16):
            turned_c = cosine * step_c - sine * step_s
            turned_s = cosine * step_s + sine * step_c
            rows = slice(pair * 16, pair * 16 + 16)
            tab_ref[r, rows, :quarter] = jnp.concatenate([cosine, turned_c], axis=0).astype(jnp.bfloat16)
            tab_ref[r, rows, quarter:] = jnp.concatenate([sine, turned_s], axis=0).astype(jnp.bfloat16)
            cosine = turned_c * step_c - turned_s * step_s
            sine = turned_c * step_s + turned_s * step_c

    for load in loads[:5]:
        load.wait()

    channel = lax.broadcasted_iota(jnp.int32, (1, channels), 1).astype(jnp.float32)
    position = first_x + channel * (2.0 / receivers)
    spread = lax.rsqrt(position)
    for i, j in partners:
        freq, sub = ahead(i, j)
        pl.semaphore_signal(
            barrier,
            inc=1,
            device_id={"freq": freq, "sub": sub},
            device_id_type=pl.DeviceIdType.MESH,
        )

    nodes = consts_ref[:, 0:1]

    def coefficients(i):
        for s in range(4):
            number = i * 4 + s
            offset = position - (ranges_ref[number] + centre)
            cosine, sine = sincos_turns(nodes * offset * (1.0 / TWO_PI))
            even = jnp.zeros((FAST_HALF, channels), jnp.float32)
            odd = jnp.zeros((FAST_HALF, channels), jnp.float32)
            for j in range(half):
                even = even + consts_ref[:, 1 + j : 2 + j] * cosine[j : j + 1, :]
                odd = odd + consts_ref[:, 1 + half + j : 2 + half + j] * sine[j : j + 1, :]
            mid_c, mid_s = cosine[half : half + 1, :] * spread, sine[half : half + 1, :] * spread
            parts = jnp.concatenate([mid_c * even, -mid_s * odd, -mid_s * even, -mid_c * odd], axis=0)
            for z in range(depth_grid):
                here = jnp.where(depths_ref[number] == z, 1.0, 0.0)
                rows = slice(z * 4 * FAST_HALF, (z + 1) * 4 * FAST_HALF)
                cols = slice(s * channels, (s + 1) * channels)
                coef_ref[i, rows, cols] = (parts * here).astype(jnp.bfloat16)

    coefficients(0)

    def filled(value, rows):
        lack = rows - value.shape[0]
        if lack == 0:
            return value
        return jnp.concatenate([value, jnp.zeros((lack, value.shape[1]), value.dtype)], axis=0)

    for block, first in enumerate(range(0, bins, LANES)):
        for load in loads[5 + 3 * block : 8 + 3 * block]:
            load.wait()
        cols = slice(first, first + LANES)
        deep = -(-top_of(first + LANES - 1) // LANES) * LANES
        rows = min(-(-top_of(first + LANES - 1) // 16) * 16, modes)
        whole = -(-rows // 16) * 16
        wave = wave_ref[:rows, cols]
        cosine, sine = sincos_turns(wave * (centre * (1.0 / TWO_PI)))
        index = lax.broadcasted_iota(jnp.int32, (rows, LANES), 0)
        factor = receiver_ref[:rows, cols].astype(jnp.float32) * (8.0 / math.sqrt(bins * modes))
        factor = jnp.where(index < counts_ref[:, cols], factor * lax.rsqrt(wave), 0.0)
        xi = (wave - K_MID) * (1.0 / K_HALF)
        xi_ref[cols, :deep] = filled(filled(xi, whole), deep).T
        weights = (factor * cosine, factor * sine)
        base = block * modes * depth_grid
        flat_ref[base : base + rows * depth_grid, :] = (
            source_ref[:rows, :, cols].astype(jnp.float32).reshape(rows * depth_grid, LANES)
        )
        for z in range(depth_grid):
            source = flat_ref[pl.ds(base + z, rows, stride=depth_grid), :]
            for c in range(2):
                value = filled(source * weights[c], whole).astype(jnp.bfloat16)
                left_ref[z * 2 + c, cols, :deep] = filled(value, deep).T

    loads[-1].wait()
    for block in range(samples // LANES):
        rows = slice(block * LANES, (block + 1) * LANES)
        wave_t_ref[rows, :] = recorded_ref[:, rows].T

    across = (((1,), (1,)), ((), ()))
    terms = 2 * FAST_HALF
    kinds = 2 * depth_grid
    same_bin = (
        lax.broadcasted_iota(jnp.int32, (16, terms * 16), 0)
        == lax.broadcasted_iota(jnp.int32, (16, terms * 16), 1) % 16
    )
    for g in range(bins // 16):
        rows = slice(g * 16, g * 16 + 16)
        deep = -(-top_of(g * 16 + 15) // LANES) * LANES
        xi = xi_ref[rows, :deep]
        double = xi + xi
        before, now = jnp.ones_like(xi), xi
        right = [before.astype(jnp.bfloat16)]
        for n in range(1, FAST_TERMS):
            right.append(now.astype(jnp.bfloat16))
            before, now = now, double * now - before
        right = right + [jnp.zeros_like(right[0])] * (terms - FAST_TERMS)
        left = jnp.concatenate([left_ref[k, rows, :deep] for k in range(kinds)], axis=0)
        pairs = lax.dot_general(
            left, jnp.concatenate(right, axis=0), across, preferred_element_type=jnp.float32
        )
        for k in range(kinds):
            value = jnp.where(same_bin, pairs[k * 16 : k * 16 + 16], 0.0)
            apart_ref[rows, k * terms * 16 : (k + 1) * terms * 16] = value.astype(jnp.bfloat16)

    term = lax.broadcasted_iota(jnp.int32, (terms * 16, group), 0) // 16
    column = lax.broadcasted_iota(jnp.int32, (terms * 16, group), 1)
    column = column - (term // 2 + FAST_HALF * (term % 2))
    column = jnp.where(term < FAST_TERMS, column, -1)
    gathers = []
    for k in range(kinds):
        z, c = k // 2, k % 2
        plain = jnp.where(column == k * terms, 1.0, 0.0)
        turned = jnp.where(column == (z * 2 + 1 - c) * terms, 1.0 - 2.0 * c, 0.0)
        gathers.append(jnp.concatenate([plain, turned], axis=1).astype(jnp.bfloat16))
    gather = jnp.concatenate(gathers, axis=0)
    middle = bins // 2
    moments = jnp.concatenate(
        [
            jnp.dot(apart_ref[:middle, :], gather, preferred_element_type=jnp.float32),
            jnp.dot(apart_ref[middle:, :], gather, preferred_element_type=jnp.float32),
        ],
        axis=0,
    )
    moment_ref[:bins, :] = moments[:, :group]
    moment_ref[bins:, :] = moments[:, group:]
    weights = []
    for r in range(4):
        plain = moment_ref[pl.ds(r, quarter, stride=4), :].astype(jnp.bfloat16)
        turned = moment_ref[pl.ds(bins + r, quarter, stride=4), :].astype(jnp.bfloat16)
        weight = jnp.concatenate([plain, turned], axis=0)
        if r % 2:
            weight = jnp.concatenate([weight, jnp.concatenate([turned, -plain], axis=0)], axis=1)
        weights.append(weight)
    piece = 512
    for r in range(4):
        sides = weights[r].shape[1]
        weights_ref[r, :, :sides] = weights[r]

    def transform(i, carry):
        start = pl.multiple_of(i * piece, piece)
        rows = pl.ds(start, piece)
        p0, p1, p2, p3 = (
            jnp.dot(
                tab_ref[r, rows, :],
                weights_ref[r, :, : group * (1 + r % 2)],
                preferred_element_type=jnp.float32,
            )
            for r in range(4)
        )
        odd, turned = p1[:, :group] + p3[:, :group], p1[:, group:] - p3[:, group:]
        even, gap = p0 + p2, p0 - p2
        for q, value in enumerate((even + odd, gap + turned, even - odd, gap - turned)):
            psi_ref[pl.ds(q * span + start, piece), :] = value.astype(jnp.bfloat16)
        return carry

    lax.fori_loop(0, span // piece, transform, 0)

    section_row = sections_ref[...]
    lane_in_row = section_row % 8
    own_rows = receivers // 4 // count // 8
    slots = lax.broadcasted_iota(jnp.int32, (count * own_rows, channels), 0)
    member_ref[...] = (slots == section_row // 8).astype(jnp.float32).astype(jnp.bfloat16)

    def quad(i, carry):
        series = jnp.dot(psi_ref[...], coef_ref[i], preferred_element_type=jnp.float32)
        waveform = wave_t_ref[...].astype(jnp.float32)
        slot = lax.broadcasted_iota(jnp.int32, (8, channels), 0)
        for s in range(4):
            product = jnp.tanh(series[:, s * channels : (s + 1) * channels]) * waveform
            total = jnp.sum(product.reshape(samples // 8, 8, channels), axis=0)
            for shift in (4, 2, 1):
                total = total + pltpu.roll(total, shift, 0)
            rows = pl.ds((sources - 1 - s - 4 * i) * 8, 8)
            kept_ref[rows, :] = jnp.where(slot == lane_in_row, total, 0.0)
        if i + 1 < sources // 4:
            coefficients(i + 1)
        return carry

    for i in range(sources // 4):
        quad(i, 0)

    member = member_ref[...]
    kept = kept_ref[...] * (1.0 / math.sqrt(samples * 4))
    high = kept.astype(jnp.bfloat16)
    low = (kept - high.astype(jnp.float32)).astype(jnp.bfloat16)
    blocks = lax.dot_general(
        jnp.concatenate([member, member], axis=1),
        jnp.concatenate([high, low], axis=1),
        across,
        preferred_element_type=jnp.float32,
    )
    for target in range(count):
        block_ref[target] = blocks[target * own_rows : (target + 1) * own_rows]

    pl.semaphore_wait(barrier, count - 1)

    def copy_to(freq, sub, slot, source):
        return pltpu.make_async_remote_copy(
            src_ref=block_ref.at[freq * sub_size + sub],
            dst_ref=held_ref.at[source],
            send_sem=send_sem.at[slot],
            recv_sem=recv_sem.at[source],
            device_id={"freq": freq, "sub": sub},
            device_id_type=pl.DeviceIdType.MESH,
        )

    sends = []
    for slot, (i, j) in enumerate(partners):
        freq, sub = ahead(i, j)
        sends.append(copy_to(freq, sub, slot, me))
        sends[-1].start()
    total = block_ref[me]
    for slot, (i, j) in enumerate(partners):
        freq, sub = ahead(freq_size - i, sub_size - j)
        source = freq * sub_size + sub
        copy_to(freq, sub, slot, source).wait_recv()
        total = total + held_ref[source]

    halves = [jnp.zeros((8, LANES), jnp.float32)] * (sources // 8)
    for r in range(own_rows):
        spread_row = jnp.broadcast_to(total[r : r + 1, :], (8, LANES))
        moved = pltpu.roll(spread_row, 0, 1, stride=8, stride_axis=0)
        for h in range(sources // 8):
            placed = pltpu.roll(moved, (8 * r + 8 + 64 * h) % LANES, 1)
            halves[h] = jnp.where(lane // 8 == r, placed, halves[h])
    out_ref[...] = jnp.concatenate(halves, axis=0)[:, : own_rows * 8]

    for send in sends:
        send.wait_send()


def fast_fits(mesh_sizes, wavenumbers, source_shapes, source_depths, recorded):
    count = mesh_sizes[0] * mesh_sizes[1]
    bins = wavenumbers.shape[0]
    channels, samples = recorded.shape
    own = channels // 4
    return (
        channels == LANES
        and source_depths.shape[0] * 8 == LANES
        and source_shapes.shape[1] * 4 * FAST_HALF == LANES
        and bins == 4 * LANES
        and samples % (4 * LANES) == 0
        and own % 8 == 0
        and own // 8 <= 8
        and count * (own // 8) % 16 == 0
    )


def per_device(
    mesh_sizes,
    wavenumbers,
    receiver_shapes,
    source_shapes,
    mode_counts,
    source_depths,
    source_ranges,
    sections,
    recorded,
):
    args = (
        wavenumbers,
        receiver_shapes,
        source_shapes,
        mode_counts,
        source_depths,
        source_ranges,
        sections,
        recorded,
    )
    if not fast_fits(mesh_sizes, wavenumbers, source_shapes, source_depths, recorded):
        return per_device_general(mesh_sizes, *args)
    freq_size, sub_size = mesh_sizes
    count = freq_size * sub_size
    bins, modes = wavenumbers.shape
    depth_grid = source_shapes.shape[1]
    sources = source_depths.shape[0]
    channels, samples = recorded.shape
    receivers = channels * count
    reach = 2.0 * (channels - 1) / receivers
    top_phase = K_HALF * 0.5 * (reach + R_TOP)
    assert 2.0 * (0.5 * top_phase) ** FAST_TERMS / math.factorial(FAST_TERMS) < 1e-6

    shape = (bins, modes, depth_grid, sources, channels, samples, mesh_sizes)
    group = depth_grid * 4 * FAST_HALF
    deep = -(-modes // LANES) * LANES
    own = channels // 4
    return pl.pallas_call(
        functools.partial(score_kernel, shape),
        out_shape=pltpu.VMEM((sources, own), jnp.float32),
        in_specs=[pl.BlockSpec(memory_space=pl.ANY)] * 9,
        out_specs=pl.BlockSpec(memory_space=pltpu.VMEM),
        scratch_shapes=[
            pltpu.SMEM((sources,), jnp.int32),
            pltpu.SMEM((sources,), jnp.float32),
            pltpu.VMEM((FAST_HALF, LANES), jnp.float32),
            pltpu.VMEM((1, channels), jnp.int32),
            pltpu.VMEM((1, bins), jnp.int32),
            pltpu.VMEM((modes, bins), jnp.float32),
            pltpu.VMEM((modes, bins), jnp.bfloat16),
            pltpu.VMEM((modes, depth_grid, bins), jnp.bfloat16),
            pltpu.VMEM((channels, samples), jnp.bfloat16),
            pltpu.VMEM((bins // LANES * modes * depth_grid, LANES), jnp.float32),
            pltpu.VMEM((2 * depth_grid, bins, deep), jnp.bfloat16),
            pltpu.VMEM((bins, deep), jnp.float32),
            pltpu.VMEM((bins, group * 2 * FAST_HALF), jnp.bfloat16),
            pltpu.VMEM((2 * bins, group), jnp.float32),
            pltpu.VMEM((4, bins // 2, 2 * group), jnp.bfloat16),
            pltpu.VMEM((4, samples // 4, bins // 2), jnp.bfloat16),
            pltpu.VMEM((samples, group), jnp.bfloat16),
            pltpu.VMEM((sources // 4 + 1, group, 4 * channels), jnp.bfloat16),
            pltpu.VMEM((samples, channels), jnp.bfloat16),
            pltpu.VMEM((sources * 8, channels), jnp.float32),
            pltpu.VMEM((count * (own // 8), channels), jnp.bfloat16),
            pltpu.VMEM((count, own // 8, LANES), jnp.float32),
            pltpu.VMEM((count, own // 8, LANES), jnp.float32),
            pltpu.SemaphoreType.DMA((6 + 3 * bins // LANES,)),
            pltpu.SemaphoreType.DMA((count - 1,)),
            pltpu.SemaphoreType.DMA((count,)),
        ],
        compiler_params=pltpu.CompilerParams(
            vmem_limit_bytes=60 * 1024 * 1024, collective_id=1, has_side_effects=True
        ),
        name="score",
    )(
        source_depths,
        source_ranges,
        jnp.asarray(fast_constants()),
        sections.reshape(1, channels),
        mode_counts.reshape(1, bins),
        wavenumbers.T,
        receiver_shapes.T,
        source_shapes.transpose(2, 1, 0),
        recorded,
    )


def per_device_general(
    mesh_sizes,
    wavenumbers,
    receiver_shapes,
    source_shapes,
    mode_counts,
    source_depths,
    source_ranges,
    sections,
    recorded,
):
    freq_size, sub_size = mesh_sizes
    count = freq_size * sub_size
    me = lax.axis_index("freq") * sub_size + lax.axis_index("sub")
    bins, modes = wavenumbers.shape
    depth_grid = source_shapes.shape[1]
    sources = source_depths.shape[0]
    channels, samples = recorded.shape
    receivers = channels * count

    first_x = 1.0 + 2.0 * (me * channels).astype(jnp.float32) / receivers
    reach = 2.0 * (channels - 1) / receivers
    centre = first_x + 0.5 * (reach - R_TOP)
    top_phase = K_HALF * 0.5 * (reach + R_TOP)
    assert 2.0 * (0.5 * top_phase) ** TERMS / math.factorial(TERMS) < 1e-9
    assert depth_grid * 2 * TERMS <= LANES

    extra = -modes % 8
    wave = wavenumbers.T
    live = jnp.arange(modes, dtype=jnp.int32)[:, None] < mode_counts[None, :]
    factor = receiver_shapes.T.astype(jnp.float32) * (8.0 / math.sqrt(bins))
    factor = jnp.where(live, factor / jnp.sqrt(wave * modes), 0.0)
    factor = jnp.pad(factor, ((0, extra), (0, 0)))
    wave = jnp.pad(wave, ((0, extra), (0, 0)), constant_values=K_MID)
    shape = (bins, modes, depth_grid, sources, channels, samples, receivers)
    matched = pl.pallas_call(
        functools.partial(replica_kernel, shape),
        out_shape=jax.ShapeDtypeStruct((channels, LANES), jnp.float32),
        in_specs=[pl.BlockSpec(memory_space=pltpu.SMEM)] * 3
        + [pl.BlockSpec(memory_space=pltpu.VMEM)] * 5,
        out_specs=pl.BlockSpec(memory_space=pltpu.VMEM),
        scratch_shapes=[
            pltpu.VMEM((depth_grid * 2 * TERMS, bins), jnp.float32),
            pltpu.VMEM((16, LANES), jnp.float32),
            pltpu.VMEM((TERMS * 8, LANES), jnp.float32),
            pltpu.VMEM((bins // 2, samples // 4), jnp.bfloat16),
            pltpu.VMEM((4, depth_grid * 2 * TERMS, samples // 4), jnp.float32),
            pltpu.VMEM((depth_grid * 2 * TERMS, samples), jnp.bfloat16),
            pltpu.VMEM((sources, channels, 2 * TERMS), jnp.bfloat16),
        ],
        compiler_params=pltpu.CompilerParams(vmem_limit_bytes=48 * 1024 * 1024),
        name="replica",
    )(
        source_depths,
        jnp.stack([first_x, centre]),
        source_ranges,
        jnp.asarray(term_constants()),
        wave,
        factor,
        source_shapes.transpose(2, 1, 0),
        recorded,
    )

    section_count = receivers // 4
    own = section_count // count
    per_row = min(LANES // sources, own)
    own_rows = own // per_row
    assert LANES % sources == 0 and own % per_row == 0
    padded = -(-own_rows // 8) * 8
    slot = jnp.arange(count * padded, dtype=jnp.int32)
    wanted = jnp.where(
        slot % padded < own_rows, slot // padded * own_rows + slot % padded, -1
    )
    member = (wanted[:, None] == (sections // per_row)[None, :]).astype(jnp.float32)
    lane_part = jnp.arange(LANES, dtype=jnp.int32) // sources
    kept = jnp.where((sections % per_row)[:, None] == lane_part[None, :], matched, 0.0)
    blocks = jnp.dot(member, kept, precision=lax.Precision.HIGHEST) * (
        1.0 / math.sqrt(samples * (receivers // section_count))
    )
    blocks = blocks.reshape(count, padded, LANES)
    total = pl.pallas_call(
        functools.partial(exchange_kernel, (freq_size, sub_size)),
        out_shape=jax.ShapeDtypeStruct((padded, LANES), jnp.float32),
        in_specs=[pl.BlockSpec(memory_space=pltpu.VMEM)],
        out_specs=pl.BlockSpec(memory_space=pltpu.VMEM),
        scratch_shapes=[
            pltpu.VMEM((count, padded, LANES), jnp.float32),
            pltpu.SemaphoreType.DMA((count,)),
            pltpu.SemaphoreType.DMA((count,)),
        ],
        compiler_params=pltpu.CompilerParams(collective_id=0, has_side_effects=True),
        name="exchange",
    )(blocks)
    total = total[:own_rows, : per_row * sources].reshape(own_rows, per_row, sources)
    return total.transpose(2, 0, 1).reshape(sources, own)


def solution(mesh):
    sizes = (mesh.shape["freq"], mesh.shape["sub"])
    in_specs = (
        P(),
        P(),
        P(),
        P(),
        P("groups"),
        P("groups"),
        P(("freq", "sub")),
        P(("freq", "sub"), None),
    )
    out_specs = P("groups", ("freq", "sub"))
    return jax.shard_map(
        functools.partial(per_device, sizes),
        mesh=mesh,
        in_specs=in_specs,
        out_specs=out_specs,
        check_vma=False,
    )
```

```python
import functools
import math

import jax
import jax.numpy as jnp
import numpy as np
from jax import lax
from jax.experimental import pallas as pl
from jax.experimental.pallas import tpu as pltpu
from jax.sharding import PartitionSpec as P

MMIN = 64
F0 = 256
SPREAD = 16
K_LOW, K_TOP = 1.0, 20.0
R_TOP = 0.5
K_MID, K_HALF = 0.5 * (K_LOW + K_TOP), 0.5 * (K_TOP - K_LOW)
LANES = 128
TERMS = 16
TWO_PI = 2.0 * math.pi


def fitted(function, count):
    angle = np.pi * (np.arange(200) + 0.5) / 200
    square = 0.125 * (1.0 + np.cos(angle))
    series = np.polynomial.chebyshev.Chebyshev.fit(
        square, function(np.sqrt(square)), count - 1, domain=[0.0, 0.25]
    )
    return [float(c) for c in series.convert(kind=np.polynomial.Polynomial).coef]


SINE = fitted(lambda x: np.sin(np.pi * x) / x, 5)
COSINE = fitted(lambda x: np.cos(np.pi * x), 5)


def horner(coefficients, x):
    value = coefficients[-1] * x + coefficients[-2]
    for c in coefficients[-3::-1]:
        value = value * x + c
    return value


def sincos_turns(turns):
    part = turns - jnp.floor(turns + 0.5)
    square = part * part
    s = horner(SINE, square) * part
    c = horner(COSINE, square)
    twice = s + s
    return 1.0 - twice * s, twice * c


def term_constants():
    nodes = np.cos(np.pi * (np.arange(TERMS) + 0.5) / TERMS)[: TERMS // 2]
    order = np.arange(TERMS)
    table = np.cos(order[:, None] * np.arccos(nodes)[None, :])
    table *= (np.where(order == 0, 1.0, 2.0) * 2.0 / TERMS)[:, None]
    half = TERMS // 2
    out = np.zeros((half, LANES), np.float32)
    out[:, 0] = K_HALF * nodes
    out[:, 1 : 1 + half] = table[0::2]
    out[:, 1 + half : 1 + 2 * half] = table[1::2]
    return out


def place_of(n):
    return n // 2 if n % 2 == 0 else TERMS // 2 + n // 2


def replica_kernel(
    shape,
    depths_ref,
    place_ref,
    ranges_ref,
    consts_ref,
    wave_ref,
    factor_ref,
    source_ref,
    recorded_ref,
    out_ref,
    sum_ref,
    weight_ref,
    term_ref,
    tab_ref,
    part_ref,
    psi_ref,
    coef_ref,
):
    bins, modes, depth_grid, sources, channels, samples, receivers = shape
    quarter = bins // 4
    span = samples // 4
    half = TERMS // 2
    first_x = place_ref[0]
    centre = place_ref[1]

    for first in range(0, bins, LANES):
        last = first + LANES - 1
        top = min(modes, MMIN + (modes - MMIN) * last // max(bins - 1, 1) + SPREAD)
        cols = slice(first, first + LANES)

        def modal(step, sums, cols=cols):
            start = pl.multiple_of(step * 8, 8)
            rows = pl.ds(start, 8)
            wave = wave_ref[rows, cols]
            cosine, sine = sincos_turns(wave * (centre * (1.0 / TWO_PI)))
            factor = factor_ref[rows, cols]
            weight_ref[0:8, :] = factor * cosine
            weight_ref[8:16, :] = factor * sine
            xi = (wave - K_MID) * (1.0 / K_HALF)
            before, now = jnp.ones_like(xi), xi
            for n in range(1, TERMS):
                term_ref[n * 8 : n * 8 + 8, :] = now
                before, now = now, 2.0 * xi * now - before
            sums = list(sums)
            for i in range(8):
                source = source_ref[jnp.minimum(start + i, modes - 1), :, cols].astype(jnp.float32)
                value = jnp.concatenate(
                    [source * weight_ref[i : i + 1, :], source * weight_ref[8 + i : 9 + i, :]], axis=0
                )
                sums[0] = sums[0] + value
                for n in range(1, TERMS):
                    sums[n] = sums[n] + value * term_ref[n * 8 + i : n * 8 + i + 1, :]
            return tuple(sums)

        zero = jnp.zeros((2 * depth_grid, LANES), jnp.float32)
        sums = lax.fori_loop(0, -(-top // 8), modal, (zero,) * TERMS)
        for n in range(TERMS):
            for z in range(depth_grid):
                for c in range(2):
                    at = z * 2 * TERMS + c * TERMS + place_of(n)
                    row = c * depth_grid + z
                    sum_ref[at : at + 1, cols] = sums[n][row : row + 1, :]

    def times_i(value):
        blocks = []
        for z in range(depth_grid):
            base = z * 2 * TERMS
            blocks.append(-value[base + TERMS : base + 2 * TERMS])
            blocks.append(value[base : base + TERMS])
        return jnp.concatenate(blocks, axis=0)

    moments = sum_ref[...]
    moments = jnp.concatenate([moments, -times_i(moments)], axis=0).astype(jnp.bfloat16)
    group = depth_grid * 2 * TERMS

    for r in range(4):
        row = lax.broadcasted_iota(jnp.int32, (quarter, LANES), 0)
        column = lax.broadcasted_iota(jnp.int32, (quarter, LANES), 1)
        number = F0 + 4 * row + r
        whole = (number * column) % samples
        cosine, sine = sincos_turns(whole.astype(jnp.float32) * (1.0 / samples))
        turn = (number * LANES) % samples
        step_c, step_s = sincos_turns(turn.astype(jnp.float32) * (1.0 / samples))
        for block in range(span // LANES):
            cols = slice(block * LANES, (block + 1) * LANES)
            tab_ref[:quarter, cols] = cosine.astype(jnp.bfloat16)
            tab_ref[quarter:, cols] = (-sine).astype(jnp.bfloat16)
            cosine, sine = cosine * step_c - sine * step_s, cosine * step_s + sine * step_c
        bin_row = lax.broadcasted_iota(jnp.int32, (bins, quarter), 0)
        bin_column = lax.broadcasted_iota(jnp.int32, (bins, quarter), 1)
        chosen = (bin_row == 4 * bin_column + r).astype(jnp.float32).astype(jnp.bfloat16)
        picked = jnp.dot(moments, chosen, preferred_element_type=jnp.float32)
        left = jnp.concatenate([picked[:group], picked[group:]], axis=1)
        part_ref[r] = jnp.dot(
            left.astype(jnp.bfloat16), tab_ref[...], preferred_element_type=jnp.float32
        )

    for block in range(span // LANES):
        cols = slice(block * LANES, (block + 1) * LANES)
        p0, p1, p2, p3 = (part_ref[r, :, cols] for r in range(4))
        even, odd = p0 + p2, p1 + p3
        gap, turned = p0 - p2, times_i(p1 - p3)
        for q, value in enumerate((even + odd, gap + turned, even - odd, gap - turned)):
            at = q * span + block * LANES
            psi_ref[:, at : at + LANES] = value.astype(jnp.bfloat16)

    channel = lax.broadcasted_iota(jnp.int32, (1, channels), 1).astype(jnp.float32)
    position = first_x + channel * (2.0 / receivers)
    spread = lax.rsqrt(position)
    nodes = consts_ref[:, 0:1]
    for s in range(sources):
        offset = position - (ranges_ref[s] + centre)
        cosine, sine = sincos_turns(nodes * offset * (1.0 / TWO_PI))
        even = jnp.zeros((half, channels), jnp.float32)
        odd = jnp.zeros((half, channels), jnp.float32)
        for j in range(half):
            even = even + consts_ref[:, 1 + j : 2 + j] * cosine[j : j + 1, :]
            odd = odd + consts_ref[:, 1 + half + j : 2 + half + j] * sine[j : j + 1, :]
        mid_c, mid_s = sincos_turns(offset * (K_MID / TWO_PI))
        mid_c, mid_s = mid_c * spread, mid_s * spread
        rows = jnp.concatenate([mid_c * even, -mid_s * odd, -mid_s * even, -mid_c * odd], axis=0)
        coef_ref[s] = rows.T.astype(jnp.bfloat16)

    chunk = 512

    def source(s, matched):
        z = depths_ref[s]
        terms = pl.ds(pl.multiple_of(z * (2 * TERMS), 2 * TERMS), 2 * TERMS)
        coef = coef_ref[s]
        total = jnp.zeros((channels, LANES), jnp.float32)
        for start in range(0, samples, chunk):
            series = jnp.dot(
                coef, psi_ref[terms, start : start + chunk], preferred_element_type=jnp.float32
            )
            product = jnp.tanh(series) * recorded_ref[:, start : start + chunk].astype(jnp.float32)
            for tile in range(chunk // LANES):
                total = total + product[:, tile * LANES : (tile + 1) * LANES]
        value = jnp.sum(total, axis=1, keepdims=True)
        lane = lax.broadcasted_iota(jnp.int32, (channels, LANES), 1)
        return jnp.where(lane % sources == s, value, matched)

    out_ref[...] = lax.fori_loop(
        0, sources, source, jnp.zeros((channels, LANES), jnp.float32)
    )


def exchange_kernel(sizes, block_ref, out_ref, held_ref, send_sem, recv_sem):
    freq_size, sub_size = sizes
    count = freq_size * sub_size
    me = lax.axis_index("freq") * sub_size + lax.axis_index("sub")
    barrier = pltpu.get_barrier_semaphore()

    def place(number):
        return {"freq": number // sub_size, "sub": number % sub_size}

    def greet(i, carry):
        pl.semaphore_signal(
            barrier,
            inc=1,
            device_id=place((me + i) % count),
            device_id_type=pl.DeviceIdType.MESH,
        )
        return carry

    lax.fori_loop(1, count, greet, 0)
    pl.semaphore_wait(barrier, count - 1)

    def copy_to(target, source):
        return pltpu.make_async_remote_copy(
            src_ref=block_ref.at[target],
            dst_ref=held_ref.at[source],
            send_sem=send_sem.at[target],
            recv_sem=recv_sem.at[source],
            device_id=place(target),
            device_id_type=pl.DeviceIdType.MESH,
        )

    def send(i, carry):
        copy_to((me + i) % count, me).start()
        return carry

    lax.fori_loop(1, count, send, 0)

    def receive(i, total):
        source = (me + count - i) % count
        copy_to(source, source).wait_recv()
        return total + held_ref[source]

    out_ref[...] = lax.fori_loop(1, count, receive, block_ref[me])

    def drain(i, carry):
        copy_to((me + i) % count, me).wait_send()
        return carry

    lax.fori_loop(1, count, drain, 0)

FAST_TERMS = 12
FAST_HALF = 8


def fast_constants():
    nodes = np.cos(np.pi * (np.arange(FAST_TERMS) + 0.5) / FAST_TERMS)[: FAST_TERMS // 2]
    order = np.arange(FAST_TERMS)
    table = np.cos(order[:, None] * np.arccos(nodes)[None, :])
    table *= (np.where(order == 0, 1.0, 2.0) * 2.0 / FAST_TERMS)[:, None]
    half = FAST_TERMS // 2
    out = np.zeros((FAST_HALF, LANES), np.float32)
    out[:half, 0] = K_HALF * nodes
    out[half, 0] = K_MID
    out[:half, 1 : 1 + half] = table[0::2]
    out[:half, 1 + half : 1 + 2 * half] = table[1::2]
    return out


def fast_place(n):
    return n // 2 if n % 2 == 0 else FAST_HALF + n // 2


def score_kernel(
    shape,
    depths_hbm,
    ranges_hbm,
    consts_hbm,
    sections_hbm,
    counts_hbm,
    wave_hbm,
    receiver_hbm,
    source_hbm,
    recorded_hbm,
    out_ref,
    depths_ref,
    ranges_ref,
    consts_ref,
    sections_ref,
    counts_ref,
    wave_ref,
    receiver_ref,
    source_ref,
    recorded_ref,
    flat_ref,
    left_ref,
    xi_ref,
    apart_ref,
    moment_ref,
    weights_ref,
    tab_ref,
    psi_ref,
    coef_ref,
    wave_t_ref,
    kept_ref,
    member_ref,
    block_ref,
    held_ref,
    load_sem,
    send_sem,
    recv_sem,
):
    bins, modes, depth_grid, sources, channels, samples, sizes = shape
    freq_size, sub_size = sizes
    count = freq_size * sub_size
    receivers = channels * count
    quarter = bins // 4
    span = samples // 4
    half = FAST_TERMS // 2
    group = depth_grid * 4 * FAST_HALF
    me = lax.axis_index("freq") * sub_size + lax.axis_index("sub")
    barrier = pltpu.get_barrier_semaphore()

    def top_of(last):
        return min(modes, MMIN + (modes - MMIN) * last // max(bins - 1, 1) + SPREAD)

    pairs = [
        (depths_hbm, depths_ref),
        (ranges_hbm, ranges_ref),
        (consts_hbm, consts_ref),
        (sections_hbm, sections_ref),
        (counts_hbm, counts_ref),
    ]
    for first in range(0, bins, LANES):
        cols = slice(first, first + LANES)
        rows = min(-(-top_of(first + LANES - 1) // 16) * 16, modes)
        pairs.append((wave_hbm.at[:rows, cols], wave_ref.at[:rows, cols]))
        pairs.append((receiver_hbm.at[:rows, cols], receiver_ref.at[:rows, cols]))
        pairs.append((source_hbm.at[:rows, :, cols], source_ref.at[:rows, :, cols]))
    pairs.append((recorded_hbm, recorded_ref))
    loads = [
        pltpu.make_async_copy(source, target, load_sem.at[i])
        for i, (source, target) in enumerate(pairs)
    ]
    for load in loads:
        load.start()

    my_freq = lax.axis_index("freq")
    my_sub = lax.axis_index("sub")
    partners = [(i, j) for i in range(1, freq_size) for j in range(sub_size)]
    partners += [(0, j) for j in range(1, sub_size)]

    def ahead(i, j):
        return lax.rem(my_freq + i, freq_size), lax.rem(my_sub + j, sub_size)

    reach = 2.0 * (channels - 1) / receivers
    first_x = 1.0 + (me * channels).astype(jnp.float32) * (2.0 / receivers)
    centre = first_x + 0.5 * (reach - R_TOP)

    lane = lax.broadcasted_iota(jnp.int32, (8, LANES), 1)
    row = lax.broadcasted_iota(jnp.int32, (8, LANES), 0)
    starts, steps = [], []
    for r in range(4):
        number = F0 + 4 * lane + r
        whole = (number * row) % samples
        starts.append(sincos_turns(whole.astype(jnp.float32) * (1.0 / samples)))
        turn = (number * 8) % samples
        steps.append(sincos_turns(turn.astype(jnp.float32) * (1.0 / samples)))
    for pair in range(span // 16):
        rows = slice(pair * 16, pair * 16 + 16)
        for r in range(4):
            (cosine, sine), (step_c, step_s) = starts[r], steps[r]
            turned_c = cosine * step_c - sine * step_s
            turned_s = cosine * step_s + sine * step_c
            tab_ref[r, rows, :quarter] = jnp.concatenate([cosine, turned_c], axis=0).astype(jnp.bfloat16)
            tab_ref[r, rows, quarter:] = jnp.concatenate([sine, turned_s], axis=0).astype(jnp.bfloat16)
            starts[r] = (
                turned_c * step_c - turned_s * step_s,
                turned_c * step_s + turned_s * step_c,
            )

    for load in loads[:5]:
        load.wait()

    channel = lax.broadcasted_iota(jnp.int32, (1, channels), 1).astype(jnp.float32)
    position = first_x + channel * (2.0 / receivers)
    spread = lax.rsqrt(position)
    for i, j in partners:
        freq, sub = ahead(i, j)
        pl.semaphore_signal(
            barrier,
            inc=1,
            device_id={"freq": freq, "sub": sub},
            device_id_type=pl.DeviceIdType.MESH,
        )

    nodes = consts_ref[:, 0:1]

    def coefficients(i):
        for s in range(4):
            number = i * 4 + s
            offset = position - (ranges_ref[number] + centre)
            cosine, sine = sincos_turns(nodes * offset * (1.0 / TWO_PI))
            even = jnp.zeros((FAST_HALF, channels), jnp.float32)
            odd = jnp.zeros((FAST_HALF, channels), jnp.float32)
            for j in range(half):
                even = even + consts_ref[:, 1 + j : 2 + j] * cosine[j : j + 1, :]
                odd = odd + consts_ref[:, 1 + half + j : 2 + half + j] * sine[j : j + 1, :]
            mid_c, mid_s = cosine[half : half + 1, :] * spread, sine[half : half + 1, :] * spread
            parts = jnp.concatenate([mid_c * even, -mid_s * odd, -mid_s * even, -mid_c * odd], axis=0)
            for z in range(depth_grid):
                here = jnp.where(depths_ref[number] == z, 1.0, 0.0)
                rows = slice(z * 4 * FAST_HALF, (z + 1) * 4 * FAST_HALF)
                cols = slice(s * channels, (s + 1) * channels)
                coef_ref[i, rows, cols] = (parts * here).astype(jnp.bfloat16)

    coefficients(0)

    def filled(value, rows):
        lack = rows - value.shape[0]
        if lack == 0:
            return value
        return jnp.concatenate([value, jnp.zeros((lack, value.shape[1]), value.dtype)], axis=0)

    for block, first in enumerate(range(0, bins, LANES)):
        for load in loads[5 + 3 * block : 8 + 3 * block]:
            load.wait()
        cols = slice(first, first + LANES)
        deep = -(-top_of(first + LANES - 1) // LANES) * LANES
        rows = min(-(-top_of(first + LANES - 1) // 16) * 16, modes)
        whole = -(-rows // 16) * 16
        wave = wave_ref[:rows, cols]
        cosine, sine = sincos_turns(wave * (centre * (1.0 / TWO_PI)))
        index = lax.broadcasted_iota(jnp.int32, (rows, LANES), 0)
        factor = receiver_ref[:rows, cols].astype(jnp.float32) * (8.0 / math.sqrt(bins * modes))
        factor = jnp.where(index < counts_ref[:, cols], factor * lax.rsqrt(wave), 0.0)
        xi = (wave - K_MID) * (1.0 / K_HALF)
        xi_ref[cols, :deep] = filled(filled(xi, whole), deep).T
        weights = (factor * cosine, factor * sine)
        base = block * modes * depth_grid
        flat_ref[base : base + rows * depth_grid, :] = (
            source_ref[:rows, :, cols].astype(jnp.float32).reshape(rows * depth_grid, LANES)
        )
        for z in range(depth_grid):
            source = flat_ref[pl.ds(base + z, rows, stride=depth_grid), :]
            for c in range(2):
                value = filled(source * weights[c], whole).astype(jnp.bfloat16)
                left_ref[z * 2 + c, cols, :deep] = filled(value, deep).T

    loads[-1].wait()
    for block in range(samples // LANES):
        rows = slice(block * LANES, (block + 1) * LANES)
        wave_t_ref[rows, :] = recorded_ref[:, rows].T

    across = (((1,), (1,)), ((), ()))
    terms = 2 * FAST_HALF
    kinds = 2 * depth_grid
    same_bin = (
        lax.broadcasted_iota(jnp.int32, (16, terms * 16), 0)
        == lax.broadcasted_iota(jnp.int32, (16, terms * 16), 1) % 16
    )
    for g in range(bins // 16):
        rows = slice(g * 16, g * 16 + 16)
        deep = -(-top_of(g * 16 + 15) // LANES) * LANES
        xi = xi_ref[rows, :deep]
        double = xi + xi
        before, now = jnp.ones_like(xi), xi
        right = [before.astype(jnp.bfloat16)]
        for n in range(1, FAST_TERMS):
            right.append(now.astype(jnp.bfloat16))
            before, now = now, double * now - before
        right = right + [jnp.zeros_like(right[0])] * (terms - FAST_TERMS)
        left = jnp.concatenate([left_ref[k, rows, :deep] for k in range(kinds)], axis=0)
        pairs = lax.dot_general(
            left, jnp.concatenate(right, axis=0), across, preferred_element_type=jnp.float32
        )
        for k in range(kinds):
            value = jnp.where(same_bin, pairs[k * 16 : k * 16 + 16], 0.0)
            apart_ref[rows, k * terms * 16 : (k + 1) * terms * 16] = value.astype(jnp.bfloat16)

    term = lax.broadcasted_iota(jnp.int32, (terms * 16, group), 0) // 16
    column = lax.broadcasted_iota(jnp.int32, (terms * 16, group), 1)
    column = column - (term // 2 + FAST_HALF * (term % 2))
    column = jnp.where(term < FAST_TERMS, column, -1)
    gathers = []
    for k in range(kinds):
        z, c = k // 2, k % 2
        plain = jnp.where(column == k * terms, 1.0, 0.0)
        turned = jnp.where(column == (z * 2 + 1 - c) * terms, 1.0 - 2.0 * c, 0.0)
        gathers.append(jnp.concatenate([plain, turned], axis=1).astype(jnp.bfloat16))
    gather = jnp.concatenate(gathers, axis=0)
    middle = bins // 2
    moments = jnp.concatenate(
        [
            jnp.dot(apart_ref[:middle, :], gather, preferred_element_type=jnp.float32),
            jnp.dot(apart_ref[middle:, :], gather, preferred_element_type=jnp.float32),
        ],
        axis=0,
    )
    moment_ref[:bins, :] = moments[:, :group]
    moment_ref[bins:, :] = moments[:, group:]
    weights = []
    for r in range(4):
        plain = moment_ref[pl.ds(r, quarter, stride=4), :].astype(jnp.bfloat16)
        turned = moment_ref[pl.ds(bins + r, quarter, stride=4), :].astype(jnp.bfloat16)
        weight = jnp.concatenate([plain, turned], axis=0)
        if r % 2:
            weight = jnp.concatenate([weight, jnp.concatenate([turned, -plain], axis=0)], axis=1)
        weights.append(weight)
    piece = 512
    for r in range(4):
        sides = weights[r].shape[1]
        weights_ref[r, :, :sides] = weights[r]

    def transform(i, carry):
        start = pl.multiple_of(i * piece, piece)
        rows = pl.ds(start, piece)
        p0, p1, p2, p3 = (
            jnp.dot(
                tab_ref[r, rows, :],
                weights_ref[r, :, : group * (1 + r % 2)],
                preferred_element_type=jnp.float32,
            )
            for r in range(4)
        )
        odd, turned = p1[:, :group] + p3[:, :group], p1[:, group:] - p3[:, group:]
        even, gap = p0 + p2, p0 - p2
        for q, value in enumerate((even + odd, gap + turned, even - odd, gap - turned)):
            psi_ref[pl.ds(q * span + start, piece), :] = value.astype(jnp.bfloat16)
        return carry

    lax.fori_loop(0, span // piece, transform, 0)

    section_row = sections_ref[...]
    lane_in_row = section_row % 8
    own_rows = receivers // 4 // count // 8
    slots = lax.broadcasted_iota(jnp.int32, (count * own_rows, channels), 0)
    member_ref[...] = (slots == section_row // 8).astype(jnp.float32).astype(jnp.bfloat16)

    def quad(i, carry):
        series = jnp.dot(psi_ref[...], coef_ref[i], preferred_element_type=jnp.float32)
        waveform = wave_t_ref[...].astype(jnp.float32)
        slot = lax.broadcasted_iota(jnp.int32, (8, channels), 0)
        for s in range(4):
            product = jnp.tanh(series[:, s * channels : (s + 1) * channels]) * waveform
            total = jnp.sum(product.reshape(samples // 8, 8, channels), axis=0)
            for shift in (4, 2, 1):
                total = total + pltpu.roll(total, shift, 0)
            rows = pl.ds((sources - 1 - s - 4 * i) * 8, 8)
            kept_ref[rows, :] = jnp.where(slot == lane_in_row, total, 0.0)
        if i + 1 < sources // 4:
            coefficients(i + 1)
        return carry

    for i in range(sources // 4):
        quad(i, 0)

    member = member_ref[...]
    kept = kept_ref[...] * (1.0 / math.sqrt(samples * 4))
    high = kept.astype(jnp.bfloat16)
    low = (kept - high.astype(jnp.float32)).astype(jnp.bfloat16)
    blocks = lax.dot_general(
        jnp.concatenate([member, member], axis=1),
        jnp.concatenate([high, low], axis=1),
        across,
        preferred_element_type=jnp.float32,
    )
    for target in range(count):
        block_ref[target] = blocks[target * own_rows : (target + 1) * own_rows]

    pl.semaphore_wait(barrier, count - 1)

    def copy_to(freq, sub, slot, source):
        return pltpu.make_async_remote_copy(
            src_ref=block_ref.at[freq * sub_size + sub],
            dst_ref=held_ref.at[source],
            send_sem=send_sem.at[slot],
            recv_sem=recv_sem.at[source],
            device_id={"freq": freq, "sub": sub},
            device_id_type=pl.DeviceIdType.MESH,
        )

    sends = []
    for slot, (i, j) in enumerate(partners):
        freq, sub = ahead(i, j)
        sends.append(copy_to(freq, sub, slot, me))
        sends[-1].start()
    total = block_ref[me]
    for slot, (i, j) in enumerate(partners):
        freq, sub = ahead(freq_size - i, sub_size - j)
        source = freq * sub_size + sub
        copy_to(freq, sub, slot, source).wait_recv()
        total = total + held_ref[source]

    halves = [jnp.zeros((8, LANES), jnp.float32)] * (sources // 8)
    for r in range(own_rows):
        spread_row = jnp.broadcast_to(total[r : r + 1, :], (8, LANES))
        moved = pltpu.roll(spread_row, 0, 1, stride=8, stride_axis=0)
        for h in range(sources // 8):
            placed = pltpu.roll(moved, (8 * r + 8 + 64 * h) % LANES, 1)
            halves[h] = jnp.where(lane // 8 == r, placed, halves[h])
    out_ref[...] = jnp.concatenate(halves, axis=0)[:, : own_rows * 8]

    for send in sends:
        send.wait_send()


def fast_fits(mesh_sizes, wavenumbers, source_shapes, source_depths, recorded):
    count = mesh_sizes[0] * mesh_sizes[1]
    bins = wavenumbers.shape[0]
    channels, samples = recorded.shape
    own = channels // 4
    return (
        channels == LANES
        and source_depths.shape[0] * 8 == LANES
        and source_shapes.shape[1] * 4 * FAST_HALF == LANES
        and bins == 4 * LANES
        and samples % (4 * LANES) == 0
        and own % 8 == 0
        and own // 8 <= 8
        and count * (own // 8) % 16 == 0
    )


def per_device(
    mesh_sizes,
    wavenumbers,
    receiver_shapes,
    source_shapes,
    mode_counts,
    source_depths,
    source_ranges,
    sections,
    recorded,
):
    args = (
        wavenumbers,
        receiver_shapes,
        source_shapes,
        mode_counts,
        source_depths,
        source_ranges,
        sections,
        recorded,
    )
    if not fast_fits(mesh_sizes, wavenumbers, source_shapes, source_depths, recorded):
        return per_device_general(mesh_sizes, *args)
    freq_size, sub_size = mesh_sizes
    count = freq_size * sub_size
    bins, modes = wavenumbers.shape
    depth_grid = source_shapes.shape[1]
    sources = source_depths.shape[0]
    channels, samples = recorded.shape
    receivers = channels * count
    reach = 2.0 * (channels - 1) / receivers
    top_phase = K_HALF * 0.5 * (reach + R_TOP)
    assert 2.0 * (0.5 * top_phase) ** FAST_TERMS / math.factorial(FAST_TERMS) < 1e-6

    shape = (bins, modes, depth_grid, sources, channels, samples, mesh_sizes)
    group = depth_grid * 4 * FAST_HALF
    deep = -(-modes // LANES) * LANES
    own = channels // 4
    return pl.pallas_call(
        functools.partial(score_kernel, shape),
        out_shape=pltpu.VMEM((sources, own), jnp.float32),
        in_specs=[pl.BlockSpec(memory_space=pl.ANY)] * 9,
        out_specs=pl.BlockSpec(memory_space=pltpu.VMEM),
        scratch_shapes=[
            pltpu.SMEM((sources,), jnp.int32),
            pltpu.SMEM((sources,), jnp.float32),
            pltpu.VMEM((FAST_HALF, LANES), jnp.float32),
            pltpu.VMEM((1, channels), jnp.int32),
            pltpu.VMEM((1, bins), jnp.int32),
            pltpu.VMEM((modes, bins), jnp.float32),
            pltpu.VMEM((modes, bins), jnp.bfloat16),
            pltpu.VMEM((modes, depth_grid, bins), jnp.bfloat16),
            pltpu.VMEM((channels, samples), jnp.bfloat16),
            pltpu.VMEM((bins // LANES * modes * depth_grid, LANES), jnp.float32),
            pltpu.VMEM((2 * depth_grid, bins, deep), jnp.bfloat16),
            pltpu.VMEM((bins, deep), jnp.float32),
            pltpu.VMEM((bins, group * 2 * FAST_HALF), jnp.bfloat16),
            pltpu.VMEM((2 * bins, group), jnp.float32),
            pltpu.VMEM((4, bins // 2, 2 * group), jnp.bfloat16),
            pltpu.VMEM((4, samples // 4, bins // 2), jnp.bfloat16),
            pltpu.VMEM((samples, group), jnp.bfloat16),
            pltpu.VMEM((sources // 4 + 1, group, 4 * channels), jnp.bfloat16),
            pltpu.VMEM((samples, channels), jnp.bfloat16),
            pltpu.VMEM((sources * 8, channels), jnp.float32),
            pltpu.VMEM((count * (own // 8), channels), jnp.bfloat16),
            pltpu.VMEM((count, own // 8, LANES), jnp.float32),
            pltpu.VMEM((count, own // 8, LANES), jnp.float32),
            pltpu.SemaphoreType.DMA((6 + 3 * bins // LANES,)),
            pltpu.SemaphoreType.DMA((count - 1,)),
            pltpu.SemaphoreType.DMA((count,)),
        ],
        compiler_params=pltpu.CompilerParams(
            vmem_limit_bytes=60 * 1024 * 1024, collective_id=1, has_side_effects=True
        ),
        name="score",
    )(
        source_depths,
        source_ranges,
        jnp.asarray(fast_constants()),
        sections.reshape(1, channels),
        mode_counts.reshape(1, bins),
        wavenumbers.T,
        receiver_shapes.T,
        source_shapes.transpose(2, 1, 0),
        recorded,
    )


def per_device_general(
    mesh_sizes,
    wavenumbers,
    receiver_shapes,
    source_shapes,
    mode_counts,
    source_depths,
    source_ranges,
    sections,
    recorded,
):
    freq_size, sub_size = mesh_sizes
    count = freq_size * sub_size
    me = lax.axis_index("freq") * sub_size + lax.axis_index("sub")
    bins, modes = wavenumbers.shape
    depth_grid = source_shapes.shape[1]
    sources = source_depths.shape[0]
    channels, samples = recorded.shape
    receivers = channels * count

    first_x = 1.0 + 2.0 * (me * channels).astype(jnp.float32) / receivers
    reach = 2.0 * (channels - 1) / receivers
    centre = first_x + 0.5 * (reach - R_TOP)
    top_phase = K_HALF * 0.5 * (reach + R_TOP)
    assert 2.0 * (0.5 * top_phase) ** TERMS / math.factorial(TERMS) < 1e-9
    assert depth_grid * 2 * TERMS <= LANES

    extra = -modes % 8
    wave = wavenumbers.T
    live = jnp.arange(modes, dtype=jnp.int32)[:, None] < mode_counts[None, :]
    factor = receiver_shapes.T.astype(jnp.float32) * (8.0 / math.sqrt(bins))
    factor = jnp.where(live, factor / jnp.sqrt(wave * modes), 0.0)
    factor = jnp.pad(factor, ((0, extra), (0, 0)))
    wave = jnp.pad(wave, ((0, extra), (0, 0)), constant_values=K_MID)
    shape = (bins, modes, depth_grid, sources, channels, samples, receivers)
    matched = pl.pallas_call(
        functools.partial(replica_kernel, shape),
        out_shape=jax.ShapeDtypeStruct((channels, LANES), jnp.float32),
        in_specs=[pl.BlockSpec(memory_space=pltpu.SMEM)] * 3
        + [pl.BlockSpec(memory_space=pltpu.VMEM)] * 5,
        out_specs=pl.BlockSpec(memory_space=pltpu.VMEM),
        scratch_shapes=[
            pltpu.VMEM((depth_grid * 2 * TERMS, bins), jnp.float32),
            pltpu.VMEM((16, LANES), jnp.float32),
            pltpu.VMEM((TERMS * 8, LANES), jnp.float32),
            pltpu.VMEM((bins // 2, samples // 4), jnp.bfloat16),
            pltpu.VMEM((4, depth_grid * 2 * TERMS, samples // 4), jnp.float32),
            pltpu.VMEM((depth_grid * 2 * TERMS, samples), jnp.bfloat16),
            pltpu.VMEM((sources, channels, 2 * TERMS), jnp.bfloat16),
        ],
        compiler_params=pltpu.CompilerParams(vmem_limit_bytes=48 * 1024 * 1024),
        name="replica",
    )(
        source_depths,
        jnp.stack([first_x, centre]),
        source_ranges,
        jnp.asarray(term_constants()),
        wave,
        factor,
        source_shapes.transpose(2, 1, 0),
        recorded,
    )

    section_count = receivers // 4
    own = section_count // count
    per_row = min(LANES // sources, own)
    own_rows = own // per_row
    assert LANES % sources == 0 and own % per_row == 0
    padded = -(-own_rows // 8) * 8
    slot = jnp.arange(count * padded, dtype=jnp.int32)
    wanted = jnp.where(
        slot % padded < own_rows, slot // padded * own_rows + slot % padded, -1
    )
    member = (wanted[:, None] == (sections // per_row)[None, :]).astype(jnp.float32)
    lane_part = jnp.arange(LANES, dtype=jnp.int32) // sources
    kept = jnp.where((sections % per_row)[:, None] == lane_part[None, :], matched, 0.0)
    blocks = jnp.dot(member, kept, precision=lax.Precision.HIGHEST) * (
        1.0 / math.sqrt(samples * (receivers // section_count))
    )
    blocks = blocks.reshape(count, padded, LANES)
    total = pl.pallas_call(
        functools.partial(exchange_kernel, (freq_size, sub_size)),
        out_shape=jax.ShapeDtypeStruct((padded, LANES), jnp.float32),
        in_specs=[pl.BlockSpec(memory_space=pltpu.VMEM)],
        out_specs=pl.BlockSpec(memory_space=pltpu.VMEM),
        scratch_shapes=[
            pltpu.VMEM((count, padded, LANES), jnp.float32),
            pltpu.SemaphoreType.DMA((count,)),
            pltpu.SemaphoreType.DMA((count,)),
        ],
        compiler_params=pltpu.CompilerParams(collective_id=0, has_side_effects=True),
        name="exchange",
    )(blocks)
    total = total[:own_rows, : per_row * sources].reshape(own_rows, per_row, sources)
    return total.transpose(2, 0, 1).reshape(sources, own)


def solution(mesh):
    sizes = (mesh.shape["freq"], mesh.shape["sub"])
    in_specs = (
        P(),
        P(),
        P(),
        P(),
        P("groups"),
        P("groups"),
        P(("freq", "sub")),
        P(("freq", "sub"), None),
    )
    out_specs = P("groups", ("freq", "sub"))
    return jax.shard_map(
        functools.partial(per_device, sizes),
        mesh=mesh,
        in_specs=in_specs,
        out_specs=out_specs,
        check_vma=False,
    )
```
